32 devices in a mesh: replica: 8 (over z, core), group: 4 (over y, x).
Axes of the slice: x: 2, y: 2, z: 4, core: 2. Of those that a mesh axis runs over, the one named last changes fastest.
Arguments:
- tokens: bfloat16 [4096, 2048], P(('replica', 'group')), may hold values from -6 to 6
- lengths: int32 [8], P('replica'), may hold values from 128 to 512, as said below
- exit_layers: int32 [4096], P(('replica', 'group')), may hold values from 7 to 20, as said below
- pre_gain: bfloat16 [2048], P('group'), may hold values from 0.099609375 to 1.8984375
- pre_shift: bfloat16 [2048], P('group'), may hold values from -3 to 3
- query_weight: bfloat16 [2048, 2048], P('group'), may hold values from -0.1875 to 0.1875
- query_bias: bfloat16 [2048], P('group'), may hold values from -3 to 3
- key_weight: bfloat16 [2048, 2048], P('group'), may hold values from -0.1875 to 0.1875
- value_weight: bfloat16 [2048, 2048], P('group'), may hold values from -0.125 to 0.125
- value_bias: bfloat16 [2048], P('group'), may hold values from -3 to 3
- out_weight: bfloat16 [2048, 2048], P('group'), may hold values from -0.5 to 0.5
- out_bias: bfloat16 [2048], P('group'), may hold values from -1.75 to 1.75
- mid_gain: bfloat16 [2048], P('group'), may hold values from 0.099609375 to 1.8984375
- mid_shift: bfloat16 [2048], P('group'), may hold values from -3 to 3
- up_weight: bfloat16 [2048, 8192], P(None, 'group'), may hold values from -0.125 to 0.125
- up_bias: bfloat16 [8192], P('group'), may hold values from -3 to 3
- down_weight: bfloat16 [8192, 2048], P('group'), may hold values from -0.0625 to 0.0625
- down_bias: bfloat16 [2048], P('group'), may hold values from -1.75 to 1.75
- cotangent: bfloat16 [4096, 2048], P(('replica', 'group')), may hold values from -6 to 6
Outputs:
- output: bfloat16 [4096, 2048], P(('replica', 'group'))
- token_grad: bfloat16 [4096, 2048], P(('replica', 'group'))
- pre_gain_grad: float32 [2048], P('group')
- pre_shift_grad: float32 [2048], P('group')
- query_weight_grad: float32 [2048, 2048], P('group')
- query_bias_grad: float32 [2048], P('group')
- key_weight_grad: float32 [2048, 2048], P('group')
- value_weight_grad: float32 [2048, 2048], P('group')
- value_bias_grad: float32 [2048], P('group')
- out_weight_grad: float32 [2048, 2048], P('group')
- out_bias_grad: float32 [2048], P('group')
- mid_gain_grad: float32 [2048], P('group')
- mid_shift_grad: float32 [2048], P('group')
- up_weight_grad: float32 [2048, 8192], P(None, 'group')
- up_bias_grad: float32 [8192], P('group')
- down_weight_grad: float32 [8192, 2048], P('group')
- down_bias_grad: float32 [2048], P('group')
The draws below stay inside these ranges and needn't reach their ends.
Inputs may be any that keep to these rules, and one draw needn't show every extreme that they name: `lengths`: some sequence has length 512 and some other has length 128. Within each sequence, exit_layers never rise from one position to the next.
All inputs are finite; a program needn't handle non-finite values.
Results may differ from the reference program's by a relative error of at most 0.02.
Values may be sent and summed in bfloat16 or wider, within the bound.
No kernel may reach another device: no remote copies, remote signals or barrier semaphores. Data moves between devices by JAX's collectives and lax.ppermute only.
A program may use at most 640 MiB of HBM per device.

```python
import jax
import jax.numpy as jnp
from jax import lax

D = 2048
H = 32
HD = 64
FF = 8192
LAYER = 12
LEN = 512
SEQS = 8
TOKENS = 4096


def draw_lengths(key, part):
    first, second = jax.random.split(jax.random.fold_in(key, 3))
    values = jax.random.randint(first, (SEQS,), LEN // 4, LEN + 1)
    chosen = jax.random.randint(second, (), 0, SEQS)
    other = (chosen + 1) % SEQS
    index = jnp.arange(SEQS)
    values = jnp.where(index == other, LEN // 4, values)
    return jnp.where(index == chosen, LEN, values).astype(jnp.int32)


def draw_exit_layers(key, part):
    first, second = jax.random.split(jax.random.fold_in(key, 7))
    cutoff = jax.random.randint(first, (SEQS, 1), LEN // 4, LEN + 1)
    chosen = jax.random.randint(second, (), 0, SEQS)
    other = (chosen + 1) % SEQS
    index = jnp.arange(SEQS)[:, None]
    cutoff = jnp.where(index == other, LEN // 4, cutoff)
    cutoff = jnp.where(index == chosen, LEN, cutoff)
    position = jnp.arange(LEN)[None, :]
    stride = LEN // 8
    before = LAYER + 1 + (cutoff - 1 - position) // stride
    after = LAYER - jnp.minimum((position - cutoff) // stride, LAYER)
    return jnp.where(position < cutoff, before, after).reshape(SEQS * LEN).astype(jnp.int32)


def shard_levels(rng, dims, cuts, low, largest):
    gain, own = 1.0, jax.random.fold_in(rng, 6)
    for axis_at, blocks in cuts:
        heights = jnp.exp(jax.random.uniform(jax.random.fold_in(own, axis_at), (blocks,), jnp.float32, low / len(cuts), largest / len(cuts)))
        gain = gain * jnp.repeat(heights, dims[axis_at] // blocks).reshape([-1 if axis == axis_at else 1 for axis in range(len(dims))])
    return gain


def bell_draw(rng, dims, width, most, cuts=(), kind=jnp.bfloat16):
    drawn = jax.random.normal(rng, dims, jnp.float32) * width
    if len(cuts) > 0:
        drawn = shard_levels(rng, dims, cuts, -0.22, 0.18) * drawn
    return jnp.clip(drawn, min=-most, max=most).astype(kind)


def setup_inputs(seed: int = 0) -> dict:
    arg_keys = jax.random.split(jax.random.key(seed), 20)
    tokens = bell_draw(arg_keys[0], (TOKENS, D), 1.0, 6.0, ((0, 32),))
    lengths = draw_lengths(jax.random.fold_in(arg_keys[19], 71), 0)
    exit_layers = draw_exit_layers(jax.random.fold_in(arg_keys[19], 71), 0)
    pre_gain = jnp.clip(1.0 + 0.18 * jax.random.normal(arg_keys[3], (D,), jnp.float32), 0.099609375, 1.8984375).astype(jnp.bfloat16)
    pre_shift = bell_draw(arg_keys[4], (D,), 0.5, 3.0, ((0, 4),))
    query_weight = bell_draw(arg_keys[5], (D, D), (D // 2) ** -0.5, 0.1875, ((0, 4),))
    query_bias = bell_draw(arg_keys[6], (D,), 0.5, 3.0, ((0, 4),))
    key_weight = bell_draw(arg_keys[7], (D, D), (D // 2) ** -0.5, 0.1875, ((0, 4),))
    value_weight = bell_draw(arg_keys[8], (D, D), D ** -0.5, 0.125, ((0, 4),))
    value_bias = bell_draw(arg_keys[9], (D,), 0.5, 3.0, ((0, 4),))
    out_weight = bell_draw(arg_keys[10], (D, D), (D // 16) ** -0.5, 0.5, ((0, 4),))
    out_bias = bell_draw(arg_keys[11], (D,), 0.3, 1.75, ((0, 4),))
    mid_gain = jnp.clip(1.0 + 0.18 * jax.random.normal(arg_keys[12], (D,), jnp.float32), 0.099609375, 1.8984375).astype(jnp.bfloat16)
    mid_shift = bell_draw(arg_keys[13], (D,), 0.5, 3.0, ((0, 4),))
    up_weight = bell_draw(arg_keys[14], (D, FF), D ** -0.5, 0.125, ((1, 4),))
    up_bias = bell_draw(arg_keys[15], (FF,), 0.5, 3.0, ((0, 4),))
    down_weight = bell_draw(arg_keys[16], (FF, D), FF ** -0.5, 0.0625, ((0, 4),))
    down_bias = bell_draw(arg_keys[17], (D,), 0.3, 1.75, ((0, 4),))
    cotangent = bell_draw(arg_keys[18], (TOKENS, D), 1.0, 6.0, ((0, 32),))
    return {"tokens": tokens, "lengths": lengths, "exit_layers": exit_layers, "pre_gain": pre_gain, "pre_shift": pre_shift, "query_weight": query_weight, "query_bias": query_bias, "key_weight": key_weight, "value_weight": value_weight, "value_bias": value_bias, "out_weight": out_weight, "out_bias": out_bias, "mid_gain": mid_gain, "mid_shift": mid_shift, "up_weight": up_weight, "up_bias": up_bias, "down_weight": down_weight, "down_bias": down_bias, "cotangent": cotangent}


@jax.custom_vjp
def low(v):
    return lax.optimization_barrier(v.astype(jnp.bfloat16)).astype(jnp.float32)

@jax.custom_vjp
def low_back(v):
    return v

def low_keep(v):
    return (low(v), None)

def low_pass(kept, grad):
    return (grad,)

def back_keep(v):
    return (v, None)

def back_low(kept, grad):
    return (low(grad),)
low.defvjp(low_keep, low_pass)
low_back.defvjp(back_keep, back_low)
highest = lax.Precision.HIGHEST

def product(left, right):
    return jnp.dot(left, right, precision=highest)

def gelu(values):
    return 0.5 * values * (1.0 + jnp.tanh(0.7978845608 * (values + 0.044715 * values * values * values)))

def normed(values):
    center = values - lax.optimization_barrier(jnp.mean(values, -1, keepdims=True))
    spread = lax.optimization_barrier(jnp.mean(center * center, -1, keepdims=True))
    return center * lax.rsqrt(spread + 1e-05)

def attend(queries, keys, values):
    block = min(512, LEN)
    count = LEN // block
    query_blocks = queries.reshape(count, block, H, HD)
    starts = jnp.arange(count, dtype=jnp.int32) * block

    def one_block(operands):
        query_block, start = operands
        position = start + jnp.arange(block, dtype=jnp.int32)
        allowed = jnp.arange(LEN, dtype=jnp.int32)[None, :] <= position[:, None]
        scores = jnp.einsum('qhd,khd->hqk', query_block, keys, precision=highest) * 0.125
        scores = low_back(scores)
        scores = jnp.where(allowed[None], scores, -1e+30)
        top = lax.optimization_barrier(jnp.max(scores, -1, keepdims=True))
        logsum = top + jnp.log(lax.optimization_barrier(jnp.sum(jnp.exp(scores - top), -1, keepdims=True)))
        weights = low(jnp.exp(scores - logsum))
        return jnp.einsum('hqk,khd->qhd', weights, values, precision=highest)
    context = lax.map(jax.checkpoint(one_block), (query_blocks, starts))
    return context.reshape(LEN, D)

def layer(inputs, active, pre_gain, pre_shift, query_weight, query_bias, key_weight, value_weight, value_bias, out_weight, out_bias, mid_gain, mid_shift, up_weight, up_bias, down_weight, down_bias):
    attn_in = low(normed(inputs) * pre_gain + pre_shift)
    queries = low(low_back(product(attn_in, query_weight) + query_bias))
    keys = low(low_back(product(attn_in, key_weight)))
    values = low(low_back(product(attn_in, value_weight) + value_bias))
    context = attend(queries.reshape(LEN, H, HD), keys.reshape(LEN, H, HD), values.reshape(LEN, H, HD))
    context = low(low_back(context))
    attn_out = low_back(product(context, out_weight) + out_bias)
    hidden = inputs + active * attn_out
    ffn_in = low(normed(hidden) * mid_gain + mid_shift)
    pre_act = product(ffn_in, up_weight) + up_bias
    act_low = low(low_back(gelu(pre_act)))
    branch = low_back(product(act_low, down_weight) + down_bias)
    return hidden + active * branch

def reference(tokens, lengths, exit_layers, pre_gain, pre_shift, query_weight, query_bias, key_weight, value_weight, value_bias, out_weight, out_bias, mid_gain, mid_shift, up_weight, up_bias, down_weight, down_bias, cotangent):
    params = tuple((item.astype(jnp.float32) for item in (pre_gain, pre_shift, query_weight, query_bias, key_weight, value_weight, value_bias, out_weight, out_bias, mid_gain, mid_shift, up_weight, up_bias, down_weight, down_bias)))
    rows = tokens.astype(jnp.float32).reshape(SEQS, LEN, D)
    grads_in = cotangent.astype(jnp.float32).reshape(SEQS, LEN, D)
    position = jnp.arange(LEN, dtype=jnp.int32)
    active = (position[None, :] < lengths[:, None]) & (exit_layers.reshape(SEQS, LEN) > LAYER)
    active = active.astype(jnp.float32)[..., None]

    def one_sequence(carry, operands):
        row_block, grad_block, active_block = operands
        result, pullback = jax.vjp(lambda values, *weights: layer(values, active_block, *weights), row_block, *params)
        grads = pullback(grad_block)
        summed = tuple((total + piece for total, piece in zip(carry, grads[1:])))
        return (summed, (result, grads[0]))
    start = tuple((jnp.zeros_like(item) for item in params))
    totals, (results, token_grads) = lax.scan(one_sequence, start, (rows, grads_in, active))
    output = results.reshape(TOKENS, D).astype(jnp.bfloat16)
    token_grad = token_grads.reshape(TOKENS, D).astype(jnp.bfloat16)
    return (output, token_grad, totals[0], totals[1], totals[2], totals[3], totals[4], totals[5], totals[6], totals[7], totals[8], totals[9], totals[10], totals[11], totals[12], totals[13], totals[14])
```

```python
import jax
import jax.numpy as jnp
from jax import lax
from jax.sharding import PartitionSpec as P

HD = 64
LAYER = 12

bf16 = jnp.bfloat16
f32 = jnp.float32


def layer_norm(values):
    center = values - jnp.mean(values, -1, keepdims=True)
    spread = jnp.mean(center * center, -1, keepdims=True)
    factor = lax.rsqrt(spread + 1e-05)
    return (center * factor, factor)


def norm_back(grad, normal, factor):
    return factor * (
        grad
        - jnp.mean(grad, -1, keepdims=True)
        - normal * jnp.mean(grad * normal, -1, keepdims=True)
    )


def gelu_both(values):
    inner = 0.7978845608 * (values + 0.044715 * values * values * values)
    tangent = jnp.tanh(inner)
    slope = 0.5 * (1.0 + tangent) + 0.5 * values * (1.0 - tangent * tangent) * 0.7978845608 * (
        1.0 + 3.0 * 0.044715 * values * values
    )
    return 0.5 * values * (1.0 + tangent), slope


def matmul(left, right):
    return jnp.dot(left, right, preferred_element_type=f32)


def matmul_nt(left, right):
    return lax.dot_general(left, right, (((1,), (1,)), ((), ())), preferred_element_type=f32)


def matmul_tn(left, right):
    return lax.dot_general(left, right, (((0,), (0,)), ((), ())), preferred_element_type=f32)


def column_sums(matrix):
    return jnp.sum(matrix.astype(f32), 0)


def swap(block, step):
    count = lax.axis_size("group")
    return lax.ppermute(block, "group", [(i, i ^ step) for i in range(count)])


def exchange(blocks):
    return [blocks[0]] + [swap(blocks[step], step) for step in range(1, len(blocks))]


def gather_blocks(block):
    return exchange([block] * lax.axis_size("group"))


def in_order(blocks):
    me = lax.axis_index("group")
    rows = blocks[0].shape[0]
    whole = jnp.zeros((len(blocks) * rows,) + blocks[0].shape[1:], blocks[0].dtype)
    for step, block in enumerate(blocks):
        start = ((me ^ step) * rows,) + (0,) * (block.ndim - 1)
        whole = lax.dynamic_update_slice(whole, block, start)
    return whole


def scatter_terms(partial):
    count = lax.axis_size("group")
    me = lax.axis_index("group")
    rows = partial.shape[0] // count
    terms = [lax.dynamic_slice_in_dim(partial, me * rows, rows, 0)]
    for step in range(1, count):
        sent = lax.dynamic_slice_in_dim(partial, (me ^ step) * rows, rows, 0)
        terms.append(swap(sent.astype(bf16), step).astype(f32))
    return terms


def scatter_sum(partial):
    return sum(scatter_terms(partial))


def gather_rows(block):
    return lax.all_gather(block, "group", axis=0, tiled=True)


def scatter_rows(partial):
    return lax.psum_scatter(
        partial.astype(bf16), "group", scatter_dimension=0, tiled=True
    ).astype(f32)


def reorder(stack):
    me = lax.axis_index("group")
    count = stack.shape[0]
    bit = 1
    while bit < count:
        pairs = stack.reshape((count // (2 * bit), 2, bit) + stack.shape[1:])
        pairs = jnp.where((me & bit) != 0, pairs[:, ::-1], pairs)
        stack = pairs.reshape(stack.shape)
        bit *= 2
    return stack


def after(value, *others):
    return lax.optimization_barrier((value,) + others)[0]


def core_swap(block):
    count = lax.axis_size("replica")
    return lax.ppermute(block, "replica", [(i, i ^ 1) for i in range(count)])


def core_join(mine, axis):
    core = lax.axis_index("replica") % 2
    other = core_swap(mine)
    first = jnp.where(core == 0, mine, other)
    second = jnp.where(core == 0, other, mine)
    return jnp.concatenate([first, second], axis)


class Order:
    def __init__(self):
        self.last = ()

    def __call__(self, *values):
        values = lax.optimization_barrier(values + self.last)[: len(values)]
        return values[0] if len(values) == 1 else values

    def mark(self, *values):
        self.last = values


def replica_sum_small(values):
    count = lax.axis_size("replica")
    step = 1
    while step < count:
        values = values + lax.ppermute(values, "replica", [(i, i ^ step) for i in range(count)])
        step *= 2
    return values


def shards(
    tokens,
    lengths,
    exit_layers,
    pre_gain,
    pre_shift,
    query_weight,
    query_bias,
    key_weight,
    value_weight,
    value_bias,
    out_weight,
    out_bias,
    mid_gain,
    mid_shift,
    up_weight,
    up_bias,
    down_weight,
    down_bias,
    cotangent,
):
    rows, width = tokens.shape
    count = lax.axis_size("group")
    me = lax.axis_index("group")
    cols = width // count
    heads = cols // HD
    local = me * rows + jnp.arange(rows, dtype=jnp.int32)
    active = ((local < lengths[0]) & (exit_layers > LAYER)).astype(f32)[:, None]
    position = jnp.arange(count * rows, dtype=jnp.int32)
    allowed = position[None, :] <= position[:, None]
    core = lax.axis_index("replica") % 2
    half = cols // 2

    grad_out = cotangent.astype(f32)
    branch_grad = (active * grad_out).astype(bf16)
    tokens_all = in_order(gather_blocks(tokens))

    vectors = jnp.concatenate([pre_gain, pre_shift, out_bias, mid_gain, mid_shift, down_bias])
    vectors = vectors.reshape(2, 3 * cols)

    def column_block(step, start, length):
        at = (start, (me ^ step) * cols)
        parts = [
            lax.dynamic_slice(w, at, (length, cols)) for w in (query_weight, key_weight, value_weight)
        ]
        return jnp.concatenate(parts, 1)

    blocks = [vectors] + [
        jnp.concatenate([column_block(step, core * half, half), vectors])
        for step in range(1, count)
    ]
    blocks = exchange(blocks)
    arrived = jnp.stack([block[:half] for block in blocks[1:]])
    vectors = in_order([block[-2:][None] for block in blocks]).reshape(count, 6, cols)
    vectors = vectors.transpose(1, 0, 2).reshape(6, width).astype(f32)
    gain_one, shift_one, obias, gain_two, shift_two, dbias = (vectors[i] for i in range(6))
    others = core_swap(arrived)
    qkv_weight = jnp.zeros((count, 2, half, 3 * cols), bf16)
    for step in range(1, count):
        for place, block in ((core, arrived), (1 - core, others)):
            qkv_weight = lax.dynamic_update_slice(
                qkv_weight, block[step - 1][None, None], (me ^ step, place, 0, 0)
            )
    own = column_block(0, 0, cols).reshape(1, 2, half, 3 * cols)
    qkv_weight = lax.dynamic_update_slice(qkv_weight, own, (me, 0, 0, 0))
    qkv_weight = qkv_weight.reshape(width, 3 * cols)
    branch_blocks = gather_blocks(after(branch_grad, arrived))
    branch_all = in_order(branch_blocks)
    everyone = ("replica", "group")
    branch_wide = lax.all_gather(branch_grad, everyone, axis=0, tiled=True)

    normed_all, _ = layer_norm(tokens_all.astype(f32))
    attn_in = (normed_all * gain_one + shift_one).astype(bf16)
    qkv_bias = jnp.concatenate([query_bias, jnp.zeros_like(query_bias), value_bias]).astype(f32)
    qkv = (matmul(attn_in, qkv_weight) + qkv_bias).astype(bf16)
    queries, keys, values = (
        qkv[:, k * cols : (k + 1) * cols].reshape(-1, heads, HD) for k in range(3)
    )

    def scores_of(query, key):
        scores = jnp.einsum("qhd,khd->hqk", query, key, preferred_element_type=f32) * 0.125
        return jnp.where(allowed[None], scores, -1e30)

    scores = scores_of(queries, keys)
    top = jnp.max(scores, -1, keepdims=True)
    logsum = top + jnp.log(jnp.sum(jnp.exp(scores - top), -1, keepdims=True))
    weights = jnp.exp(scores - logsum).astype(bf16)
    context = (
        jnp.einsum("hqk,khd->qhd", weights, values, preferred_element_type=f32)
        .astype(bf16)
        .reshape(-1, cols)
    )
    context = after(context, *branch_blocks)
    attn_out = scatter_sum(matmul(context, out_weight)) + obias
    hidden = tokens.astype(f32) + active * attn_out
    normed_two, factor_two = layer_norm(hidden)
    ffn_in = (normed_two * gain_two + shift_two).astype(bf16)
    act_grad = matmul_nt(branch_all, down_weight)
    ffn_all = in_order(gather_blocks(ffn_in))
    ffn_wide = lax.all_gather(ffn_in, everyone, axis=0, tiled=True)
    pre_act = matmul(ffn_all, up_weight) + up_bias.astype(f32)
    act, slope = gelu_both(pre_act)
    act_low, pre_grad = lax.optimization_barrier(
        (act.astype(bf16), (act_grad * slope).astype(bf16))
    )
    order = Order()
    split = up_weight.shape[1] // 2
    up_half = lax.dynamic_slice(up_weight, (0, core * split), (width, split))
    down_half = lax.dynamic_slice(down_weight, (core * split, 0), (split, width))
    bias_half = lax.dynamic_slice(up_bias, (core * split,), (split,)).astype(f32)

    partial = matmul_nt(pre_grad, up_weight)
    order.mark(partial)
    ffn_in_grad = scatter_terms(partial)
    wide_grad = matmul_nt(order(branch_wide), down_half)
    order.mark(wide_grad)

    ffn_in_grad = sum(order(*ffn_in_grad))
    hidden_grad = grad_out + norm_back(ffn_in_grad * gain_two, normed_two, factor_two)
    attn_grad = (active * hidden_grad).astype(bf16)
    order.mark(attn_grad)
    attn_blocks = gather_blocks(attn_grad)
    branch = matmul(order(act_low), down_weight)
    order.mark(branch)

    attn_all = in_order(list(order(*attn_blocks)))
    context_grad = matmul_nt(attn_all, out_weight).astype(bf16).reshape(-1, heads, HD)
    probs = jnp.exp(scores_of(queries, keys) - logsum)
    probs_grad = jnp.einsum("qhd,khd->hqk", context_grad, values, preferred_element_type=f32)
    delta = jnp.sum(probs * probs_grad, -1, keepdims=True)
    score_grad = (probs * (probs_grad - delta)).astype(bf16)
    query_grad = jnp.einsum("hqk,khd->qhd", score_grad, keys, preferred_element_type=f32) * 0.125
    key_grad = jnp.einsum("hqk,qhd->khd", score_grad, queries, preferred_element_type=f32) * 0.125
    value_grad = jnp.einsum(
        "hqk,qhd->khd", probs.astype(bf16), context_grad, preferred_element_type=f32
    )
    qkv_grad = jnp.concatenate(
        [part.astype(bf16).reshape(-1, cols) for part in (query_grad, key_grad, value_grad)], 1
    )

    qkv_part = matmul_tn(attn_in, qkv_grad).astype(bf16).reshape(count, cols, 3 * cols)
    piece = lax.psum_scatter(qkv_part, "replica", scatter_dimension=1, tiled=True)
    in_part = matmul_nt(after(qkv_grad, qkv_part), qkv_weight)
    order.mark(in_part)
    in_grad = scatter_terms(in_part)
    out_part = matmul_tn(order(context), attn_all).astype(bf16)
    out_grad = lax.psum(out_part, "replica")
    order.mark(out_part)

    wide_act, wide_slope = gelu_both(matmul(order(ffn_wide), up_half) + bias_half)
    wide_act, wide_grad = lax.optimization_barrier(
        (wide_act.astype(bf16), (wide_grad * wide_slope).astype(bf16))
    )
    order.mark(wide_act, wide_grad)

    shared = jnp.stack(
        [
            jnp.sum(in_part * normed_all, 0),
            jnp.sum(in_part, 0),
            jnp.sum(ffn_in_grad * normed_two, 0),
            jnp.sum(ffn_in_grad, 0),
        ]
    )
    shared = reorder(shared.reshape(4, count, cols).transpose(1, 0, 2))
    shared = sum(exchange([shared[k] for k in range(count)]))
    qkv_bias_part = column_sums(qkv_grad)
    small = jnp.concatenate(
        [
            shared.reshape(-1),
            lax.dynamic_slice(column_sums(attn_all), (me * cols,), (cols,)),
            qkv_bias_part[:cols],
            qkv_bias_part[2 * cols :],
        ]
    )
    small = replica_sum_small(small)
    small_parts = [small[k * cols : (k + 1) * cols] for k in range(7)]

    normed_one, factor_one = layer_norm(tokens.astype(f32))
    in_grad = sum(order(*in_grad))
    token_grad = (hidden_grad + norm_back(in_grad * gain_one, normed_one, factor_one)).astype(bf16)
    order.mark(token_grad)

    down_grad = matmul_tn(order(wide_act), branch_wide).astype(bf16)
    order.mark(down_grad)
    piece = reorder(order(piece))
    piece = reorder(jnp.stack(exchange([piece[k] for k in range(count)])))
    piece = piece.reshape(count, -1, 3, cols).transpose(1, 2, 0, 3).reshape(-1, 3 * width)
    order.mark(piece)
    qkv_wgrad = lax.all_gather(piece, "replica", axis=0, tiled=True)
    up_grad = matmul_tn(order(ffn_wide), wide_grad).astype(bf16)
    order.mark(up_grad)
    down_grad = core_join(down_grad, 0).astype(f32)
    up_grad = core_join(up_grad, 1).astype(f32)
    up_bias_grad = core_join(column_sums(wide_grad), 0)
    down_bias_grad = lax.dynamic_slice(column_sums(branch_wide), (me * cols,), (cols,))

    branch = scatter_sum(branch) + dbias
    output = (hidden + active * branch).astype(bf16)
    qkv_wgrad = order(qkv_wgrad)
    out_grad = order(out_grad).astype(f32)
    return (
        output,
        token_grad,
        small_parts[0],
        small_parts[1],
        qkv_wgrad[:, :width].astype(f32),
        small_parts[5],
        qkv_wgrad[:, width : 2 * width].astype(f32),
        qkv_wgrad[:, 2 * width :].astype(f32),
        small_parts[6],
        out_grad,
        small_parts[4],
        small_parts[2],
        small_parts[3],
        up_grad,
        up_bias_grad,
        down_grad,
        down_bias_grad,
    )


def solution(mesh):
    both = P(("replica", "group"), None)
    vector, by_rows, by_cols = P("group"), P("group", None), P(None, "group")
    return jax.shard_map(
        shards,
        mesh=mesh,
        in_specs=(
            both,
            P("replica"),
            P(("replica", "group")),
            vector,
            vector,
            by_rows,
            vector,
            by_rows,
            by_rows,
            vector,
            by_rows,
            vector,
            vector,
            vector,
            by_cols,
            vector,
            by_rows,
            vector,
            both,
        ),
        out_specs=(
            both,
            both,
            vector,
            vector,
            by_rows,
            vector,
            by_rows,
            by_rows,
            vector,
            by_rows,
            vector,
            vector,
            vector,
            by_cols,
            vector,
            by_rows,
            vector,
        ),
        check_vma=False,
    )
```

```python
import functools

import jax
import jax.numpy as jnp
from jax import lax
from jax.experimental import pallas as pl
from jax.experimental.pallas import tpu as pltpu
from jax.sharding import PartitionSpec as P

HD = 64
LAYER = 12
QB = 128

bf16 = jnp.bfloat16
f32 = jnp.float32


def layer_norm(values):
    center = values - jnp.mean(values, -1, keepdims=True)
    spread = jnp.mean(center * center, -1, keepdims=True)
    factor = lax.rsqrt(spread + 1e-05)
    return (center * factor, factor)


def norm_back(grad, normal, factor):
    return factor * (
        grad
        - jnp.mean(grad, -1, keepdims=True)
        - normal * jnp.mean(grad * normal, -1, keepdims=True)
    )


def params(mb=56):
    return pltpu.CompilerParams(vmem_limit_bytes=mb << 20)

def nt(left, right):
    return lax.dot_general(left, right, (((1,), (1,)), ((), ())), preferred_element_type=f32)
def tn(left, right):
    return lax.dot_general(left, right, (((0,), (0,)), ((), ())), preferred_element_type=f32)

def later(keys, first):
    key = lax.broadcasted_iota(jnp.int32, (keys, QB), 0)
    query = lax.broadcasted_iota(jnp.int32, (keys, QB), 1) + first
    return key <= query

def attend_body(q_ref, k_ref, v_ref, out_ref):
    rows = q_ref.shape[0]
    for first in range(0, rows, QB):
        keys = first + QB
        parts = []
        for lane in range(0, q_ref.shape[1], HD):
            at = slice(lane, lane + HD)
            query = q_ref[first:keys, at] * 0.125
            scores = jnp.where(later(keys, first), nt(k_ref[:keys, at], query), -1e30)
            grown = jnp.exp(scores - jnp.max(scores, 0, keepdims=True))
            probs = grown * (1.0 / jnp.sum(grown, 0, keepdims=True))
            parts.append(tn(probs.astype(bf16), v_ref[:keys, at]))
        out_ref[first:keys, :] = jnp.concatenate(parts, 1).astype(bf16)

def attend_back_body(q_ref, k_ref, v_ref, g_ref, dq_ref, dk_ref, dv_ref, key_acc, value_acc):
    rows = q_ref.shape[0]
    key_acc[...] = jnp.zeros_like(key_acc)
    value_acc[...] = jnp.zeros_like(value_acc)
    for first in range(0, rows, QB):
        keys = first + QB
        q_parts, k_parts, v_parts = [], [], []
        for lane in range(0, q_ref.shape[1], HD):
            at = slice(lane, lane + HD)
            query = q_ref[first:keys, at] * 0.125
            grad = g_ref[first:keys, at]
            key = k_ref[:keys, at]
            scores = jnp.where(later(keys, first), nt(key, query), -1e30)
            grown = jnp.exp(scores - jnp.max(scores, 0, keepdims=True))
            probs = grown * (1.0 / jnp.sum(grown, 0, keepdims=True))
            probs_grad = nt(v_ref[:keys, at], grad)
            delta = jnp.sum(probs * probs_grad, 0, keepdims=True)
            score_grad = (probs * (probs_grad - delta)).astype(bf16)
            v_parts.append(jnp.dot(probs.astype(bf16), grad, preferred_element_type=f32))
            k_parts.append(jnp.dot(score_grad, query, preferred_element_type=f32))
            q_parts.append(tn(score_grad, key) * 0.125)
        dq_ref[first:keys, :] = jnp.concatenate(q_parts, 1).astype(bf16)
        key_acc[:keys, :] += jnp.concatenate(k_parts, 1)
        value_acc[:keys, :] += jnp.concatenate(v_parts, 1)
    dk_ref[...] = key_acc[...].astype(bf16)
    dv_ref[...] = value_acc[...].astype(bf16)

def attention(qkv):
    rows, cols = qkv.shape[0], qkv.shape[1] // 3
    lanes = 2 * HD
    pairs = cols // lanes
    spec = lambda part: pl.BlockSpec((rows, lanes), lambda h: (0, part * pairs + h))
    work = 2 * rows * rows * cols
    return pl.pallas_call(
        attend_body, grid=(pairs,), in_specs=[spec(0), spec(1), spec(2)], out_specs=spec(0),
        out_shape=jax.ShapeDtypeStruct((rows, cols), bf16), compiler_params=params(),
        cost_estimate=pl.CostEstimate(flops=2 * work, bytes_accessed=8 * rows * cols, transcendentals=rows * rows * cols // HD),
    )(qkv, qkv, qkv)

def attention_back(qkv, grad):
    rows, cols = grad.shape
    lanes = 2 * HD
    pairs = cols // lanes
    spec = lambda part: pl.BlockSpec((rows, lanes), lambda h: (0, part * pairs + h))
    work = 2 * rows * rows * cols
    one = jax.ShapeDtypeStruct((rows, cols), bf16)
    return pl.pallas_call(
        attend_back_body, grid=(pairs,), in_specs=[spec(0), spec(1), spec(2), spec(0)], out_specs=[spec(0)] * 3,
        out_shape=[one] * 3, scratch_shapes=[pltpu.VMEM((rows, lanes), f32)] * 2, compiler_params=params(),
        cost_estimate=pl.CostEstimate(flops=5 * work, bytes_accessed=14 * rows * cols, transcendentals=rows * rows * cols // HD),
    )(qkv, qkv, qkv, grad)

def gelu_body(tile, place_ref, x_ref, w_ref, b_ref, g_ref, act_ref, grad_ref, sum_ref):
    first = pl.program_id(1) == 0
    for start in range(0, w_ref.shape[1], tile):
        at = slice(start, start + tile)
        value = jnp.dot(x_ref[...], w_ref[:, at], preferred_element_type=f32) + b_ref[:, at].astype(f32)
        square = value * value
        tangent = jnp.tanh(value * (0.7978845608 + (0.7978845608 * 0.044715) * square))
        share = 0.5 * value
        act_ref[:, at] = (share + share * tangent).astype(bf16)
        bend = share * (0.7978845608 + (3.0 * 0.7978845608 * 0.044715) * square)
        slope = (0.5 + 0.5 * tangent) + bend * (1.0 - tangent * tangent)
        grad = g_ref[:, at].astype(f32) * slope
        grad_ref[:, at] = grad.astype(bf16)
        total = jnp.sum(grad, 0, keepdims=True)
        sum_ref[:, at] = jnp.where(first, total, sum_ref[:, at] + total)

def gelu_product(x, weight, bias, grad, place, width, row_tile, col_tile):
    rows, depth = x.shape
    steps = width // col_tile
    grid = pltpu.PrefetchScalarGridSpec(
        num_scalar_prefetch=1, grid=(steps, rows // row_tile),
        in_specs=[
            pl.BlockSpec((row_tile, depth), lambda j, i, s: (i, 0)),
            pl.BlockSpec((depth, col_tile), lambda j, i, s: (0, s[0] * steps + j)),
            pl.BlockSpec((1, col_tile), lambda j, i, s: (0, s[0] * steps + j)),
            pl.BlockSpec((row_tile, col_tile), lambda j, i, s: (i, j)),
        ],
        out_specs=[
            pl.BlockSpec((row_tile, col_tile), lambda j, i, s: (i, j)),
            pl.BlockSpec((row_tile, col_tile), lambda j, i, s: (i, j)),
            pl.BlockSpec((1, col_tile), lambda j, i, s: (0, j)),
        ])
    return pl.pallas_call(
        functools.partial(gelu_body, min(256, col_tile)), grid_spec=grid,
        out_shape=[jax.ShapeDtypeStruct((rows, width), bf16)] * 2 + [jax.ShapeDtypeStruct((1, width), f32)],
        compiler_params=params(),
        cost_estimate=pl.CostEstimate(flops=2 * rows * depth * width, bytes_accessed=2 * (rows * depth + depth * width + 3 * rows * width), transcendentals=rows * width),
    )(place, x, weight, bias[None], grad)

def put_body(place_ref, part_ref, *refs):
    refs[-1][...] = part_ref[...].astype(f32)

def put_half(part, place, axis, whole=None):
    rows, width = part.shape
    tile = min(256, rows)
    steps = rows // tile
    shape = (2 * rows, width) if axis == 0 else (rows, 2 * width)
    at = (lambda i, s: (s[0] * steps + i, 0)) if axis == 0 else (lambda i, s: (i, s[0]))
    in_specs = [pl.BlockSpec((tile, width), lambda i, s: (i, 0))]
    args = [place, part]
    alias = {}
    if whole is not None:
        in_specs.append(pl.BlockSpec(memory_space=pl.ANY))
        args.append(whole)
        alias = {2: 0}
    return pl.pallas_call(
        put_body, grid_spec=pltpu.PrefetchScalarGridSpec(num_scalar_prefetch=1, grid=(steps,), in_specs=in_specs, out_specs=pl.BlockSpec((tile, width), at)),
        out_shape=jax.ShapeDtypeStruct(shape, f32), input_output_aliases=alias, compiler_params=params(),
        cost_estimate=pl.CostEstimate(flops=0, bytes_accessed=6 * rows * width, transcendentals=0),
    )(*args)


def matmul(left, right):
    return jnp.dot(left, right, preferred_element_type=f32)


def column_sums(matrix):
    return jnp.sum(matrix.astype(f32), 0)


def swap(block, step):
    count = lax.axis_size("group")
    return lax.ppermute(block, "group", [(i, i ^ step) for i in range(count)])


def exchange(blocks):
    return [blocks[0]] + [swap(blocks[step], step) for step in range(1, len(blocks))]


def gather_blocks(block):
    return exchange([block] * lax.axis_size("group"))


def in_order(blocks):
    me = lax.axis_index("group")
    rows = blocks[0].shape[0]
    whole = jnp.zeros((len(blocks) * rows,) + blocks[0].shape[1:], blocks[0].dtype)
    for step, block in enumerate(blocks):
        start = ((me ^ step) * rows,) + (0,) * (block.ndim - 1)
        whole = lax.dynamic_update_slice(whole, block, start)
    return whole


def scatter_terms(partial):
    count = lax.axis_size("group")
    me = lax.axis_index("group")
    rows = partial.shape[0] // count
    terms = [lax.dynamic_slice_in_dim(partial, me * rows, rows, 0)]
    for step in range(1, count):
        sent = lax.dynamic_slice_in_dim(partial, (me ^ step) * rows, rows, 0)
        terms.append(swap(sent.astype(bf16), step))
    return terms


def add_terms(terms):
    return sum(term.astype(f32) for term in terms)


def scatter_sum(partial):
    return add_terms(scatter_terms(partial))


def gather_rows(block):
    return lax.all_gather(block, "group", axis=0, tiled=True)


def scatter_rows(partial):
    return lax.psum_scatter(
        partial.astype(bf16), "group", scatter_dimension=0, tiled=True
    ).astype(f32)


def reorder(stack):
    me = lax.axis_index("group")
    count = stack.shape[0]
    bit = 1
    while bit < count:
        pairs = stack.reshape((count // (2 * bit), 2, bit) + stack.shape[1:])
        pairs = jnp.where((me & bit) != 0, pairs[:, ::-1], pairs)
        stack = pairs.reshape(stack.shape)
        bit *= 2
    return stack


def after(value, *others):
    return lax.optimization_barrier((value,) + others)[0]


def core_swap(block):
    count = lax.axis_size("replica")
    return lax.ppermute(block, "replica", [(i, i ^ 1) for i in range(count)])


def core_join(mine, axis):
    core = lax.axis_index("replica") % 2
    other = core_swap(mine)
    first = jnp.where(core == 0, mine, other)
    second = jnp.where(core == 0, other, mine)
    return jnp.concatenate([first, second], axis)


class Order:
    def __init__(self):
        self.last = ()

    def __call__(self, *values):
        values = lax.optimization_barrier(values + self.last)[: len(values)]
        return values[0] if len(values) == 1 else values

    def mark(self, *values):
        self.last = values


def replica_sum_small(values):
    count = lax.axis_size("replica")
    step = 1
    while step < count:
        values = values + lax.ppermute(values, "replica", [(i, i ^ step) for i in range(count)])
        step *= 2
    return values


def shards(
    tokens,
    lengths,
    exit_layers,
    pre_gain,
    pre_shift,
    query_weight,
    query_bias,
    key_weight,
    value_weight,
    value_bias,
    out_weight,
    out_bias,
    mid_gain,
    mid_shift,
    up_weight,
    up_bias,
    down_weight,
    down_bias,
    cotangent,
):
    rows, width = tokens.shape
    count = lax.axis_size("group")
    me = lax.axis_index("group")
    cols = width // count
    local = me * rows + jnp.arange(rows, dtype=jnp.int32)
    active = ((local < lengths[0]) & (exit_layers > LAYER)).astype(f32)[:, None]
    core = lax.axis_index("replica") % 2
    other = core_swap(mine)
    first = jnp.where(core == 0, mine, other)
    second = jnp.where(core == 0, other, mine)
    return jnp.concatenate([first, second], axis)


class Order:
    def __init__(self):
        self.last = ()

    def __call__(self, *values):
        values = lax.optimization_barrier(values + self.last)[: len(values)]
        return values[0] if len(values) == 1 else values

    def mark(self, *values):
        self.last = values


def replica_sum_small(values):
    count = lax.axis_size("replica")
    step = 1
    while step < count:
        values = values + lax.ppermute(values, "replica", [(i, i ^ step) for i in range(count)])
        step *= 2
    return values


def shards(
    tokens,
    lengths,
    exit_layers,
    pre_gain,
    pre_shift,
    query_weight,
    query_bias,
    key_weight,
    value_weight,
    value_bias,
    out_weight,
    out_bias,
    mid_gain,
    mid_shift,
    up_weight,
    up_bias,
    down_weight,
    down_bias,
    cotangent,
):
    rows, width = tokens.shape
    count = lax.axis_size("group")
    me = lax.axis_index("group")
    cols = width // count
    local = me * rows + jnp.arange(rows, dtype=jnp.int32)
    active = ((local < lengths[0]) & (exit_layers > LAYER)).astype(f32)[:, None]
    position = jnp.arange(count * rows, dtype=jnp.int32)
    allowed = position[None, :] <= position[:, None]
    core = lax.axis_index("replica") % 2
    half = cols // 2

    grad_out = cotangent.astype(f32)
    branch_grad = (active * grad_out).astype(bf16)
    tokens_all = in_order(gather_blocks(after(tokens, branch_grad)))

    vectors = jnp.concatenate([pre_gain, pre_shift, out_bias, mid_gain, mid_shift, down_bias])
    vectors = vectors.reshape(2, 3 * cols)

    def column_block(step, start, length):
        at = (start, (me ^ step) * cols)
        parts = [
            lax.dynamic_slice(w, at, (length, cols)) for w in (query_weight, key_weight, value_weight)
        ]
        return jnp.concatenate(parts, 1)

    blocks = [vectors] + [
        jnp.concatenate([column_block(step, core * half, half), vectors])
        for step in range(1, count)
    ]
    blocks = exchange(blocks)
    arrived = jnp.stack([block[:half] for block in blocks[1:]])
    vectors = in_order([block[-2:][None] for block in blocks]).reshape(count, 6, cols)
    vectors = vectors.transpose(1, 0, 2).reshape(6, width).astype(f32)
    gain_one, shift_one, obias, gain_two, shift_two, dbias = (vectors[i] for i in range(6))
    others = core_swap(arrived)
    qkv_weight = jnp.zeros((count, 2, half, 3 * cols), bf16)
    for step in range(1, count):
        for place, block in ((core, arrived), (1 - core, others)):
            qkv_weight = lax.dynamic_update_slice(
                qkv_weight, block[step - 1][None, None], (me ^ step, place, 0, 0)
            )
    own = column_block(0, 0, cols).reshape(1, 2, half, 3 * cols)
    qkv_weight = lax.dynamic_update_slice(qkv_weight, own, (me, 0, 0, 0))
    qkv_weight = qkv_weight.reshape(width, 3 * cols)
    everyone = ("replica", "group")
    branch_wide = lax.all_gather(branch_grad, everyone, axis=0, tiled=True)
    seq = count * rows
    branch_all = lax.dynamic_slice_in_dim(branch_wide, lax.axis_index("replica") * seq, seq, 0)

    normed_all, _ = layer_norm(tokens_all.astype(f32))
    attn_in = (normed_all * gain_one + shift_one).astype(bf16)
    qkv_bias = jnp.concatenate([query_bias, jnp.zeros_like(query_bias), value_bias]).astype(f32)
    qkv = (matmul(attn_in, qkv_weight) + qkv_bias).astype(bf16)
    context = attention(qkv)
    attn_out = scatter_sum(matmul(context, out_weight)) + obias
    hidden = tokens.astype(f32) + active * attn_out
    normed_two, factor_two = layer_norm(hidden)
    ffn_in = (normed_two * gain_two + shift_two).astype(bf16)
    act_grad = nt(branch_all, down_weight).astype(bf16)
    ffn_all = in_order(gather_blocks(ffn_in))
    ffn_wide = lax.all_gather(ffn_in, everyone, axis=0, tiled=True)
    here = jnp.full((1,), core, jnp.int32)
    ff = up_weight.shape[1]
    act_low, pre_grad, _ = gelu_product(
        ffn_all, up_weight, up_bias, act_grad, jnp.zeros((1,), jnp.int32), ff, ffn_all.shape[0], 256
    )
    order = Order()
    order.mark(act_low, pre_grad)
    split = ff // 2
    down_half = lax.dynamic_slice(down_weight, (core * split, 0), (split, width))

    partial = nt(pre_grad, up_weight).astype(bf16)
    order.mark(partial)
    ffn_in_grad = scatter_terms(partial)
    wide_grad = nt(order(branch_wide), down_half).astype(bf16)
    order.mark(wide_grad)

    ffn_in_grad = add_terms(order(*ffn_in_grad))
    hidden_grad = grad_out + norm_back(ffn_in_grad * gain_two, normed_two, factor_two)
    attn_grad = (active * hidden_grad).astype(bf16)
    order.mark(attn_grad)
    attn_blocks = gather_blocks(attn_grad)
    branch = matmul(order(act_low), down_weight)
    branch_sums = column_sums(branch_wide)
    order.mark(branch, branch_sums)

    attn_all = in_order(list(order(*attn_blocks)))
    context_grad = nt(attn_all, out_weight).astype(bf16)
    qkv_grad = jnp.concatenate(attention_back(qkv, context_grad), 1)

    qkv_part = tn(attn_in, qkv_grad).astype(bf16).reshape(count, cols, 3 * cols)
    out_part = tn(context, attn_all).astype(bf16)
    out_blocks = [out_part[:, k * cols : (k + 1) * cols] for k in range(count)]
    parts = jnp.concatenate([qkv_part, jnp.stack(out_blocks)], 2)
    piece = lax.psum_scatter(parts, "replica", scatter_dimension=1, tiled=True)
    in_part = nt(after(qkv_grad, parts), qkv_weight)
    order.mark(in_part)
    in_grad = scatter_terms(in_part)

    wide_act, wide_grad, wide_sums = gelu_product(
        order(ffn_wide), up_weight, up_bias, wide_grad, here, split, min(512, rows * count), split
    )
    order.mark(wide_act, wide_grad)

    shared = jnp.stack(
        [
            jnp.sum(in_part * normed_all, 0),
            jnp.sum(in_part, 0),
            jnp.sum(ffn_in_grad * normed_two, 0),
            jnp.sum(ffn_in_grad, 0),
        ]
    )
    shared = reorder(shared.reshape(4, count, cols).transpose(1, 0, 2))
    shared = sum(exchange([shared[k] for k in range(count)]))
    qkv_bias_part = column_sums(qkv_grad)
    small = jnp.concatenate(
        [
            shared.reshape(-1),
            lax.dynamic_slice(column_sums(attn_all), (me * cols,), (cols,)),
            qkv_bias_part[:cols],
            qkv_bias_part[2 * cols :],
        ]
    )
    small = replica_sum_small(small)
    small_parts = [small[k * cols : (k + 1) * cols] for k in range(7)]

    normed_one, factor_one = layer_norm(tokens.astype(f32))
    in_grad = add_terms(order(*in_grad))
    token_grad = (hidden_grad + norm_back(in_grad * gain_one, normed_one, factor_one)).astype(bf16)
    order.mark(token_grad)

    down_grad = tn(order(wide_act), branch_wide).astype(bf16)
    order.mark(down_grad)
    piece = order(piece)
    mixed = reorder(piece[:, :, : 3 * cols])
    mixed = reorder(jnp.stack(exchange([mixed[k] for k in range(count)])))
    mixed = mixed.reshape(count, -1, 3, cols).transpose(1, 2, 0, 3).reshape(-1, 3 * width)
    piece = jnp.concatenate([mixed] + [piece[k, :, 3 * cols :] for k in range(count)], 1)
    order.mark(piece)
    attn_wgrad = lax.all_gather(piece, "replica", axis=0, tiled=True)
    up_grad = tn(order(ffn_wide), wide_grad).astype(bf16)
    order.mark(up_grad)
    down_other, up_other = core_swap(down_grad), core_swap(up_grad)
    down_grad = put_half(down_grad, here, 0)
    up_grad = put_half(up_grad, here, 1)
    down_grad = put_half(down_other, 1 - here, 0, down_grad)
    up_grad = put_half(up_other, 1 - here, 1, up_grad)
    up_bias_grad = core_join(wide_sums.reshape(-1), 0)
    down_bias_grad = lax.dynamic_slice(branch_sums, (me * cols,), (cols,))

    branch = scatter_sum(branch) + dbias
    output = (hidden + active * branch).astype(bf16)
    attn_wgrad = order(attn_wgrad)
    query_wgrad, key_wgrad, value_wgrad, out_wgrad = (
        attn_wgrad[:, k * width : (k + 1) * width].astype(f32) for k in range(4)
    )
    return (
        output,
        token_grad,
        small_parts[0],
        small_parts[1],
        query_wgrad,
        small_parts[5],
        key_wgrad,
        value_wgrad,
        small_parts[6],
        out_wgrad,
        small_parts[4],
        small_parts[2],
        small_parts[3],
        up_grad,
        up_bias_grad,
        down_grad,
        down_bias_grad,
    )


def solution(mesh):
    both = P(("replica", "group"), None)
    vector, by_rows, by_cols = P("group"), P("group", None), P(None, "group")
    return jax.shard_map(
        shards,
        mesh=mesh,
        in_specs=(
            both,
            P("replica"),
            P(("replica", "group")),
            vector,
            vector,
            by_rows,
            vector,
            by_rows,
            by_rows,
            vector,
            by_rows,
            vector,
            vector,
            vector,
            by_cols,
            vector,
            by_rows,
            vector,
            both,
        ),
        out_specs=(
            both,
            both,
            vector,
            vector,
            by_rows,
            vector,
            by_rows,
            by_rows,
            vector,
            by_rows,
            vector,
            vector,
            vector,
            by_cols,
            vector,
            by_rows,
            vector,
        ),
        check_vma=False,
    )
```

```python
import functools

import jax
import jax.numpy as jnp
from jax import lax
from jax.experimental import pallas as pl
from jax.experimental.pallas import tpu as pltpu
from jax.sharding import PartitionSpec as P

HD = 64
LAYER = 12
QB = 128

bf16 = jnp.bfloat16
f32 = jnp.float32


def layer_norm(values):
    center = values - jnp.mean(values, -1, keepdims=True)
    spread = jnp.mean(center * center, -1, keepdims=True)
    factor = lax.rsqrt(spread + 1e-05)
    return (center * factor, factor)


def norm_back(grad, normal, factor):
    return factor * (
        grad
        - jnp.mean(grad, -1, keepdims=True)
        - normal * jnp.mean(grad * normal, -1, keepdims=True)
    )


def params(mb=56):
    return pltpu.CompilerParams(vmem_limit_bytes=mb << 20)

def nt(left, right):
    return lax.dot_general(left, right, (((1,), (1,)), ((), ())), preferred_element_type=f32)
def tn(left, right):
    return lax.dot_general(left, right, (((0,), (0,)), ((), ())), preferred_element_type=f32)

def later(keys, first):
    key = lax.broadcasted_iota(jnp.int32, (keys, QB), 0)
    query = lax.broadcasted_iota(jnp.int32, (keys, QB), 1) + first
    return key <= query

def attend_body(q_ref, k_ref, v_ref, out_ref):
    rows = q_ref.shape[0]
    for first in range(0, rows, QB):
        keys = first + QB
        parts = []
        for lane in range(0, q_ref.shape[1], HD):
            at = slice(lane, lane + HD)
            query = q_ref[first:keys, at] * 0.125
            scores = jnp.where(later(keys, first), nt(k_ref[:keys, at], query), -1e30)
            grown = jnp.exp(scores - jnp.max(scores, 0, keepdims=True))
            probs = grown * (1.0 / jnp.sum(grown, 0, keepdims=True))
            parts.append(tn(probs.astype(bf16), v_ref[:keys, at]))
        out_ref[first:keys, :] = jnp.concatenate(parts, 1).astype(bf16)

def attend_back_body(q_ref, k_ref, v_ref, g_ref, dq_ref, dk_ref, dv_ref, key_acc, value_acc):
    rows = q_ref.shape[0]
    key_acc[...] = jnp.zeros_like(key_acc)
    value_acc[...] = jnp.zeros_like(value_acc)
    for first in range(0, rows, QB):
        keys = first + QB
        q_parts, k_parts, v_parts = [], [], []
        for lane in range(0, q_ref.shape[1], HD):
            at = slice(lane, lane + HD)
            query = q_ref[first:keys, at] * 0.125
            grad = g_ref[first:keys, at]
            key = k_ref[:keys, at]
            scores = jnp.where(later(keys, first), nt(key, query), -1e30)
            grown = jnp.exp(scores - jnp.max(scores, 0, keepdims=True))
            probs = grown * (1.0 / jnp.sum(grown, 0, keepdims=True))
            probs_grad = nt(v_ref[:keys, at], grad)
            delta = jnp.sum(probs * probs_grad, 0, keepdims=True)
            score_grad = (probs * (probs_grad - delta)).astype(bf16)
            v_parts.append(jnp.dot(probs.astype(bf16), grad, preferred_element_type=f32))
            k_parts.append(jnp.dot(score_grad, query, preferred_element_type=f32))
            q_parts.append(tn(score_grad, key) * 0.125)
        dq_ref[first:keys, :] = jnp.concatenate(q_parts, 1).astype(bf16)
        key_acc[:keys, :] += jnp.concatenate(k_parts, 1)
        value_acc[:keys, :] += jnp.concatenate(v_parts, 1)
    dk_ref[...] = key_acc[...].astype(bf16)
    dv_ref[...] = value_acc[...].astype(bf16)

def attention(qkv):
    rows, cols = qkv.shape[0], qkv.shape[1] // 3
    lanes = 2 * HD
    pairs = cols // lanes
    spec = lambda part: pl.BlockSpec((rows, lanes), lambda h: (0, part * pairs + h))
    work = 2 * rows * rows * cols
    return pl.pallas_call(
        attend_body, grid=(pairs,), in_specs=[spec(0), spec(1), spec(2)], out_specs=spec(0),
        out_shape=jax.ShapeDtypeStruct((rows, cols), bf16), compiler_params=params(),
        cost_estimate=pl.CostEstimate(flops=2 * work, bytes_accessed=8 * rows * cols, transcendentals=rows * rows * cols // HD),
    )(qkv, qkv, qkv)

def attention_back(qkv, grad):
    rows, cols = grad.shape
    lanes = 2 * HD
    pairs = cols // lanes
    spec = lambda part: pl.BlockSpec((rows, lanes), lambda h: (0, part * pairs + h))
    work = 2 * rows * rows * cols
    one = jax.ShapeDtypeStruct((rows, cols), bf16)
    return pl.pallas_call(
        attend_back_body, grid=(pairs,), in_specs=[spec(0), spec(1), spec(2), spec(0)], out_specs=[spec(0)] * 3,
        out_shape=[one] * 3, scratch_shapes=[pltpu.VMEM((rows, lanes), f32)] * 2, compiler_params=params(),
        cost_estimate=pl.CostEstimate(flops=5 * work, bytes_accessed=14 * rows * cols, transcendentals=rows * rows * cols // HD),
    )(qkv, qkv, qkv, grad)

def gelu_tiles(tile, first, x_ref, w_ref, b_ref, g_ref, act_ref, grad_ref, sum_ref):
    for start in range(0, w_ref.shape[1], tile):
        at = slice(start, start + tile)
        value = jnp.dot(x_ref[...], w_ref[:, at], preferred_element_type=f32) + b_ref[:, at].astype(f32)
        square = value * value
        tangent = jnp.tanh(value * (0.7978845608 + (0.7978845608 * 0.044715) * square))
        share = 0.5 * value
        act_ref[:, at] = (share + share * tangent).astype(bf16)
        bend = share * (0.7978845608 + (3.0 * 0.7978845608 * 0.044715) * square)
        slope = (0.5 + 0.5 * tangent) + bend * (1.0 - tangent * tangent)
        grad = g_ref[:, at].astype(f32) * slope
        grad_ref[:, at] = grad.astype(bf16)
        total = jnp.sum(grad, 0, keepdims=True)
        if first is not True:
            total = jnp.where(first, total, sum_ref[:, at] + total)
        sum_ref[:, at] = total


def gelu_body(tile, place_ref, *refs):
    gelu_tiles(tile, pl.program_id(1) == 0, *refs)


def gelu_product(x, weight, bias, grad, place, width, row_tile, col_tile):
    rows, depth = x.shape
    steps = width // col_tile
    grid = pltpu.PrefetchScalarGridSpec(
        num_scalar_prefetch=1, grid=(steps, rows // row_tile),
        in_specs=[
            pl.BlockSpec((row_tile, depth), lambda j, i, s: (i, 0)),
            pl.BlockSpec((depth, col_tile), lambda j, i, s: (0, s[0] * steps + j)),
            pl.BlockSpec((1, col_tile), lambda j, i, s: (0, s[0] * steps + j)),
            pl.BlockSpec((row_tile, col_tile), lambda j, i, s: (i, j)),
        ],
        out_specs=[
            pl.BlockSpec((row_tile, col_tile), lambda j, i, s: (i, j)),
            pl.BlockSpec((row_tile, col_tile), lambda j, i, s: (i, j)),
            pl.BlockSpec((1, col_tile), lambda j, i, s: (0, j)),
        ])
    return pl.pallas_call(
        functools.partial(gelu_body, min(256, col_tile)), grid_spec=grid,
        out_shape=[jax.ShapeDtypeStruct((rows, width), bf16)] * 2 + [jax.ShapeDtypeStruct((1, width), f32)],
        compiler_params=params(),
        cost_estimate=pl.CostEstimate(flops=2 * rows * depth * width, bytes_accessed=2 * (rows * depth + depth * width + 3 * rows * width), transcendentals=rows * width),
    )(place, x, weight, bias[None], grad)

def gelu_blocks_body(tile, member_ref, *refs):
    count = len(refs) - 7
    blocks, (w_ref, b_ref, g_ref, act_ref, grad_ref, sum_ref, x_ref) = refs[:count], refs[count:]
    rows = blocks[0].shape[0]

    @pl.when(pl.program_id(0) == 0)
    def _():
        for k, block in enumerate(blocks):
            start = pl.multiple_of(member_ref[k] * rows, rows)
            x_ref[pl.ds(start, rows), :] = block[...]

    gelu_tiles(tile, True, x_ref, w_ref, b_ref, g_ref, act_ref, grad_ref, sum_ref)


def gelu_product_blocks(blocks, members, weight, bias, grad, col_tile):
    (rows, depth), count, width = blocks[0].shape, len(blocks), weight.shape[1]
    tall = count * rows
    grid = pltpu.PrefetchScalarGridSpec(
        num_scalar_prefetch=1,
        grid=(width // col_tile,),
        in_specs=[pl.BlockSpec((rows, depth), lambda j, s: (0, 0))] * count
        + [
            pl.BlockSpec((depth, col_tile), lambda j, s: (0, j)),
            pl.BlockSpec((1, col_tile), lambda j, s: (0, j)),
            pl.BlockSpec((tall, col_tile), lambda j, s: (0, j)),
        ],
        out_specs=[
            pl.BlockSpec((tall, col_tile), lambda j, s: (0, j)),
            pl.BlockSpec((tall, col_tile), lambda j, s: (0, j)),
            pl.BlockSpec((1, col_tile), lambda j, s: (0, j)),
        ],
        scratch_shapes=[pltpu.VMEM((tall, depth), bf16)],
    )
    return pl.pallas_call(
        functools.partial(gelu_blocks_body, col_tile),
        grid_spec=grid,
        out_shape=[jax.ShapeDtypeStruct((tall, width), bf16)] * 2
        + [jax.ShapeDtypeStruct((1, width), f32)],
        compiler_params=params(),
        cost_estimate=pl.CostEstimate(
            flops=2 * tall * depth * width,
            bytes_accessed=2 * (tall * depth + depth * width + 3 * tall * width),
            transcendentals=tall * width,
        ),
    )(members, *blocks, weight, bias[None], grad)


def qkv_body(count, at_ref, x_ref, own_ref, *refs):
    blocks, b_ref, out_ref = refs[:-2], refs[-2], refs[-1]
    cols = own_ref.shape[0]
    half = cols // 2
    at = pl.multiple_of(at_ref[0], cols)
    total = jnp.dot(x_ref[:, pl.ds(at, cols)], own_ref[...], preferred_element_type=f32)
    for k, block in enumerate(blocks):
        at = pl.multiple_of(at_ref[1 + k], half)
        total += jnp.dot(x_ref[:, pl.ds(at, half)], block[...], preferred_element_type=f32)
    out_ref[...] = (total + b_ref[...].astype(f32)).astype(bf16)


def qkv_product(x, own, blocks, starts, bias):
    rows, width = x.shape
    cols = own.shape[0]
    half = cols // 2
    column = lambda size: pl.BlockSpec((size, cols), lambda j, s: (0, j))
    return pl.pallas_call(
        functools.partial(qkv_body, len(blocks)),
        grid_spec=pltpu.PrefetchScalarGridSpec(
            num_scalar_prefetch=1,
            grid=(3,),
            in_specs=[pl.BlockSpec((rows, width), lambda j, s: (0, 0)), column(cols)]
            + [column(half)] * len(blocks)
            + [column(1)],
            out_specs=column(rows),
        ),
        out_shape=jax.ShapeDtypeStruct((rows, 3 * cols), bf16),
        compiler_params=params(),
        cost_estimate=pl.CostEstimate(
            flops=6 * rows * width * cols,
            bytes_accessed=2 * (rows * width + 3 * width * cols + 3 * rows * cols),
            transcendentals=0,
        ),
    )(starts, x, own, *blocks, bias[None])


def put_body(place_ref, part_ref, *refs):
    refs[-1][...] = part_ref[...].astype(f32)

def put_half(part, place, axis, whole=None):
    rows, width = part.shape
    tile = min(256, rows)
    steps = rows // tile
    shape = (2 * rows, width) if axis == 0 else (rows, 2 * width)
    at = (lambda i, s: (s[0] * steps + i, 0)) if axis == 0 else (lambda i, s: (i, s[0]))
    in_specs = [pl.BlockSpec((tile, width), lambda i, s: (i, 0))]
    args = [place, part]
    alias = {}
    if whole is not None:
        in_specs.append(pl.BlockSpec(memory_space=pl.ANY))
        args.append(whole)
        alias = {2: 0}
    return pl.pallas_call(
        put_body, grid_spec=pltpu.PrefetchScalarGridSpec(num_scalar_prefetch=1, grid=(steps,), in_specs=in_specs, out_specs=pl.BlockSpec((tile, width), at)),
        out_shape=jax.ShapeDtypeStruct(shape, f32), input_output_aliases=alias, compiler_params=params(),
        cost_estimate=pl.CostEstimate(flops=0, bytes_accessed=6 * rows * width, transcendentals=0),
    )(*args)


def put_blocks_body(block_ref, *out_refs):
    cols = out_refs[0].shape[1]
    for w, out_ref in enumerate(out_refs):
        out_ref[...] = block_ref[0, :, w * cols : (w + 1) * cols].astype(f32)


def put_blocks(stack):
    count, rows, width = stack.shape
    cols = width // 4
    return pl.pallas_call(
        put_blocks_body,
        grid=(count,),
        in_specs=[pl.BlockSpec((1, rows, width), lambda i: (i, 0, 0))],
        out_specs=[pl.BlockSpec((rows, cols), lambda i: (0, i))] * 4,
        out_shape=[jax.ShapeDtypeStruct((rows, count * cols), f32)] * 4,
        compiler_params=params(),
        cost_estimate=pl.CostEstimate(
            flops=0, bytes_accessed=6 * count * rows * width, transcendentals=0
        ),
    )(stack)


def matmul(left, right):
    return jnp.dot(left, right, preferred_element_type=f32)


def column_sums(matrix):
    return jnp.sum(matrix.astype(f32), 0)


def swap(block, step):
    count = lax.axis_size("group")
    return lax.ppermute(block, "group", [(i, i ^ step) for i in range(count)])


def exchange(blocks):
    return [blocks[0]] + [swap(blocks[step], step) for step in range(1, len(blocks))]


def gather_blocks(block):
    return exchange([block] * lax.axis_size("group"))


def in_order(blocks):
    me = lax.axis_index("group")
    rows = blocks[0].shape[0]
    whole = jnp.zeros((len(blocks) * rows,) + blocks[0].shape[1:], blocks[0].dtype)
    for step, block in enumerate(blocks):
        start = ((me ^ step) * rows,) + (0,) * (block.ndim - 1)
        whole = lax.dynamic_update_slice(whole, block, start)
    return whole


def scatter_terms(partial):
    count = lax.axis_size("group")
    me = lax.axis_index("group")
    rows = partial.shape[0] // count
    terms = [lax.dynamic_slice_in_dim(partial, me * rows, rows, 0)]
    for step in range(1, count):
        sent = lax.dynamic_slice_in_dim(partial, (me ^ step) * rows, rows, 0)
        terms.append(swap(sent.astype(bf16), step))
    return terms


def add_terms(terms):
    return sum(term.astype(f32) for term in terms)


def scatter_sum(partial):
    return add_terms(scatter_terms(partial))


def gather_rows(block):
    return lax.all_gather(block, "group", axis=0, tiled=True)


def scatter_rows(partial):
    return lax.psum_scatter(
        partial.astype(bf16), "group", scatter_dimension=0, tiled=True
    ).astype(f32)


def reorder(stack):
    me = lax.axis_index("group")
    count = stack.shape[0]
    bit = 1
    while bit < count:
        pairs = stack.reshape((count // (2 * bit), 2, bit) + stack.shape[1:])
        pairs = jnp.where((me & bit) != 0, pairs[:, ::-1], pairs)
        stack = pairs.reshape(stack.shape)
        bit *= 2
    return stack


def after(value, *others):
    return lax.optimization_barrier((value,) + others)[0]


def core_swap(block):
    count = lax.axis_size("replica")
    return lax.ppermute(block, "replica", [(i, i ^ 1) for i in range(count)])


def core_join(mine, axis):
    core = lax.axis_index("replica") % 2
    other = core_swap(mine)
    first = jnp.where(core == 0, mine, other)
    second = jnp.where(core == 0, other, mine)
    return jnp.concatenate([first, second], axis)


class Order:
    def __init__(self):
        self.last = ()

    def __call__(self, *values):
        values = lax.optimization_barrier(values + self.last)[: len(values)]
        return values[0] if len(values) == 1 else values

    def mark(self, *values):
        self.last = values


def replica_swap(values, step):
    count = lax.axis_size("replica")
    return lax.ppermute(values, "replica", [(i, i ^ step) for i in range(count)])


def shards(
    tokens,
    lengths,
    exit_layers,
    pre_gain,
    pre_shift,
    query_weight,
    query_bias,
    key_weight,
    value_weight,
    value_bias,
    out_weight,
    out_bias,
    mid_gain,
    mid_shift,
    up_weight,
    up_bias,
    down_weight,
    down_bias,
    cotangent,
):
    rows, width = tokens.shape
    count = lax.axis_size("group")
    me = lax.axis_index("group")
    cols = width // count
    local = me * rows + jnp.arange(rows, dtype=jnp.int32)
    active = ((local < lengths[0]) & (exit_layers > LAYER)).astype(f32)[:, None]
    core = lax.axis_index("replica") % 2
    other = core_swap(mine)
    first = jnp.where(core == 0, mine, other)
    second = jnp.where(core == 0, other, mine)
    return jnp.concatenate([first, second], axis)


class Order:
    def __init__(self):
        self.last = ()

    def __call__(self, *values):
        values = lax.optimization_barrier(values + self.last)[: len(values)]
        return values[0] if len(values) == 1 else values

    def mark(self, *values):
        self.last = values


def replica_sum_small(values):
    count = lax.axis_size("replica")
    step = 1
    while step < count:
        values = values + lax.ppermute(values, "replica", [(i, i ^ step) for i in range(count)])
        step *= 2
    return values


def shards(
    tokens,
    lengths,
    exit_layers,
    pre_gain,
    pre_shift,
    query_weight,
    query_bias,
    key_weight,
    value_weight,
    value_bias,
    out_weight,
    out_bias,
    mid_gain,
    mid_shift,
    up_weight,
    up_bias,
    down_weight,
    down_bias,
    cotangent,
):
    rows, width = tokens.shape
    count = lax.axis_size("group")
    me = lax.axis_index("group")
    cols = width // count
    local = me * rows + jnp.arange(rows, dtype=jnp.int32)
    active = ((local < lengths[0]) & (exit_layers > LAYER)).astype(f32)[:, None]
    position = jnp.arange(count * rows, dtype=jnp.int32)
    allowed = position[None, :] <= position[:, None]
    core = lax.axis_index("replica") % 2
    half = cols // 2

    grad_out = cotangent.astype(f32)
    branch_grad = (active * grad_out).astype(bf16)
    vectors = jnp.concatenate([pre_gain, pre_shift, out_bias, mid_gain, mid_shift, down_bias])
    extra = -(-vectors.size // width)
    vectors = jnp.pad(vectors, (0, extra * width - vectors.size)).reshape(extra, width)
    sent = after(jnp.concatenate([tokens, vectors]), branch_grad)
    got = gather_blocks(sent)
    tokens_all = in_order([block[:rows] for block in got])
    vectors = in_order([block[rows:].reshape(1, -1)[:, : 6 * cols] for block in got])
    vectors = vectors.reshape(count, 6, cols).transpose(1, 0, 2).reshape(6, width).astype(f32)
    gain_one, shift_one, obias, gain_two, shift_two, dbias = (vectors[i] for i in range(6))

    def column_block(step, start, length):
        at = (start, (me ^ step) * cols)
        parts = [
            lax.dynamic_slice(w, at, (length, cols)) for w in (query_weight, key_weight, value_weight)
        ]
        return jnp.concatenate(parts, 1)

    normed_all, _ = layer_norm(tokens_all.astype(f32))
    attn_in = (normed_all * gain_one + shift_one).astype(bf16)
    own = column_block(0, 0, cols)
    blocks = exchange([own] + [column_block(step, core * half, half) for step in range(1, count)])
    arrived = [after(block, attn_in, own) for block in blocks[1:]]
    others = [core_swap(block) for block in arrived]
    starts = [(me ^ k) * cols + core * half for k in range(1, count)]
    starts += [(me ^ k) * cols + (1 - core) * half for k in range(1, count)]
    starts = jnp.stack([me * cols] + starts).astype(jnp.int32)
    everyone = ("replica", "group")
    branch_wide = lax.all_gather(branch_grad, everyone, axis=0, tiled=True)
    seq = count * rows
    branch_all = lax.dynamic_slice_in_dim(branch_wide, lax.axis_index("replica") * seq, seq, 0)

    qkv_bias = jnp.concatenate([query_bias, jnp.zeros_like(query_bias), value_bias])
    qkv = qkv_product(attn_in, own, arrived + others, starts, qkv_bias)
    context = attention(qkv)
    attn_out = scatter_sum(matmul(context, out_weight)) + obias
    hidden = tokens.astype(f32) + active * attn_out
    normed_two, factor_two = layer_norm(hidden)
    ffn_in = (normed_two * gain_two + shift_two).astype(bf16)
    act_grad = nt(branch_all, down_weight).astype(bf16)
    ffn_blocks = gather_blocks(ffn_in)
    ffn_blocks = ffn_blocks[:1] + [after(block, act_grad) for block in ffn_blocks[1:]]
    ffn_wide = lax.all_gather(ffn_in, everyone, axis=0, tiled=True)
    here = jnp.full((1,), core, jnp.int32)
    ff = up_weight.shape[1]
    members = (me ^ jnp.arange(count, dtype=jnp.int32)).astype(jnp.int32)
    act_low, pre_grad, _ = gelu_product_blocks(
        ffn_blocks, members, up_weight, up_bias, act_grad, 256
    )
    order = Order()
    order.mark(act_low, pre_grad)
    split = ff // 2
    down_half = lax.dynamic_slice(down_weight, (core * split, 0), (split, width))

    partial = nt(pre_grad, up_weight).astype(bf16)
    order.mark(partial)
    ffn_in_grad = scatter_terms(partial)
    wide_grad = nt(order(branch_wide), down_half).astype(bf16)
    order.mark(wide_grad)

    ffn_in_grad = add_terms(order(*ffn_in_grad))
    hidden_grad = grad_out + norm_back(ffn_in_grad * gain_two, normed_two, factor_two)
    attn_grad = (active * hidden_grad).astype(bf16)
    order.mark(attn_grad)
    attn_blocks = gather_blocks(attn_grad)
    branch = matmul(order(act_low), down_weight)
    order.mark(branch)
    branch_sums = column_sums(order(branch_wide))
    order.mark(branch_sums)

    attn_all = in_order(list(order(*attn_blocks)))
    context_grad = nt(attn_all, out_weight).astype(bf16)
    out_part = tn(context, attn_all).astype(bf16)
    qkv_grad = jnp.concatenate(attention_back(qkv, after(context_grad, out_part)), 1)

    qkv_part = tn(attn_in, qkv_grad).astype(bf16).reshape(count, cols, 3 * cols)
    out_blocks = [out_part[:, k * cols : (k + 1) * cols] for k in range(count)]
    parts = jnp.concatenate([qkv_part, jnp.stack(out_blocks)], 2)
    piece = lax.psum_scatter(parts, "replica", scatter_dimension=1, tiled=True)
    qkv_weight = jnp.zeros((width, 3 * cols), bf16)
    for start, block in zip([me * cols] + [starts[1 + k] for k in range(2 * count - 2)], [own] + arrived + others):
        block = after(block, hidden)
        qkv_weight = lax.dynamic_update_slice(qkv_weight, block, (start, 0))
    in_part = nt(after(qkv_grad, parts), qkv_weight)
    order.mark(in_part)
    in_grad = scatter_terms(in_part)

    wide_act, wide_grad, wide_sums = gelu_product(
        order(ffn_wide), up_weight, up_bias, wide_grad, here, split, min(512, rows * count), split
    )
    order.mark(wide_act, wide_grad)

    shared = jnp.stack(
        [
            jnp.sum(in_part * normed_all, 0),
            jnp.sum(in_part, 0),
            jnp.sum(ffn_in_grad * normed_two, 0),
            jnp.sum(ffn_in_grad, 0),
        ]
    )
    qkv_bias_part = column_sums(qkv_grad)
    shared = reorder(shared.reshape(4, count, cols).transpose(1, 0, 2))
    shared, qkv_bias_part = order(shared, qkv_bias_part)
    shared = exchange([shared[k] for k in range(count)])

    def join_shared():
        values = jnp.concatenate(
            [
                sum(order(*shared)).reshape(-1),
                lax.dynamic_slice(column_sums(attn_all), (me * cols,), (cols,)),
                qkv_bias_part[:cols],
                qkv_bias_part[2 * cols :],
            ]
        )
        order.mark(values)
        return values, replica_swap(values, 1)

    def small_step(step):
        def run(pair):
            values, arrived = pair
            values = values + order(arrived)
            order.mark(values)
            return values if 2 * step >= replicas else (values, replica_swap(values, 2 * step))

        return run

    replicas = lax.axis_size("replica")
    small_steps, step = [lambda _: join_shared()], 1
    while step < replicas:
        small_steps.append(small_step(step))
        step *= 2

    normed_one, factor_one = layer_norm(tokens.astype(f32))
    in_grad = add_terms(order(*in_grad))
    token_grad = (hidden_grad + norm_back(in_grad * gain_one, normed_one, factor_one)).astype(bf16)
    order.mark(token_grad)

    down_grad = tn(order(wide_act), branch_wide).astype(bf16)
    order.mark(down_grad)
    small = small_steps[0](None)
    piece = order(piece)
    size = (1,) + piece.shape[1:2] + (3 * cols,)
    sent = [lax.dynamic_slice(piece, (me ^ step, 0, 0), size) for step in range(1, count)]
    sent = lax.optimization_barrier(tuple(sent))
    owned = lax.optimization_barrier(tuple(swap(s, k + 1) for k, s in enumerate(sent)))
    for step in range(1, count):
        piece = lax.dynamic_update_slice(piece, owned[step - 1], (me ^ step, 0, 0))
    order.mark(piece)
    attn_wgrad = lax.all_gather(piece, "replica", axis=1, tiled=True)
    small = small_steps[1](small)
    up_grad = tn(order(ffn_wide), wide_grad).astype(bf16)
    order.mark(up_grad)
    branch = scatter_terms(order(branch))
    down_other, up_other = core_swap(down_grad), core_swap(up_grad)
    down_grad = put_half(order(down_grad), here, 0)
    order.mark(down_grad)
    small = small_steps[2](small)
    up_grad = put_half(order(up_grad), here, 1)
    order.mark(up_grad)
    for run in small_steps[3:]:
        small = run(small)
    down_grad = put_half(order(down_other), 1 - here, 0, down_grad)
    up_grad = put_half(up_other, 1 - here, 1, up_grad)
    order.mark(down_grad, up_grad)
    output = (hidden + active * (add_terms(order(*branch)) + dbias)).astype(bf16)
    order.mark(output)
    up_bias_grad = core_join(wide_sums.reshape(-1), 0)
    down_bias_grad = lax.dynamic_slice(branch_sums, (me * cols,), (cols,))

    query_wgrad, key_wgrad, value_wgrad, out_wgrad = put_blocks(order(attn_wgrad))
    small_parts = [small[k * cols : (k + 1) * cols] for k in range(7)]
    return (
        output,
        token_grad,
        small_parts[0],
        small_parts[1],
        query_wgrad,
        small_parts[5],
        key_wgrad,
        value_wgrad,
        small_parts[6],
        out_wgrad,
        small_parts[4],
        small_parts[2],
        small_parts[3],
        up_grad,
        up_bias_grad,
        down_grad,
        down_bias_grad,
    )


def solution(mesh):
    both = P(("replica", "group"), None)
    vector, by_rows, by_cols = P("group"), P("group", None), P(None, "group")
    return jax.shard_map(
        shards,
        mesh=mesh,
        in_specs=(
            both,
            P("replica"),
            P(("replica", "group")),
            vector,
            vector,
            by_rows,
            vector,
            by_rows,
            by_rows,
            vector,
            by_rows,
            vector,
            vector,
            vector,
            by_cols,
            vector,
            by_rows,
            vector,
            both,
        ),
        out_specs=(
            both,
            both,
            vector,
            vector,
            by_rows,
            vector,
            by_rows,
            by_rows,
            vector,
            by_rows,
            vector,
            vector,
            vector,
            by_cols,
            vector,
            by_rows,
            vector,
        ),
        check_vma=False,
    )
```

```python
import functools

import jax
import jax.numpy as jnp
from jax import lax
from jax.experimental import pallas as pl
from jax.experimental.pallas import tpu as pltpu
from jax.sharding import PartitionSpec as P

HD = 64
LAYER = 12
QB = 128

bf16 = jnp.bfloat16
f32 = jnp.float32


def layer_norm(values):
    center = values - jnp.mean(values, -1, keepdims=True)
    spread = jnp.mean(center * center, -1, keepdims=True)
    factor = lax.rsqrt(spread + 1e-05)
    return (center * factor, factor)


def norm_back(grad, normal, factor):
    return factor * (
        grad
        - jnp.mean(grad, -1, keepdims=True)
        - normal * jnp.mean(grad * normal, -1, keepdims=True)
    )


def params(mb=56):
    return pltpu.CompilerParams(vmem_limit_bytes=mb << 20)

def nt(left, right):
    return lax.dot_general(left, right, (((1,), (1,)), ((), ())), preferred_element_type=f32)
def tn(left, right):
    return lax.dot_general(left, right, (((0,), (0,)), ((), ())), preferred_element_type=f32)

def later(keys, first):
    key = lax.broadcasted_iota(jnp.int32, (keys, QB), 0)
    query = lax.broadcasted_iota(jnp.int32, (keys, QB), 1) + first
    return key <= query

def attend_body(q_ref, k_ref, v_ref, out_ref):
    rows = q_ref.shape[0]
    for first in range(0, rows, QB):
        keys = first + QB
        parts = []
        for lane in range(0, q_ref.shape[1], HD):
            at = slice(lane, lane + HD)
            query = q_ref[first:keys, at] * 0.125
            scores = jnp.where(later(keys, first), nt(k_ref[:keys, at], query), -1e30)
            grown = jnp.exp(scores - jnp.max(scores, 0, keepdims=True))
            probs = grown * (1.0 / jnp.sum(grown, 0, keepdims=True))
            parts.append(tn(probs.astype(bf16), v_ref[:keys, at]))
        out_ref[first:keys, :] = jnp.concatenate(parts, 1).astype(bf16)

def attend_back_body(q_ref, k_ref, v_ref, g_ref, dq_ref, dk_ref, dv_ref, key_acc, value_acc):
    rows = q_ref.shape[0]
    key_acc[...] = jnp.zeros_like(key_acc)
    value_acc[...] = jnp.zeros_like(value_acc)
    for first in range(0, rows, QB):
        keys = first + QB
        q_parts, k_parts, v_parts = [], [], []
        for lane in range(0, q_ref.shape[1], HD):
            at = slice(lane, lane + HD)
            query = q_ref[first:keys, at] * 0.125
            grad = g_ref[first:keys, at]
            key = k_ref[:keys, at]
            scores = jnp.where(later(keys, first), nt(key, query), -1e30)
            grown = jnp.exp(scores - jnp.max(scores, 0, keepdims=True))
            probs = grown * (1.0 / jnp.sum(grown, 0, keepdims=True))
            probs_grad = nt(v_ref[:keys, at], grad)
            delta = jnp.sum(probs * probs_grad, 0, keepdims=True)
            score_grad = (probs * (probs_grad - delta)).astype(bf16)
            v_parts.append(jnp.dot(probs.astype(bf16), grad, preferred_element_type=f32))
            k_parts.append(jnp.dot(score_grad, query, preferred_element_type=f32))
            q_parts.append(tn(score_grad, key) * 0.125)
        dq_ref[first:keys, :] = jnp.concatenate(q_parts, 1).astype(bf16)
        key_acc[:keys, :] += jnp.concatenate(k_parts, 1)
        value_acc[:keys, :] += jnp.concatenate(v_parts, 1)
    dk_ref[...] = key_acc[...].astype(bf16)
    dv_ref[...] = value_acc[...].astype(bf16)

def attention(qkv):
    rows, cols = qkv.shape[0], qkv.shape[1] // 3
    lanes = 2 * HD
    pairs = cols // lanes
    spec = lambda part: pl.BlockSpec((rows, lanes), lambda h: (0, part * pairs + h))
    work = 2 * rows * rows * cols
    return pl.pallas_call(
        attend_body, grid=(pairs,), in_specs=[spec(0), spec(1), spec(2)], out_specs=spec(0),
        out_shape=jax.ShapeDtypeStruct((rows, cols), bf16), compiler_params=params(),
        cost_estimate=pl.CostEstimate(flops=2 * work, bytes_accessed=8 * rows * cols, transcendentals=rows * rows * cols // HD),
    )(qkv, qkv, qkv)

def attention_back(qkv, grad):
    rows, cols = grad.shape
    lanes = 2 * HD
    pairs = cols // lanes
    spec = lambda part: pl.BlockSpec((rows, lanes), lambda h: (0, part * pairs + h))
    work = 2 * rows * rows * cols
    one = jax.ShapeDtypeStruct((rows, cols), bf16)
    return pl.pallas_call(
        attend_back_body, grid=(pairs,), in_specs=[spec(0), spec(1), spec(2), spec(0)], out_specs=[spec(0)] * 3,
        out_shape=[one] * 3, scratch_shapes=[pltpu.VMEM((rows, lanes), f32)] * 2, compiler_params=params(),
        cost_estimate=pl.CostEstimate(flops=5 * work, bytes_accessed=14 * rows * cols, transcendentals=rows * rows * cols // HD),
    )(qkv, qkv, qkv, grad)

def gelu_tiles(tile, first, x_ref, w_ref, b_ref, g_ref, act_ref, grad_ref, sum_ref):
    for start in range(0, w_ref.shape[1], tile):
        at = slice(start, start + tile)
        value = jnp.dot(x_ref[...], w_ref[:, at], preferred_element_type=f32) + b_ref[:, at].astype(f32)
        square = value * value
        tangent = jnp.tanh(value * (0.7978845608 + (0.7978845608 * 0.044715) * square))
        share = 0.5 * value
        act_ref[:, at] = (share + share * tangent).astype(bf16)
        bend = share * (0.7978845608 + (3.0 * 0.7978845608 * 0.044715) * square)
        slope = (0.5 + 0.5 * tangent) + bend * (1.0 - tangent * tangent)
        grad = g_ref[:, at].astype(f32) * slope
        grad_ref[:, at] = grad.astype(bf16)
        total = jnp.sum(grad, 0, keepdims=True)
        if first is not True:
            total = jnp.where(first, total, sum_ref[:, at] + total)
        sum_ref[:, at] = total


def gelu_body(tile, place_ref, *refs):
    gelu_tiles(tile, pl.program_id(1) == 0, *refs)


def gelu_product(x, weight, bias, grad, place, width, row_tile, col_tile):
    rows, depth = x.shape
    steps = width // col_tile
    grid = pltpu.PrefetchScalarGridSpec(
        num_scalar_prefetch=1, grid=(steps, rows // row_tile),
        in_specs=[
            pl.BlockSpec((row_tile, depth), lambda j, i, s: (i, 0)),
            pl.BlockSpec((depth, col_tile), lambda j, i, s: (0, s[0] * steps + j)),
            pl.BlockSpec((1, col_tile), lambda j, i, s: (0, s[0] * steps + j)),
            pl.BlockSpec((row_tile, col_tile), lambda j, i, s: (i, j)),
        ],
        out_specs=[
            pl.BlockSpec((row_tile, col_tile), lambda j, i, s: (i, j)),
            pl.BlockSpec((row_tile, col_tile), lambda j, i, s: (i, j)),
            pl.BlockSpec((1, col_tile), lambda j, i, s: (0, j)),
        ])
    return pl.pallas_call(
        functools.partial(gelu_body, min(256, col_tile)), grid_spec=grid,
        out_shape=[jax.ShapeDtypeStruct((rows, width), bf16)] * 2 + [jax.ShapeDtypeStruct((1, width), f32)],
        compiler_params=params(),
        cost_estimate=pl.CostEstimate(flops=2 * rows * depth * width, bytes_accessed=2 * (rows * depth + depth * width + 3 * rows * width), transcendentals=rows * width),
    )(place, x, weight, bias[None], grad)

def parts_body(x_ref, q_ref, k_ref, v_ref, context_ref, grad_ref, out_ref):
    cols = q_ref.shape[1]
    for w, ref in enumerate((q_ref, k_ref, v_ref)):
        out_ref[0, :, w * cols : (w + 1) * cols] = tn(x_ref[...], ref[...]).astype(bf16)
    out_ref[0, :, 3 * cols :] = tn(context_ref[...], grad_ref[...]).astype(bf16)


def weight_parts(x, query_grad, key_grad, value_grad, context, grad):
    rows, cols = context.shape
    count = x.shape[1] // cols
    whole = pl.BlockSpec((rows, cols), lambda i: (0, 0))
    block = pl.BlockSpec((rows, cols), lambda i: (0, i))
    return pl.pallas_call(
        parts_body,
        grid=(count,),
        in_specs=[block, whole, whole, whole, whole, block],
        out_specs=pl.BlockSpec((1, cols, 4 * cols), lambda i: (i, 0, 0)),
        out_shape=jax.ShapeDtypeStruct((count, cols, 4 * cols), bf16),
        compiler_params=params(),
        cost_estimate=pl.CostEstimate(
            flops=8 * count * rows * cols * cols,
            bytes_accessed=2 * (2 * rows * count * cols + 4 * rows * cols + 4 * count * cols * cols),
            transcendentals=0,
        ),
    )(x, query_grad, key_grad, value_grad, context, grad)


def gelu_blocks_body(tile, member_ref, *refs):
    count = len(refs) - 7
    blocks, (w_ref, b_ref, g_ref, act_ref, grad_ref, sum_ref, x_ref) = refs[:count], refs[count:]
    rows = blocks[0].shape[0]

    @pl.when(pl.program_id(0) == 0)
    def _():
        for k, block in enumerate(blocks):
            start = pl.multiple_of(member_ref[k] * rows, rows)
            x_ref[pl.ds(start, rows), :] = block[...]

    gelu_tiles(tile, True, x_ref, w_ref, b_ref, g_ref, act_ref, grad_ref, sum_ref)


def gelu_product_blocks(blocks, members, weight, bias, grad, col_tile):
    (rows, depth), count, width = blocks[0].shape, len(blocks), weight.shape[1]
    tall = count * rows
    grid = pltpu.PrefetchScalarGridSpec(
        num_scalar_prefetch=1,
        grid=(width // col_tile,),
        in_specs=[pl.BlockSpec((rows, depth), lambda j, s: (0, 0))] * count
        + [
            pl.BlockSpec((depth, col_tile), lambda j, s: (0, j)),
            pl.BlockSpec((1, col_tile), lambda j, s: (0, j)),
            pl.BlockSpec((tall, col_tile), lambda j, s: (0, j)),
        ],
        out_specs=[
            pl.BlockSpec((tall, col_tile), lambda j, s: (0, j)),
            pl.BlockSpec((tall, col_tile), lambda j, s: (0, j)),
            pl.BlockSpec((1, col_tile), lambda j, s: (0, j)),
        ],
        scratch_shapes=[pltpu.VMEM((tall, depth), bf16)],
    )
    return pl.pallas_call(
        functools.partial(gelu_blocks_body, col_tile),
        grid_spec=grid,
        out_shape=[jax.ShapeDtypeStruct((tall, width), bf16)] * 2
        + [jax.ShapeDtypeStruct((1, width), f32)],
        compiler_params=params(),
        cost_estimate=pl.CostEstimate(
            flops=2 * tall * depth * width,
            bytes_accessed=2 * (tall * depth + depth * width + 3 * tall * width),
            transcendentals=tall * width,
        ),
    )(members, *blocks, weight, bias[None], grad)


def qkv_body(count, at_ref, x_ref, own_ref, *refs):
    blocks, b_ref, out_ref = refs[:-2], refs[-2], refs[-1]
    cols = own_ref.shape[0]
    half = cols // 2
    at = pl.multiple_of(at_ref[0], cols)
    total = jnp.dot(x_ref[:, pl.ds(at, cols)], own_ref[...], preferred_element_type=f32)
    for k, block in enumerate(blocks):
        at = pl.multiple_of(at_ref[1 + k], half)
        total += jnp.dot(x_ref[:, pl.ds(at, half)], block[...], preferred_element_type=f32)
    out_ref[...] = (total + b_ref[...].astype(f32)).astype(bf16)


def qkv_product(x, own, blocks, starts, bias):
    rows, width = x.shape
    cols = own.shape[0]
    half = cols // 2
    column = lambda size: pl.BlockSpec((size, cols), lambda j, s: (0, j))
    return pl.pallas_call(
        functools.partial(qkv_body, len(blocks)),
        grid_spec=pltpu.PrefetchScalarGridSpec(
            num_scalar_prefetch=1,
            grid=(3,),
            in_specs=[pl.BlockSpec((rows, width), lambda j, s: (0, 0)), column(cols)]
            + [column(half)] * len(blocks)
            + [column(1)],
            out_specs=column(rows),
        ),
        out_shape=jax.ShapeDtypeStruct((rows, 3 * cols), bf16),
        compiler_params=params(),
        cost_estimate=pl.CostEstimate(
            flops=6 * rows * width * cols,
            bytes_accessed=2 * (rows * width + 3 * width * cols + 3 * rows * cols),
            transcendentals=0,
        ),
    )(starts, x, own, *blocks, bias[None])


def put_body(place_ref, part_ref, *refs):
    refs[-1][...] = part_ref[...].astype(f32)

def put_half(part, place, axis, whole=None):
    rows, width = part.shape
    tile = min(256, rows)
    steps = rows // tile
    shape = (2 * rows, width) if axis == 0 else (rows, 2 * width)
    at = (lambda i, s: (s[0] * steps + i, 0)) if axis == 0 else (lambda i, s: (i, s[0]))
    in_specs = [pl.BlockSpec((tile, width), lambda i, s: (i, 0))]
    args = [place, part]
    alias = {}
    if whole is not None:
        in_specs.append(pl.BlockSpec(memory_space=pl.ANY))
        args.append(whole)
        alias = {2: 0}
    return pl.pallas_call(
        put_body, grid_spec=pltpu.PrefetchScalarGridSpec(num_scalar_prefetch=1, grid=(steps,), in_specs=in_specs, out_specs=pl.BlockSpec((tile, width), at)),
        out_shape=jax.ShapeDtypeStruct(shape, f32), input_output_aliases=alias, compiler_params=params(),
        cost_estimate=pl.CostEstimate(flops=0, bytes_accessed=6 * rows * width, transcendentals=0),
    )(*args)


def put_blocks_body(block_ref, *out_refs):
    cols = out_refs[0].shape[1]
    for w, out_ref in enumerate(out_refs):
        out_ref[...] = block_ref[0, :, w * cols : (w + 1) * cols].astype(f32)


def put_blocks(stack):
    count, rows, width = stack.shape
    cols = width // 4
    return pl.pallas_call(
        put_blocks_body,
        grid=(count, 2),
        in_specs=[pl.BlockSpec((1, rows // 2, width), lambda i, h: (i, h, 0))],
        out_specs=[pl.BlockSpec((rows // 2, cols), lambda i, h: (h, i))] * 4,
        out_shape=[jax.ShapeDtypeStruct((rows, count * cols), f32)] * 4,
        compiler_params=params(),
        cost_estimate=pl.CostEstimate(
            flops=0, bytes_accessed=6 * count * rows * width, transcendentals=0
        ),
    )(stack)


def matmul(left, right):
    return jnp.dot(left, right, preferred_element_type=f32)


def column_sums(matrix):
    return jnp.sum(matrix.astype(f32), 0)


def swap(block, step):
    count = lax.axis_size("group")
    return lax.ppermute(block, "group", [(i, i ^ step) for i in range(count)])


def exchange(blocks):
    return [blocks[0]] + [swap(blocks[step], step) for step in range(1, len(blocks))]


def gather_blocks(block):
    return exchange([block] * lax.axis_size("group"))


def gather_halves(block):
    count, width = lax.axis_size("group"), block.shape[1] // 2
    bits = [1 << b for b in range(count.bit_length() - 1)]
    held = []
    for side, path in enumerate((bits, bits[::-1])):
        held.append((block[:, side * width : (side + 1) * width], [0], path))
    for turn in range(len(bits)):
        moved = []
        for value, members, path in held:
            bit = path[turn]
            arrived = swap(value, bit)
            moved.append((jnp.concatenate([value, arrived]), members + [m ^ bit for m in members], path))
        held = moved
    rows, sides = block.shape[0], []
    for value, members, _ in held:
        at = {m: value[i * rows : (i + 1) * rows] for i, m in enumerate(members)}
        sides.append([at[k] for k in range(count)])
    return sides


def in_order(blocks):
    me = lax.axis_index("group")
    rows = blocks[0].shape[0]
    whole = jnp.zeros((len(blocks) * rows,) + blocks[0].shape[1:], blocks[0].dtype)
    for step, block in enumerate(blocks):
        start = ((me ^ step) * rows,) + (0,) * (block.ndim - 1)
        whole = lax.dynamic_update_slice(whole, block, start)
    return whole


def scatter_terms(partial):
    count = lax.axis_size("group")
    me = lax.axis_index("group")
    rows = partial.shape[0] // count
    terms = [lax.dynamic_slice_in_dim(partial, me * rows, rows, 0)]
    for step in range(1, count):
        sent = lax.dynamic_slice_in_dim(partial, (me ^ step) * rows, rows, 0)
        terms.append(swap(sent.astype(bf16), step))
    return terms


def add_terms(terms):
    return sum(term.astype(f32) for term in terms)


def scatter_sum(partial):
    return add_terms(scatter_terms(partial))


def gather_rows(block):
    return lax.all_gather(block, "group", axis=0, tiled=True)


def scatter_rows(partial):
    return lax.psum_scatter(
        partial.astype(bf16), "group", scatter_dimension=0, tiled=True
    ).astype(f32)


def reorder(stack):
    me = lax.axis_index("group")
    count = stack.shape[0]
    bit = 1
    while bit < count:
        pairs = stack.reshape((count // (2 * bit), 2, bit) + stack.shape[1:])
        pairs = jnp.where((me & bit) != 0, pairs[:, ::-1], pairs)
        stack = pairs.reshape(stack.shape)
        bit *= 2
    return stack


def after(value, *others):
    return lax.optimization_barrier((value,) + others)[0]


def core_swap(block):
    count = lax.axis_size("replica")
    return lax.ppermute(block, "replica", [(i, i ^ 1) for i in range(count)])


def core_join(mine, axis):
    core = lax.axis_index("replica") % 2
    other = core_swap(mine)
    first = jnp.where(core == 0, mine, other)
    second = jnp.where(core == 0, other, mine)
    return jnp.concatenate([first, second], axis)


class Order:
    def __init__(self):
        self.last = ()

    def __call__(self, *values):
        values = lax.optimization_barrier(values + self.last)[: len(values)]
        return values[0] if len(values) == 1 else values

    def mark(self, *values):
        self.last = values


def replica_swap(values, step):
    count = lax.axis_size("replica")
    return lax.ppermute(values, "replica", [(i, i ^ step) for i in range(count)])


def shards(
    tokens,
    lengths,
    exit_layers,
    pre_gain,
    pre_shift,
    query_weight,
    query_bias,
    key_weight,
    value_weight,
    value_bias,
    out_weight,
    out_bias,
    mid_gain,
    mid_shift,
    up_weight,
    up_bias,
    down_weight,
    down_bias,
    cotangent,
):
    rows, width = tokens.shape
    count = lax.axis_size("group")
    me = lax.axis_index("group")
    cols = width // count
    local = me * rows + jnp.arange(rows, dtype=jnp.int32)
    active = ((local < lengths[0]) & (exit_layers > LAYER)).astype(f32)[:, None]
    core = lax.axis_index("replica") % 2
    other = core_swap(mine)
    first = jnp.where(core == 0, mine, other)
    second = jnp.where(core == 0, other, mine)
    return jnp.concatenate([first, second], axis)


class Order:
    def __init__(self):
        self.last = ()

    def __call__(self, *values):
        values = lax.optimization_barrier(values + self.last)[: len(values)]
        return values[0] if len(values) == 1 else values

    def mark(self, *values):
        self.last = values


def replica_sum_small(values):
    count = lax.axis_size("replica")
    step = 1
    while step < count:
        values = values + lax.ppermute(values, "replica", [(i, i ^ step) for i in range(count)])
        step *= 2
    return values


def shards(
    tokens,
    lengths,
    exit_layers,
    pre_gain,
    pre_shift,
    query_weight,
    query_bias,
    key_weight,
    value_weight,
    value_bias,
    out_weight,
    out_bias,
    mid_gain,
    mid_shift,
    up_weight,
    up_bias,
    down_weight,
    down_bias,
    cotangent,
):
    rows, width = tokens.shape
    count = lax.axis_size("group")
    me = lax.axis_index("group")
    cols = width // count
    local = me * rows + jnp.arange(rows, dtype=jnp.int32)
    active = ((local < lengths[0]) & (exit_layers > LAYER)).astype(f32)[:, None]
    position = jnp.arange(count * rows, dtype=jnp.int32)
    allowed = position[None, :] <= position[:, None]
    core = lax.axis_index("replica") % 2
    half = cols // 2

    grad_out = cotangent.astype(f32)
    branch_grad = (active * grad_out).astype(bf16)
    vectors = jnp.concatenate([pre_gain, pre_shift, out_bias, mid_gain, mid_shift, down_bias])
    extra = -(-vectors.size // width)
    vectors = jnp.pad(vectors, (0, extra * width - vectors.size)).reshape(extra, width)
    sent = after(jnp.concatenate([tokens, vectors]), branch_grad)
    got = gather_blocks(sent)
    tokens_all = in_order([block[:rows] for block in got])
    vectors = in_order([block[rows:].reshape(1, -1)[:, : 6 * cols] for block in got])
    vectors = vectors.reshape(count, 6, cols).transpose(1, 0, 2).reshape(6, width).astype(f32)
    gain_one, shift_one, obias, gain_two, shift_two, dbias = (vectors[i] for i in range(6))

    def column_block(step, start, length):
        at = (start, (me ^ step) * cols)
        parts = [
            lax.dynamic_slice(w, at, (length, cols)) for w in (query_weight, key_weight, value_weight)
        ]
        return jnp.concatenate(parts, 1)

    normed_all, _ = layer_norm(tokens_all.astype(f32))
    attn_in = (normed_all * gain_one + shift_one).astype(bf16)
    own = column_block(0, 0, cols)
    blocks = exchange([own] + [column_block(step, core * half, half) for step in range(1, count)])
    arrived = [after(block, attn_in, own) for block in blocks[1:]]
    others = [core_swap(block) for block in arrived]
    starts = [(me ^ k) * cols + core * half for k in range(1, count)]
    starts += [(me ^ k) * cols + (1 - core) * half for k in range(1, count)]
    starts = jnp.stack([me * cols] + starts).astype(jnp.int32)
    everyone = ("replica", "group")
    branch_wide = lax.all_gather(branch_grad, everyone, axis=0, tiled=True)
    seq = count * rows
    branch_all = lax.dynamic_slice_in_dim(branch_wide, lax.axis_index("replica") * seq, seq, 0)

    qkv_bias = jnp.concatenate([query_bias, jnp.zeros_like(query_bias), value_bias])
    qkv = qkv_product(attn_in, own, arrived + others, starts, qkv_bias)
    context = attention(qkv)
    attn_out = scatter_sum(matmul(context, out_weight)) + obias
    hidden = tokens.astype(f32) + active * attn_out
    normed_two, factor_two = layer_norm(hidden)
    ffn_in = (normed_two * gain_two + shift_two).astype(bf16)
    act_grad = nt(branch_all, down_weight).astype(bf16)
    ffn_blocks = gather_blocks(ffn_in)
    ffn_blocks = ffn_blocks[:1] + [after(block, act_grad) for block in ffn_blocks[1:]]
    ffn_wide = lax.all_gather(ffn_in, everyone, axis=0, tiled=True)
    here = jnp.full((1,), core, jnp.int32)
    ff = up_weight.shape[1]
    members = (me ^ jnp.arange(count, dtype=jnp.int32)).astype(jnp.int32)
    act_low, pre_grad, _ = gelu_product_blocks(
        ffn_blocks, members, up_weight, up_bias, act_grad, 256
    )
    order = Order()
    order.mark(act_low, pre_grad)
    split = ff // 2
    down_half = lax.dynamic_slice(down_weight, (core * split, 0), (split, width))

    partial = nt(pre_grad, up_weight).astype(bf16)
    order.mark(partial)
    ffn_in_grad = scatter_terms(partial)
    wide_grad = nt(order(branch_wide), down_half).astype(bf16)
    order.mark(wide_grad)

    ffn_in_grad = add_terms(order(*ffn_in_grad))
    hidden_grad = grad_out + norm_back(ffn_in_grad * gain_two, normed_two, factor_two)
    attn_grad = (active * hidden_grad).astype(bf16)
    order.mark(attn_grad)
    attn_sides = gather_halves(attn_grad)
    branch = matmul(order(act_low), down_weight)
    order.mark(branch)
    branch_sums = column_sums(order(branch_wide))
    order.mark(branch_sums)

    attn_sides = order(*(attn_sides[0] + attn_sides[1]))
    attn_all = in_order([jnp.concatenate(pair, 1) for pair in zip(attn_sides[:count], attn_sides[count:])])
    context_grad = nt(attn_all, out_weight).astype(bf16)
    qkv_grads = attention_back(qkv, context_grad)

    parts = weight_parts(attn_in, *qkv_grads, context, attn_all)
    qkv_grad = jnp.concatenate(qkv_grads, 1)
    piece = lax.psum_scatter(parts, "replica", scatter_dimension=1, tiled=True)
    qkv_weight = jnp.zeros((width, 3 * cols), bf16)
    for start, block in zip([me * cols] + [starts[1 + k] for k in range(2 * count - 2)], [own] + arrived + others):
        block = after(block, hidden)
        qkv_weight = lax.dynamic_update_slice(qkv_weight, block, (start, 0))
    in_part = nt(after(qkv_grad, parts), qkv_weight)
    order.mark(in_part)
    in_grad = scatter_terms(in_part)

    wide_act, wide_grad, wide_sums = gelu_product(
        order(ffn_wide), up_weight, up_bias, wide_grad, here, split, min(512, rows * count), split
    )
    order.mark(wide_act, wide_grad)

    shared = jnp.stack(
        [
            jnp.sum(in_part * normed_all, 0),
            jnp.sum(in_part, 0),
            jnp.sum(ffn_in_grad * normed_two, 0),
            jnp.sum(ffn_in_grad, 0),
        ]
    )
    qkv_bias_part = column_sums(qkv_grad)
    shared = reorder(shared.reshape(4, count, cols).transpose(1, 0, 2))
    shared, qkv_bias_part = order(shared, qkv_bias_part)
    shared = exchange([shared[k] for k in range(count)])

    def join_shared():
        values = jnp.concatenate(
            [
                sum(order(*shared)).reshape(-1),
                lax.dynamic_slice(column_sums(attn_all), (me * cols,), (cols,)),
                qkv_bias_part[:cols],
                qkv_bias_part[2 * cols :],
            ]
        )
        order.mark(values)
        return values, replica_swap(values, 1)

    def small_step(step):
        def run(pair):
            values, arrived = pair
            values = values + order(arrived)
            order.mark(values)
            return values if 2 * step >= replicas else (values, replica_swap(values, 2 * step))

        return run

    replicas = lax.axis_size("replica")
    small_steps, step = [lambda _: join_shared()], 1
    while step < replicas:
        small_steps.append(small_step(step))
        step *= 2

    normed_one, factor_one = layer_norm(tokens.astype(f32))
    in_grad = add_terms(order(*in_grad))
    token_grad = (hidden_grad + norm_back(in_grad * gain_one, normed_one, factor_one)).astype(bf16)
    order.mark(token_grad)

    down_grad = tn(order(wide_act), branch_wide).astype(bf16)
    order.mark(down_grad)
    small = small_steps[0](None)
    piece = order(piece)
    size = (1,) + piece.shape[1:2] + (3 * cols,)
    sent = [lax.dynamic_slice(piece, (me ^ step, 0, 0), size) for step in range(1, count)]
    sent = lax.optimization_barrier(tuple(sent))
    owned = lax.optimization_barrier(tuple(swap(s, k + 1) for k, s in enumerate(sent)))
    for step in range(1, count):
        piece = lax.dynamic_update_slice(piece, owned[step - 1], (me ^ step, 0, 0))
    order.mark(piece)
    attn_wgrad = lax.all_gather(piece, "replica", axis=1, tiled=True)
    small = small_steps[1](small)
    up_grad = tn(order(ffn_wide), wide_grad).astype(bf16)
    order.mark(up_grad)
    branch = scatter_terms(order(branch))
    down_other, up_other = core_swap(down_grad), core_swap(up_grad)
    down_grad = put_half(order(down_grad), here, 0)
    order.mark(down_grad)
    small = small_steps[2](small)
    up_grad = put_half(order(up_grad), here, 1)
    order.mark(up_grad)
    for run in small_steps[3:]:
        small = run(small)
    down_grad = put_half(order(down_other), 1 - here, 0, down_grad)
    up_grad = put_half(up_other, 1 - here, 1, up_grad)
    order.mark(down_grad, up_grad)
    output = (hidden + active * (add_terms(order(*branch)) + dbias)).astype(bf16)
    order.mark(output)
    up_bias_grad = core_join(wide_sums.reshape(-1), 0)
    down_bias_grad = lax.dynamic_slice(branch_sums, (me * cols,), (cols,))

    query_wgrad, key_wgrad, value_wgrad, out_wgrad = put_blocks(order(attn_wgrad))
    small_parts = [small[k * cols : (k + 1) * cols] for k in range(7)]
    return (
        output,
        token_grad,
        small_parts[0],
        small_parts[1],
        query_wgrad,
        small_parts[5],
        key_wgrad,
        value_wgrad,
        small_parts[6],
        out_wgrad,
        small_parts[4],
        small_parts[2],
        small_parts[3],
        up_grad,
        up_bias_grad,
        down_grad,
        down_bias_grad,
    )


def solution(mesh):
    both = P(("replica", "group"), None)
    vector, by_rows, by_cols = P("group"), P("group", None), P(None, "group")
    return jax.shard_map(
        shards,
        mesh=mesh,
        in_specs=(
            both,
            P("replica"),
            P(("replica", "group")),
            vector,
            vector,
            by_rows,
            vector,
            by_rows,
            by_rows,
            vector,
            by_rows,
            vector,
            vector,
            vector,
            by_cols,
            vector,
            by_rows,
            vector,
            both,
        ),
        out_specs=(
            both,
            both,
            vector,
            vector,
            by_rows,
            vector,
            by_rows,
            by_rows,
            vector,
            by_rows,
            vector,
            vector,
            vector,
            by_cols,
            vector,
            by_rows,
            vector,
        ),
        check_vma=False,
    )
```

```python
import functools

import jax
import jax.numpy as jnp
from jax import lax
from jax.experimental import pallas as pl
from jax.experimental.pallas import tpu as pltpu
from jax.sharding import PartitionSpec as P

HD = 64
LAYER = 12
QB = 128

bf16 = jnp.bfloat16
f32 = jnp.float32


def layer_norm(values):
    center = values - jnp.mean(values, -1, keepdims=True)
    spread = jnp.mean(center * center, -1, keepdims=True)
    factor = lax.rsqrt(spread + 1e-05)
    return (center * factor, factor)


def norm_back(grad, normal, factor):
    return factor * (
        grad
        - jnp.mean(grad, -1, keepdims=True)
        - normal * jnp.mean(grad * normal, -1, keepdims=True)
    )


def params(mb=56):
    return pltpu.CompilerParams(vmem_limit_bytes=mb << 20)

def nt(left, right):
    return lax.dot_general(left, right, (((1,), (1,)), ((), ())), preferred_element_type=f32)
def tn(left, right):
    return lax.dot_general(left, right, (((0,), (0,)), ((), ())), preferred_element_type=f32)

def later(keys, first):
    key = lax.broadcasted_iota(jnp.int32, (keys, QB), 0)
    query = lax.broadcasted_iota(jnp.int32, (keys, QB), 1) + first
    return key <= query

def attend_body(q_ref, k_ref, v_ref, out_ref):
    rows = q_ref.shape[0]
    for first in range(0, rows, QB):
        keys = first + QB
        parts = []
        for lane in range(0, q_ref.shape[1], HD):
            at = slice(lane, lane + HD)
            query = q_ref[first:keys, at] * 0.125
            scores = jnp.where(later(keys, first), nt(k_ref[:keys, at], query), -1e30)
            grown = jnp.exp(scores - jnp.max(scores, 0, keepdims=True))
            probs = grown * (1.0 / jnp.sum(grown, 0, keepdims=True))
            parts.append(tn(probs.astype(bf16), v_ref[:keys, at]))
        out_ref[first:keys, :] = jnp.concatenate(parts, 1).astype(bf16)

def attend_back_body(q_ref, k_ref, v_ref, g_ref, dq_ref, dk_ref, dv_ref, key_acc, value_acc):
    rows = q_ref.shape[0]
    key_acc[...] = jnp.zeros_like(key_acc)
    value_acc[...] = jnp.zeros_like(value_acc)
    for first in range(0, rows, QB):
        keys = first + QB
        q_parts, k_parts, v_parts = [], [], []
        for lane in range(0, q_ref.shape[1], HD):
            at = slice(lane, lane + HD)
            query = q_ref[first:keys, at] * 0.125
            grad = g_ref[first:keys, at]
            key = k_ref[:keys, at]
            scores = jnp.where(later(keys, first), nt(key, query), -1e30)
            grown = jnp.exp(scores - jnp.max(scores, 0, keepdims=True))
            probs = grown * (1.0 / jnp.sum(grown, 0, keepdims=True))
            probs_grad = nt(v_ref[:keys, at], grad)
            delta = jnp.sum(probs * probs_grad, 0, keepdims=True)
            score_grad = (probs * (probs_grad - delta)).astype(bf16)
            v_parts.append(jnp.dot(probs.astype(bf16), grad, preferred_element_type=f32))
            k_parts.append(jnp.dot(score_grad, query, preferred_element_type=f32))
            q_parts.append(tn(score_grad, key) * 0.125)
        dq_ref[first:keys, :] = jnp.concatenate(q_parts, 1).astype(bf16)
        key_acc[:keys, :] += jnp.concatenate(k_parts, 1)
        value_acc[:keys, :] += jnp.concatenate(v_parts, 1)
    dk_ref[...] = key_acc[...].astype(bf16)
    dv_ref[...] = value_acc[...].astype(bf16)

def attention(qkv):
    rows, cols = qkv.shape[0], qkv.shape[1] // 3
    lanes = 2 * HD
    pairs = cols // lanes
    spec = lambda part: pl.BlockSpec((rows, lanes), lambda h: (0, part * pairs + h))
    work = 2 * rows * rows * cols
    return pl.pallas_call(
        attend_body, grid=(pairs,), in_specs=[spec(0), spec(1), spec(2)], out_specs=spec(0),
        out_shape=jax.ShapeDtypeStruct((rows, cols), bf16), compiler_params=params(12),
        cost_estimate=pl.CostEstimate(flops=2 * work, bytes_accessed=8 * rows * cols, transcendentals=rows * rows * cols // HD),
    )(qkv, qkv, qkv)

def attention_back(qkv, grad):
    rows, cols = grad.shape
    lanes = 2 * HD
    pairs = cols // lanes
    spec = lambda part: pl.BlockSpec((rows, lanes), lambda h: (0, part * pairs + h))
    work = 2 * rows * rows * cols
    one = jax.ShapeDtypeStruct((rows, cols), bf16)
    return pl.pallas_call(
        attend_back_body, grid=(pairs,), in_specs=[spec(0), spec(1), spec(2), spec(0)], out_specs=[spec(0)] * 3,
        out_shape=[one] * 3, scratch_shapes=[pltpu.VMEM((rows, lanes), f32)] * 2, compiler_params=params(12),
        cost_estimate=pl.CostEstimate(flops=5 * work, bytes_accessed=14 * rows * cols, transcendentals=rows * rows * cols // HD),
    )(qkv, qkv, qkv, grad)

def gelu_tiles(tile, first, x_ref, w_ref, b_ref, g_ref, act_ref, grad_ref, sum_ref):
    for start in range(0, w_ref.shape[1], tile):
        at = slice(start, start + tile)
        value = jnp.dot(x_ref[...], w_ref[:, at], preferred_element_type=f32) + b_ref[:, at].astype(f32)
        square = value * value
        tangent = jnp.tanh(value * (0.7978845608 + (0.7978845608 * 0.044715) * square))
        share = 0.5 * value
        act_ref[:, at] = (share + share * tangent).astype(bf16)
        bend = share * (0.7978845608 + (3.0 * 0.7978845608 * 0.044715) * square)
        slope = (0.5 + 0.5 * tangent) + bend * (1.0 - tangent * tangent)
        grad = g_ref[:, at].astype(f32) * slope
        grad_ref[:, at] = grad.astype(bf16)
        total = jnp.sum(grad, 0, keepdims=True)
        if first is not True:
            total = jnp.where(first, total, sum_ref[:, at] + total)
        sum_ref[:, at] = total


def gelu_body(tile, place_ref, *refs):
    gelu_tiles(tile, pl.program_id(1) == 0, *refs)


def gelu_product(x, weight, bias, grad, place, width, row_tile, col_tile):
    rows, depth = x.shape
    steps = width // col_tile
    grid = pltpu.PrefetchScalarGridSpec(
        num_scalar_prefetch=1, grid=(steps, rows // row_tile),
        in_specs=[
            pl.BlockSpec((row_tile, depth), lambda j, i, s: (i, 0)),
            pl.BlockSpec((depth, col_tile), lambda j, i, s: (0, s[0] * steps + j)),
            pl.BlockSpec((1, col_tile), lambda j, i, s: (0, s[0] * steps + j)),
            pl.BlockSpec((row_tile, col_tile), lambda j, i, s: (i, j)),
        ],
        out_specs=[
            pl.BlockSpec((row_tile, col_tile), lambda j, i, s: (i, j)),
            pl.BlockSpec((row_tile, col_tile), lambda j, i, s: (i, j)),
            pl.BlockSpec((1, col_tile), lambda j, i, s: (0, j)),
        ])
    return pl.pallas_call(
        functools.partial(gelu_body, min(256, col_tile)), grid_spec=grid,
        out_shape=[jax.ShapeDtypeStruct((rows, width), bf16)] * 2 + [jax.ShapeDtypeStruct((1, width), f32)],
        compiler_params=params(30),
        cost_estimate=pl.CostEstimate(flops=2 * rows * depth * width, bytes_accessed=2 * (rows * depth + depth * width + 3 * rows * width), transcendentals=rows * width),
    )(place, x, weight, bias[None], grad)

def parts_body(x_ref, q_ref, k_ref, v_ref, context_ref, grad_ref, out_ref):
    cols = q_ref.shape[1]
    for w, ref in enumerate((q_ref, k_ref, v_ref)):
        out_ref[0, :, w * cols : (w + 1) * cols] = tn(x_ref[...], ref[...]).astype(bf16)
    out_ref[0, :, 3 * cols :] = tn(context_ref[...], grad_ref[...]).astype(bf16)


def weight_parts(x, query_grad, key_grad, value_grad, context, grad):
    rows, cols = context.shape
    count = x.shape[1] // cols
    whole = pl.BlockSpec((rows, cols), lambda i: (0, 0))
    block = pl.BlockSpec((rows, cols), lambda i: (0, i))
    return pl.pallas_call(
        parts_body,
        grid=(count,),
        in_specs=[block, whole, whole, whole, whole, block],
        out_specs=pl.BlockSpec((1, cols, 4 * cols), lambda i: (i, 0, 0)),
        out_shape=jax.ShapeDtypeStruct((count, cols, 4 * cols), bf16),
        compiler_params=params(18),
        cost_estimate=pl.CostEstimate(
            flops=8 * count * rows * cols * cols,
            bytes_accessed=2 * (2 * rows * count * cols + 4 * rows * cols + 4 * count * cols * cols),
            transcendentals=0,
        ),
    )(x, query_grad, key_grad, value_grad, context, grad)


def gelu_blocks_body(tile, member_ref, *refs):
    count = len(refs) - 7
    blocks, (w_ref, b_ref, g_ref, act_ref, grad_ref, sum_ref, x_ref) = refs[:count], refs[count:]
    rows = blocks[0].shape[0]

    @pl.when(pl.program_id(0) == 0)
    def _():
        for k, block in enumerate(blocks):
            start = pl.multiple_of(member_ref[k] * rows, rows)
            x_ref[pl.ds(start, rows), :] = block[...]

    gelu_tiles(tile, True, x_ref, w_ref, b_ref, g_ref, act_ref, grad_ref, sum_ref)


def gelu_product_blocks(blocks, members, weight, bias, grad, col_tile):
    (rows, depth), count, width = blocks[0].shape, len(blocks), weight.shape[1]
    tall = count * rows
    grid = pltpu.PrefetchScalarGridSpec(
        num_scalar_prefetch=1,
        grid=(width // col_tile,),
        in_specs=[pl.BlockSpec((rows, depth), lambda j, s: (0, 0))] * count
        + [
            pl.BlockSpec((depth, col_tile), lambda j, s: (0, j)),
            pl.BlockSpec((1, col_tile), lambda j, s: (0, j)),
            pl.BlockSpec((tall, col_tile), lambda j, s: (0, j)),
        ],
        out_specs=[
            pl.BlockSpec((tall, col_tile), lambda j, s: (0, j)),
            pl.BlockSpec((tall, col_tile), lambda j, s: (0, j)),
            pl.BlockSpec((1, col_tile), lambda j, s: (0, j)),
        ],
        scratch_shapes=[pltpu.VMEM((tall, depth), bf16)],
    )
    return pl.pallas_call(
        functools.partial(gelu_blocks_body, col_tile),
        grid_spec=grid,
        out_shape=[jax.ShapeDtypeStruct((tall, width), bf16)] * 2
        + [jax.ShapeDtypeStruct((1, width), f32)],
        compiler_params=params(24),
        cost_estimate=pl.CostEstimate(
            flops=2 * tall * depth * width,
            bytes_accessed=2 * (tall * depth + depth * width + 3 * tall * width),
            transcendentals=tall * width,
        ),
    )(members, *blocks, weight, bias[None], grad)


def qkv_body(count, at_ref, x_ref, own_ref, *refs):
    blocks, b_ref, out_ref = refs[:-2], refs[-2], refs[-1]
    cols = own_ref.shape[0]
    half = cols // 2
    at = pl.multiple_of(at_ref[0], cols)
    total = jnp.dot(x_ref[:, pl.ds(at, cols)], own_ref[...], preferred_element_type=f32)
    for k, block in enumerate(blocks):
        at = pl.multiple_of(at_ref[1 + k], half)
        total += jnp.dot(x_ref[:, pl.ds(at, half)], block[...], preferred_element_type=f32)
    out_ref[...] = (total + b_ref[...].astype(f32)).astype(bf16)


def qkv_product(x, own, blocks, starts, bias):
    rows, width = x.shape
    cols = own.shape[0]
    half = cols // 2
    column = lambda size: pl.BlockSpec((size, cols), lambda j, s: (0, j))
    return pl.pallas_call(
        functools.partial(qkv_body, len(blocks)),
        grid_spec=pltpu.PrefetchScalarGridSpec(
            num_scalar_prefetch=1,
            grid=(3,),
            in_specs=[pl.BlockSpec((rows, width), lambda j, s: (0, 0)), column(cols)]
            + [column(half)] * len(blocks)
            + [column(1)],
            out_specs=column(rows),
        ),
        out_shape=jax.ShapeDtypeStruct((rows, 3 * cols), bf16),
        compiler_params=params(20),
        cost_estimate=pl.CostEstimate(
            flops=6 * rows * width * cols,
            bytes_accessed=2 * (rows * width + 3 * width * cols + 3 * rows * cols),
            transcendentals=0,
        ),
    )(starts, x, own, *blocks, bias[None])


def put_body(place_ref, part_ref, *refs):
    refs[-1][...] = part_ref[...].astype(f32)

def put_half(part, place, axis, whole=None):
    rows, width = part.shape
    tile = min(256, rows)
    steps = rows // tile
    shape = (2 * rows, width) if axis == 0 else (rows, 2 * width)
    at = (lambda i, s: (s[0] * steps + i, 0)) if axis == 0 else (lambda i, s: (i, s[0]))
    in_specs = [pl.BlockSpec((tile, width), lambda i, s: (i, 0))]
    args = [place, part]
    alias = {}
    if whole is not None:
        in_specs.append(pl.BlockSpec(memory_space=pl.ANY))
        args.append(whole)
        alias = {2: 0}
    return pl.pallas_call(
        put_body, grid_spec=pltpu.PrefetchScalarGridSpec(num_scalar_prefetch=1, grid=(steps,), in_specs=in_specs, out_specs=pl.BlockSpec((tile, width), at)),
        out_shape=jax.ShapeDtypeStruct(shape, f32), input_output_aliases=alias, compiler_params=params(12),
        cost_estimate=pl.CostEstimate(flops=0, bytes_accessed=6 * rows * width, transcendentals=0),
    )(*args)


def put_blocks_body(block_ref, *out_refs):
    cols = out_refs[0].shape[1]
    for w, out_ref in enumerate(out_refs):
        out_ref[...] = block_ref[0, :, w * cols : (w + 1) * cols].astype(f32)


def put_blocks(stack):
    count, rows, width = stack.shape
    cols = width // 4
    return pl.pallas_call(
        put_blocks_body,
        grid=(count, 2),
        in_specs=[pl.BlockSpec((1, rows // 2, width), lambda i, h: (i, h, 0))],
        out_specs=[pl.BlockSpec((rows // 2, cols), lambda i, h: (h, i))] * 4,
        out_shape=[jax.ShapeDtypeStruct((rows, count * cols), f32)] * 4,
        compiler_params=params(12),
        cost_estimate=pl.CostEstimate(
            flops=0, bytes_accessed=6 * count * rows * width, transcendentals=0
        ),
    )(stack)


def matmul(left, right):
    return jnp.dot(left, right, preferred_element_type=f32)


def column_sums(matrix):
    return jnp.sum(matrix.astype(f32), 0)


def swap(block, step):
    count = lax.axis_size("group")
    return lax.ppermute(block, "group", [(i, i ^ step) for i in range(count)])


def exchange(blocks):
    return [blocks[0]] + [swap(blocks[step], step) for step in range(1, len(blocks))]


def gather_blocks(block):
    return exchange([block] * lax.axis_size("group"))


def gather_halves(block):
    count, width = lax.axis_size("group"), block.shape[1] // 2
    bits = [1 << b for b in range(count.bit_length() - 1)]
    held = []
    for side, path in enumerate((bits, bits[::-1])):
        held.append((block[:, side * width : (side + 1) * width], [0], path))
    for turn in range(len(bits)):
        moved = []
        for value, members, path in held:
            bit = path[turn]
            arrived = swap(value, bit)
            moved.append((jnp.concatenate([value, arrived]), members + [m ^ bit for m in members], path))
        held = moved
    rows, sides = block.shape[0], []
    for value, members, _ in held:
        at = {m: value[i * rows : (i + 1) * rows] for i, m in enumerate(members)}
        sides.append([at[k] for k in range(count)])
    return sides


def in_order(blocks):
    me = lax.axis_index("group")
    rows = blocks[0].shape[0]
    whole = jnp.zeros((len(blocks) * rows,) + blocks[0].shape[1:], blocks[0].dtype)
    for step, block in enumerate(blocks):
        start = ((me ^ step) * rows,) + (0,) * (block.ndim - 1)
        whole = lax.dynamic_update_slice(whole, block, start)
    return whole


def scatter_terms(partial):
    count = lax.axis_size("group")
    me = lax.axis_index("group")
    rows = partial.shape[0] // count
    terms = [lax.dynamic_slice_in_dim(partial, me * rows, rows, 0)]
    for step in range(1, count):
        sent = lax.dynamic_slice_in_dim(partial, (me ^ step) * rows, rows, 0)
        terms.append(swap(sent.astype(bf16), step))
    return terms


def add_terms(terms):
    return sum(term.astype(f32) for term in terms)


def scatter_sum(partial):
    return add_terms(scatter_terms(partial))


def gather_rows(block):
    return lax.all_gather(block, "group", axis=0, tiled=True)


def scatter_rows(partial):
    return lax.psum_scatter(
        partial.astype(bf16), "group", scatter_dimension=0, tiled=True
    ).astype(f32)


def reorder(stack):
    me = lax.axis_index("group")
    count = stack.shape[0]
    bit = 1
    while bit < count:
        pairs = stack.reshape((count // (2 * bit), 2, bit) + stack.shape[1:])
        pairs = jnp.where((me & bit) != 0, pairs[:, ::-1], pairs)
        stack = pairs.reshape(stack.shape)
        bit *= 2
    return stack


def after(value, *others):
    return lax.optimization_barrier((value,) + others)[0]


def core_swap(block):
    count = lax.axis_size("replica")
    return lax.ppermute(block, "replica", [(i, i ^ 1) for i in range(count)])


def core_join(mine, axis):
    core = lax.axis_index("replica") % 2
    other = core_swap(mine)
    first = jnp.where(core == 0, mine, other)
    second = jnp.where(core == 0, other, mine)
    return jnp.concatenate([first, second], axis)


class Order:
    def __init__(self):
        self.last = ()

    def __call__(self, *values):
        values = lax.optimization_barrier(values + self.last)[: len(values)]
        return values[0] if len(values) == 1 else values

    def mark(self, *values):
        self.last = values


def replica_swap(values, step):
    count = lax.axis_size("replica")
    return lax.ppermute(values, "replica", [(i, i ^ step) for i in range(count)])


def shards(
    tokens,
    lengths,
    exit_layers,
    pre_gain,
    pre_shift,
    query_weight,
    query_bias,
    key_weight,
    value_weight,
    value_bias,
    out_weight,
    out_bias,
    mid_gain,
    mid_shift,
    up_weight,
    up_bias,
    down_weight,
    down_bias,
    cotangent,
):
    rows, width = tokens.shape
    count = lax.axis_size("group")
    me = lax.axis_index("group")
    cols = width // count
    local = me * rows + jnp.arange(rows, dtype=jnp.int32)
    active = ((local < lengths[0]) & (exit_layers > LAYER)).astype(f32)[:, None]
    core = lax.axis_index("replica") % 2
    other = core_swap(mine)
    first = jnp.where(core == 0, mine, other)
    second = jnp.where(core == 0, other, mine)
    return jnp.concatenate([first, second], axis)


class Order:
    def __init__(self):
        self.last = ()

    def __call__(self, *values):
        values = lax.optimization_barrier(values + self.last)[: len(values)]
        return values[0] if len(values) == 1 else values

    def mark(self, *values):
        self.last = values


def replica_sum_small(values):
    count = lax.axis_size("replica")
    step = 1
    while step < count:
        values = values + lax.ppermute(values, "replica", [(i, i ^ step) for i in range(count)])
        step *= 2
    return values


def shards(
    tokens,
    lengths,
    exit_layers,
    pre_gain,
    pre_shift,
    query_weight,
    query_bias,
    key_weight,
    value_weight,
    value_bias,
    out_weight,
    out_bias,
    mid_gain,
    mid_shift,
    up_weight,
    up_bias,
    down_weight,
    down_bias,
    cotangent,
):
    rows, width = tokens.shape
    count = lax.axis_size("group")
    me = lax.axis_index("group")
    cols = width // count
    local = me * rows + jnp.arange(rows, dtype=jnp.int32)
    active = ((local < lengths[0]) & (exit_layers > LAYER)).astype(f32)[:, None]
    position = jnp.arange(count * rows, dtype=jnp.int32)
    allowed = position[None, :] <= position[:, None]
    core = lax.axis_index("replica") % 2
    half = cols // 2

    grad_out = cotangent.astype(f32)
    branch_grad = (active * grad_out).astype(bf16)
    vectors = jnp.concatenate([pre_gain, pre_shift, out_bias, mid_gain, mid_shift, down_bias])
    extra = -(-vectors.size // width)
    vectors = jnp.pad(vectors, (0, extra * width - vectors.size)).reshape(extra, width)
    sent = after(jnp.concatenate([tokens, vectors]), branch_grad)
    got = gather_blocks(sent)
    tokens_all = in_order([block[:rows] for block in got])
    vectors = in_order([block[rows:].reshape(1, -1)[:, : 6 * cols] for block in got])
    vectors = vectors.reshape(count, 6, cols).transpose(1, 0, 2).reshape(6, width).astype(f32)
    gain_one, shift_one, obias, gain_two, shift_two, dbias = (vectors[i] for i in range(6))

    def column_block(step, start, length):
        at = (start, (me ^ step) * cols)
        parts = [
            lax.dynamic_slice(w, at, (length, cols)) for w in (query_weight, key_weight, value_weight)
        ]
        return jnp.concatenate(parts, 1)

    normed_all, _ = layer_norm(tokens_all.astype(f32))
    attn_in = (normed_all * gain_one + shift_one).astype(bf16)
    own = column_block(0, 0, cols)
    blocks = exchange([own] + [column_block(step, core * half, half) for step in range(1, count)])
    arrived = [after(block, attn_in, own) for block in blocks[1:]]
    others = [core_swap(block) for block in arrived]
    starts = [(me ^ k) * cols + core * half for k in range(1, count)]
    starts += [(me ^ k) * cols + (1 - core) * half for k in range(1, count)]
    starts = jnp.stack([me * cols] + starts).astype(jnp.int32)
    everyone = ("replica", "group")
    branch_wide = lax.all_gather(branch_grad, everyone, axis=0, tiled=True)
    seq = count * rows
    branch_all = lax.dynamic_slice_in_dim(branch_wide, lax.axis_index("replica") * seq, seq, 0)

    qkv_bias = jnp.concatenate([query_bias, jnp.zeros_like(query_bias), value_bias])
    qkv = qkv_product(attn_in, own, arrived + others, starts, qkv_bias)
    context = attention(qkv)
    attn_out = scatter_sum(matmul(context, out_weight)) + obias
    hidden = tokens.astype(f32) + active * attn_out
    normed_two, factor_two = layer_norm(hidden)
    ffn_in = (normed_two * gain_two + shift_two).astype(bf16)
    act_grad = nt(branch_all, down_weight).astype(bf16)
    ffn_blocks = gather_blocks(ffn_in)
    ffn_blocks = ffn_blocks[:1] + [after(block, act_grad) for block in ffn_blocks[1:]]
    ffn_wide = lax.all_gather(ffn_in, everyone, axis=0, tiled=True)
    here = jnp.full((1,), core, jnp.int32)
    ff = up_weight.shape[1]
    members = (me ^ jnp.arange(count, dtype=jnp.int32)).astype(jnp.int32)
    act_low, pre_grad, _ = gelu_product_blocks(
        ffn_blocks, members, up_weight, up_bias, act_grad, 256
    )
    order = Order()
    order.mark(act_low, pre_grad)
    split = ff // 2
    down_half = lax.dynamic_slice(down_weight, (core * split, 0), (split, width))

    partial = nt(pre_grad, up_weight).astype(bf16)
    order.mark(partial)
    ffn_in_grad = scatter_terms(partial)
    wide_grad = nt(order(branch_wide), down_half).astype(bf16)
    order.mark(wide_grad)

    ffn_in_grad = add_terms(order(*ffn_in_grad))
    hidden_grad = grad_out + norm_back(ffn_in_grad * gain_two, normed_two, factor_two)
    attn_grad = (active * hidden_grad).astype(bf16)
    order.mark(attn_grad)
    attn_sides = gather_halves(attn_grad)
    branch = matmul(order(act_low), down_weight)
    order.mark(branch)
    branch_sums = column_sums(order(branch_wide))
    order.mark(branch_sums)

    attn_sides = order(*(attn_sides[0] + attn_sides[1]))
    attn_all = in_order([jnp.concatenate(pair, 1) for pair in zip(attn_sides[:count], attn_sides[count:])])
    context_grad = nt(attn_all, out_weight).astype(bf16)
    qkv_grads = attention_back(qkv, context_grad)

    parts = weight_parts(attn_in, *qkv_grads, context, attn_all)
    qkv_grad = jnp.concatenate(qkv_grads, 1)
    piece = lax.psum_scatter(parts, "replica", scatter_dimension=1, tiled=True)
    qkv_weight = jnp.zeros((width, 3 * cols), bf16)
    for start, block in zip([me * cols] + [starts[1 + k] for k in range(2 * count - 2)], [own] + arrived + others):
        block = after(block, hidden)
        qkv_weight = lax.dynamic_update_slice(qkv_weight, block, (start, 0))
    in_part = nt(after(qkv_grad, parts), qkv_weight)
    order.mark(in_part)
    in_grad = scatter_terms(in_part)

    wide_act, wide_grad, wide_sums = gelu_product(
        order(ffn_wide), up_weight, up_bias, wide_grad, here, split, min(512, rows * count), split
    )
    order.mark(wide_act, wide_grad)

    shared = jnp.stack(
        [
            jnp.sum(in_part * normed_all, 0),
            jnp.sum(in_part, 0),
            jnp.sum(ffn_in_grad * normed_two, 0),
            jnp.sum(ffn_in_grad, 0),
        ]
    )
    qkv_bias_part = column_sums(qkv_grad)
    shared = reorder(shared.reshape(4, count, cols).transpose(1, 0, 2))
    shared, qkv_bias_part = order(shared, qkv_bias_part)
    shared = exchange([shared[k] for k in range(count)])

    def join_shared():
        values = jnp.concatenate(
            [
                sum(order(*shared)).reshape(-1),
                lax.dynamic_slice(column_sums(attn_all), (me * cols,), (cols,)),
                qkv_bias_part[:cols],
                qkv_bias_part[2 * cols :],
            ]
        )
        order.mark(values)
        return values, replica_swap(values, 1)

    def small_step(step):
        def run(pair):
            values, arrived = pair
            values = values + order(arrived)
            order.mark(values)
            return values if 2 * step >= replicas else (values, replica_swap(values, 2 * step))

        return run

    replicas = lax.axis_size("replica")
    small_steps, step = [lambda _: join_shared()], 1
    while step < replicas:
        small_steps.append(small_step(step))
        step *= 2

    normed_one, factor_one = layer_norm(tokens.astype(f32))
    in_grad = add_terms(order(*in_grad))
    token_grad = (hidden_grad + norm_back(in_grad * gain_one, normed_one, factor_one)).astype(bf16)
    order.mark(token_grad)

    down_grad = tn(order(wide_act), branch_wide).astype(bf16)
    order.mark(down_grad)
    small = small_steps[0](None)
    piece = order(piece)
    size = (1,) + piece.shape[1:2] + (3 * cols,)
    sent = [lax.dynamic_slice(piece, (me ^ step, 0, 0), size) for step in range(1, count)]
    sent = lax.optimization_barrier(tuple(sent))
    owned = lax.optimization_barrier(tuple(swap(s, k + 1) for k, s in enumerate(sent)))
    for step in range(1, count):
        piece = lax.dynamic_update_slice(piece, owned[step - 1], (me ^ step, 0, 0))
    order.mark(piece)
    attn_wgrad = lax.all_gather(piece, "replica", axis=1, tiled=True)
    small = small_steps[1](small)
    up_grad = tn(order(ffn_wide), wide_grad).astype(bf16)
    order.mark(up_grad)
    branch = scatter_terms(order(branch))
    down_other, up_other = core_swap(down_grad), core_swap(up_grad)
    down_grad = put_half(order(down_grad), here, 0)
    order.mark(down_grad)
    small = small_steps[2](small)
    up_grad = put_half(order(up_grad), here, 1)
    order.mark(up_grad)
    for run in small_steps[3:]:
        small = run(small)
    down_grad = put_half(order(down_other), 1 - here, 0, down_grad)
    up_grad = put_half(up_other, 1 - here, 1, up_grad)
    order.mark(down_grad, up_grad)
    output = (hidden + active * (add_terms(order(*branch)) + dbias)).astype(bf16)
    order.mark(output)
    up_bias_grad = core_join(wide_sums.reshape(-1), 0)
    down_bias_grad = lax.dynamic_slice(branch_sums, (me * cols,), (cols,))

    query_wgrad, key_wgrad, value_wgrad, out_wgrad = put_blocks(order(attn_wgrad))
    small_parts = [small[k * cols : (k + 1) * cols] for k in range(7)]
    return (
        output,
        token_grad,
        small_parts[0],
        small_parts[1],
        query_wgrad,
        small_parts[5],
        key_wgrad,
        value_wgrad,
        small_parts[6],
        out_wgrad,
        small_parts[4],
        small_parts[2],
        small_parts[3],
        up_grad,
        up_bias_grad,
        down_grad,
        down_bias_grad,
    )


def solution(mesh):
    both = P(("replica", "group"), None)
    vector, by_rows, by_cols = P("group"), P("group", None), P(None, "group")
    return jax.shard_map(
        shards,
        mesh=mesh,
        in_specs=(
            both,
            P("replica"),
            P(("replica", "group")),
            vector,
            vector,
            by_rows,
            vector,
            by_rows,
            by_rows,
            vector,
            by_rows,
            vector,
            vector,
            vector,
            by_cols,
            vector,
            by_rows,
            vector,
            both,
        ),
        out_specs=(
            both,
            both,
            vector,
            vector,
            by_rows,
            vector,
            by_rows,
            by_rows,
            vector,
            by_rows,
            vector,
            vector,
            vector,
            by_cols,
            vector,
            by_rows,
            vector,
        ),
        check_vma=False,
    )
```

```python
import functools

import jax
import jax.numpy as jnp
from jax import lax
from jax.experimental import pallas as pl
from jax.experimental.pallas import tpu as pltpu
from jax.sharding import PartitionSpec as P

HD = 64
LAYER = 12
QB = 128

bf16 = jnp.bfloat16
f32 = jnp.float32


def layer_norm(values):
    center = values - jnp.mean(values, -1, keepdims=True)
    spread = jnp.mean(center * center, -1, keepdims=True)
    factor = lax.rsqrt(spread + 1e-05)
    return (center * factor, factor)


def norm_back(grad, normal, factor):
    return factor * (
        grad
        - jnp.mean(grad, -1, keepdims=True)
        - normal * jnp.mean(grad * normal, -1, keepdims=True)
    )


def params(mb=56):
    return pltpu.CompilerParams(vmem_limit_bytes=mb << 20)

def nt(left, right):
    return lax.dot_general(left, right, (((1,), (1,)), ((), ())), preferred_element_type=f32)
def tn(left, right):
    return lax.dot_general(left, right, (((0,), (0,)), ((), ())), preferred_element_type=f32)

def later(keys, first):
    key = lax.broadcasted_iota(jnp.int32, (keys, QB), 0)
    query = lax.broadcasted_iota(jnp.int32, (keys, QB), 1) + first
    return key <= query

def attend_body(q_ref, k_ref, v_ref, out_ref):
    rows = q_ref.shape[0]
    for first in range(0, rows, QB):
        keys = first + QB
        parts = []
        for lane in range(0, q_ref.shape[1], HD):
            at = slice(lane, lane + HD)
            query = q_ref[first:keys, at] * 0.125
            scores = jnp.where(later(keys, first), nt(k_ref[:keys, at], query), -1e30)
            grown = jnp.exp(scores - jnp.max(scores, 0, keepdims=True))
            probs = grown * (1.0 / jnp.sum(grown, 0, keepdims=True))
            parts.append(tn(probs.astype(bf16), v_ref[:keys, at]))
        out_ref[first:keys, :] = jnp.concatenate(parts, 1).astype(bf16)

def attend_back_body(q_ref, k_ref, v_ref, g_ref, dq_ref, dk_ref, dv_ref, key_acc, value_acc):
    rows = q_ref.shape[0]
    key_acc[...] = jnp.zeros_like(key_acc)
    value_acc[...] = jnp.zeros_like(value_acc)
    for first in range(0, rows, QB):
        keys = first + QB
        q_parts, k_parts, v_parts = [], [], []
        for lane in range(0, q_ref.shape[1], HD):
            at = slice(lane, lane + HD)
            query = q_ref[first:keys, at] * 0.125
            grad = g_ref[first:keys, at]
            key = k_ref[:keys, at]
            scores = jnp.where(later(keys, first), nt(key, query), -1e30)
            grown = jnp.exp(scores - jnp.max(scores, 0, keepdims=True))
            probs = grown * (1.0 / jnp.sum(grown, 0, keepdims=True))
            probs_grad = nt(v_ref[:keys, at], grad)
            delta = jnp.sum(probs * probs_grad, 0, keepdims=True)
            score_grad = (probs * (probs_grad - delta)).astype(bf16)
            v_parts.append(jnp.dot(probs.astype(bf16), grad, preferred_element_type=f32))
            k_parts.append(jnp.dot(score_grad, query, preferred_element_type=f32))
            q_parts.append(tn(score_grad, key) * 0.125)
        dq_ref[first:keys, :] = jnp.concatenate(q_parts, 1).astype(bf16)
        key_acc[:keys, :] += jnp.concatenate(k_parts, 1)
        value_acc[:keys, :] += jnp.concatenate(v_parts, 1)
    dk_ref[...] = key_acc[...].astype(bf16)
    dv_ref[...] = value_acc[...].astype(bf16)

def attention(qkv):
    rows, cols = qkv.shape[0], qkv.shape[1] // 3
    lanes = 2 * HD
    pairs = cols // lanes
    spec = lambda part: pl.BlockSpec((rows, lanes), lambda h: (0, part * pairs + h))
    work = 2 * rows * rows * cols
    return pl.pallas_call(
        attend_body, grid=(pairs,), in_specs=[spec(0), spec(1), spec(2)], out_specs=spec(0),
        out_shape=jax.ShapeDtypeStruct((rows, cols), bf16), compiler_params=params(12),
        cost_estimate=pl.CostEstimate(flops=2 * work, bytes_accessed=8 * rows * cols, transcendentals=rows * rows * cols // HD),
    )(qkv, qkv, qkv)

def attention_back(qkv, grad):
    rows, cols = grad.shape
    lanes = 2 * HD
    pairs = cols // lanes
    spec = lambda part: pl.BlockSpec((rows, lanes), lambda h: (0, part * pairs + h))
    work = 2 * rows * rows * cols
    one = jax.ShapeDtypeStruct((rows, cols), bf16)
    return pl.pallas_call(
        attend_back_body, grid=(pairs,), in_specs=[spec(0), spec(1), spec(2), spec(0)], out_specs=[spec(0)] * 3,
        out_shape=[one] * 3, scratch_shapes=[pltpu.VMEM((rows, lanes), f32)] * 2, compiler_params=params(12),
        cost_estimate=pl.CostEstimate(flops=5 * work, bytes_accessed=14 * rows * cols, transcendentals=rows * rows * cols // HD),
    )(qkv, qkv, qkv, grad)

def gelu_tiles(tile, first, x_ref, w_ref, b_ref, g_ref, act_ref, grad_ref, sum_ref):
    for start in range(0, w_ref.shape[1], tile):
        at = slice(start, start + tile)
        value = jnp.dot(x_ref[...], w_ref[:, at], preferred_element_type=f32) + b_ref[:, at].astype(f32)
        square = value * value
        tangent = jnp.tanh(value * (0.7978845608 + (0.7978845608 * 0.044715) * square))
        share = 0.5 * value
        act_ref[:, at] = (share + share * tangent).astype(bf16)
        bend = share * (0.7978845608 + (3.0 * 0.7978845608 * 0.044715) * square)
        slope = (0.5 + 0.5 * tangent) + bend * (1.0 - tangent * tangent)
        grad = g_ref[:, at].astype(f32) * slope
        grad_ref[:, at] = grad.astype(bf16)
        total = jnp.sum(grad, 0, keepdims=True)
        if first is not True:
            total = jnp.where(first, total, sum_ref[:, at] + total)
        sum_ref[:, at] = total


def gelu_body(tile, place_ref, *refs):
    gelu_tiles(tile, pl.program_id(1) == 0, *refs)


def gelu_product(x, weight, bias, grad, place, width, row_tile, col_tile):
    rows, depth = x.shape
    steps = width // col_tile
    grid = pltpu.PrefetchScalarGridSpec(
        num_scalar_prefetch=1, grid=(steps, rows // row_tile),
        in_specs=[
            pl.BlockSpec((row_tile, depth), lambda j, i, s: (i, 0)),
            pl.BlockSpec((depth, col_tile), lambda j, i, s: (0, s[0] * steps + j)),
            pl.BlockSpec((1, col_tile), lambda j, i, s: (0, s[0] * steps + j)),
            pl.BlockSpec((row_tile, col_tile), lambda j, i, s: (i, j)),
        ],
        out_specs=[
            pl.BlockSpec((row_tile, col_tile), lambda j, i, s: (i, j)),
            pl.BlockSpec((row_tile, col_tile), lambda j, i, s: (i, j)),
            pl.BlockSpec((1, col_tile), lambda j, i, s: (0, j)),
        ])
    return pl.pallas_call(
        functools.partial(gelu_body, min(256, col_tile)), grid_spec=grid,
        out_shape=[jax.ShapeDtypeStruct((rows, width), bf16)] * 2 + [jax.ShapeDtypeStruct((1, width), f32)],
        compiler_params=params(30),
        cost_estimate=pl.CostEstimate(flops=2 * rows * depth * width, bytes_accessed=2 * (rows * depth + depth * width + 3 * rows * width), transcendentals=rows * width),
    )(place, x, weight, bias[None], grad)

def parts_body(x_ref, q_ref, k_ref, v_ref, context_ref, grad_ref, out_ref):
    cols = q_ref.shape[1]
    for w, ref in enumerate((q_ref, k_ref, v_ref)):
        out_ref[0, :, w * cols : (w + 1) * cols] = tn(x_ref[...], ref[...]).astype(bf16)
    out_ref[0, :, 3 * cols :] = tn(context_ref[...], grad_ref[...]).astype(bf16)


def weight_parts(x, query_grad, key_grad, value_grad, context, grad):
    rows, cols = context.shape
    count = x.shape[1] // cols
    whole = pl.BlockSpec((rows, cols), lambda i: (0, 0))
    block = pl.BlockSpec((rows, cols), lambda i: (0, i))
    return pl.pallas_call(
        parts_body,
        grid=(count,),
        in_specs=[block, whole, whole, whole, whole, block],
        out_specs=pl.BlockSpec((1, cols, 4 * cols), lambda i: (i, 0, 0)),
        out_shape=jax.ShapeDtypeStruct((count, cols, 4 * cols), bf16),
        compiler_params=params(18),
        cost_estimate=pl.CostEstimate(
            flops=8 * count * rows * cols * cols,
            bytes_accessed=2 * (2 * rows * count * cols + 4 * rows * cols + 4 * count * cols * cols),
            transcendentals=0,
        ),
    )(x, query_grad, key_grad, value_grad, context, grad)


def gelu_halves_body(tile, steps, member_ref, *refs):
    pieces, (w_ref, b_ref, g_ref, act_ref, grad_ref, sum_ref, x_ref) = refs[:-7], refs[-7:]
    rows, width = pieces[0].shape

    @pl.when(pl.program_id(0) == 0)
    def _():
        at = 0
        for side in range(2):
            for group in steps[side]:
                for i, k in enumerate(group):
                    start = pl.multiple_of(member_ref[k] * rows, rows)
                    part = pieces[at][i * rows : (i + 1) * rows, :]
                    x_ref[pl.ds(start, rows), side * width : (side + 1) * width] = part
                at += 1

    gelu_tiles(tile, True, x_ref, w_ref, b_ref, g_ref, act_ref, grad_ref, sum_ref)


def gelu_product_halves(pieces, steps, members, weight, bias, grad, col_tile):
    parts = [piece for side in pieces for piece in side]
    tall, width = grad.shape
    depth = weight.shape[0]
    grid = pltpu.PrefetchScalarGridSpec(
        num_scalar_prefetch=1,
        grid=(width // col_tile,),
        in_specs=[pl.BlockSpec(part.shape, lambda j, s: (0, 0)) for part in parts]
        + [
            pl.BlockSpec((depth, col_tile), lambda j, s: (0, j)),
            pl.BlockSpec((1, col_tile), lambda j, s: (0, j)),
            pl.BlockSpec((tall, col_tile), lambda j, s: (0, j)),
        ],
        out_specs=[
            pl.BlockSpec((tall, col_tile), lambda j, s: (0, j)),
            pl.BlockSpec((tall, col_tile), lambda j, s: (0, j)),
            pl.BlockSpec((1, col_tile), lambda j, s: (0, j)),
        ],
        scratch_shapes=[pltpu.VMEM((tall, depth), bf16)],
    )
    return pl.pallas_call(
        functools.partial(gelu_halves_body, col_tile, steps),
        grid_spec=grid,
        out_shape=[jax.ShapeDtypeStruct((tall, width), bf16)] * 2
        + [jax.ShapeDtypeStruct((1, width), f32)],
        compiler_params=params(24),
        cost_estimate=pl.CostEstimate(
            flops=2 * tall * depth * width,
            bytes_accessed=2 * (tall * depth + depth * width + 3 * tall * width),
            transcendentals=tall * width,
        ),
    )(members, *parts, weight, bias[None], grad)


def qkv_body(count, at_ref, x_ref, own_ref, *refs):
    blocks, b_ref, out_ref = refs[:-2], refs[-2], refs[-1]
    cols = own_ref.shape[0]
    half = cols // 2
    at = pl.multiple_of(at_ref[0], cols)
    total = jnp.dot(x_ref[:, pl.ds(at, cols)], own_ref[...], preferred_element_type=f32)
    for k, block in enumerate(blocks):
        at = pl.multiple_of(at_ref[1 + k], half)
        total += jnp.dot(x_ref[:, pl.ds(at, half)], block[...], preferred_element_type=f32)
    out_ref[...] = (total + b_ref[...].astype(f32)).astype(bf16)


def qkv_product(x, own, blocks, starts, bias):
    rows, width = x.shape
    cols = own.shape[0]
    half = cols // 2
    column = lambda size: pl.BlockSpec((size, cols), lambda j, s: (0, j))
    return pl.pallas_call(
        functools.partial(qkv_body, len(blocks)),
        grid_spec=pltpu.PrefetchScalarGridSpec(
            num_scalar_prefetch=1,
            grid=(3,),
            in_specs=[pl.BlockSpec((rows, width), lambda j, s: (0, 0)), column(cols)]
            + [column(half)] * len(blocks)
            + [column(1)],
            out_specs=column(rows),
        ),
        out_shape=jax.ShapeDtypeStruct((rows, 3 * cols), bf16),
        compiler_params=params(20),
        cost_estimate=pl.CostEstimate(
            flops=6 * rows * width * cols,
            bytes_accessed=2 * (rows * width + 3 * width * cols + 3 * rows * cols),
            transcendentals=0,
        ),
    )(starts, x, own, *blocks, bias[None])


def put_body(place_ref, part_ref, *refs):
    refs[-1][...] = part_ref[...].astype(f32)

def put_half(part, place, axis, whole=None):
    rows, width = part.shape
    tile = min(256, rows)
    steps = rows // tile
    shape = (2 * rows, width) if axis == 0 else (rows, 2 * width)
    at = (lambda i, s: (s[0] * steps + i, 0)) if axis == 0 else (lambda i, s: (i, s[0]))
    in_specs = [pl.BlockSpec((tile, width), lambda i, s: (i, 0))]
    args = [place, part]
    alias = {}
    if whole is not None:
        in_specs.append(pl.BlockSpec(memory_space=pl.ANY))
        args.append(whole)
        alias = {2: 0}
    return pl.pallas_call(
        put_body, grid_spec=pltpu.PrefetchScalarGridSpec(num_scalar_prefetch=1, grid=(steps,), in_specs=in_specs, out_specs=pl.BlockSpec((tile, width), at)),
        out_shape=jax.ShapeDtypeStruct(shape, f32), input_output_aliases=alias, compiler_params=params(12),
        cost_estimate=pl.CostEstimate(flops=0, bytes_accessed=6 * rows * width, transcendentals=0),
    )(*args)


def put_blocks_body(block_ref, *out_refs):
    cols = out_refs[0].shape[1]
    for w, out_ref in enumerate(out_refs):
        out_ref[...] = block_ref[0, :, w * cols : (w + 1) * cols].astype(f32)


def put_blocks(stack):
    count, rows, width = stack.shape
    cols = width // 4
    return pl.pallas_call(
        put_blocks_body,
        grid=(count, 2),
        in_specs=[pl.BlockSpec((1, rows // 2, width), lambda i, h: (i, h, 0))],
        out_specs=[pl.BlockSpec((rows // 2, cols), lambda i, h: (h, i))] * 4,
        out_shape=[jax.ShapeDtypeStruct((rows, count * cols), f32)] * 4,
        compiler_params=params(12),
        cost_estimate=pl.CostEstimate(
            flops=0, bytes_accessed=6 * count * rows * width, transcendentals=0
        ),
    )(stack)


def matmul(left, right):
    return jnp.dot(left, right, preferred_element_type=f32)


def column_sums(matrix):
    return jnp.sum(matrix.astype(f32), 0)


def swap(block, step):
    count = lax.axis_size("group")
    return lax.ppermute(block, "group", [(i, i ^ step) for i in range(count)])


def exchange(blocks):
    return [blocks[0]] + [swap(blocks[step], step) for step in range(1, len(blocks))]


def gather_blocks(block):
    return exchange([block] * lax.axis_size("group"))


def group_bits():
    bits = [1 << b for b in range(lax.axis_size("group").bit_length() - 1)]
    return bits, bits[::-1]


def half_columns(block, side):
    width = block.shape[1] // 2
    return block[:, side * width : (side + 1) * width]


def gather_halves(block, fill=None):
    pieces = [[half_columns(block, side)] for side in range(2)]
    steps = [[[0]], [[0]]]
    paths = group_bits()
    for turn in range(len(paths[0])):
        arrived = []
        for side in range(2):
            mine = pieces[side]
            sent = mine[0] if turn == 0 else jnp.concatenate(mine)
            arrived.append(swap(sent, paths[side][turn]))
        if fill is not None:
            arrived = fill(turn, arrived)
        for side in range(2):
            known = [k for group in steps[side] for k in group]
            pieces[side].append(arrived[side])
            steps[side].append([k ^ paths[side][turn] for k in known])
    return pieces, steps


def ordered_halves(pieces, steps):
    me = lax.axis_index("group")
    count = lax.axis_size("group")
    rows, width = pieces[0][0].shape
    whole = jnp.zeros((count * rows, 2 * width), pieces[0][0].dtype)
    for side in range(2):
        for piece, group in zip(pieces[side], steps[side]):
            for i, k in enumerate(group):
                part = piece[i * rows : (i + 1) * rows]
                whole = lax.dynamic_update_slice(whole, part, ((me ^ k) * rows, side * width))
    return whole


def scatter_halves(partial, fill=None):
    me = lax.axis_index("group")
    count = lax.axis_size("group")
    rows = partial.shape[0] // count
    blocks = []
    for side in range(2):
        columns = half_columns(partial, side)
        blocks.append(
            [lax.dynamic_slice_in_dim(columns, (me ^ k) * rows, rows, 0) for k in range(count)]
        )
    held = [list(range(count)), list(range(count))]
    paths = group_bits()[::-1]
    for turn in range(len(paths[0])):
        arrived, leaving = [], []
        for side in range(2):
            bit = paths[side][turn]
            leaving.append([k for k in held[side] if k & bit])
            sent = jnp.concatenate([blocks[side][k] for k in leaving[side]]).astype(bf16)
            arrived.append(swap(sent, bit))
        if fill is not None:
            arrived = fill(turn, arrived)
        for side in range(2):
            bit = paths[side][turn]
            for i, k in enumerate(leaving[side]):
                part = arrived[side][i * rows : (i + 1) * rows].astype(f32)
                blocks[side][k ^ bit] = blocks[side][k ^ bit].astype(f32) + part
            held[side] = [k for k in held[side] if not k & bit]
    return jnp.concatenate([blocks[0][0], blocks[1][0]], 1).astype(f32)


def in_order(blocks):
    me = lax.axis_index("group")
    rows = blocks[0].shape[0]
    whole = jnp.zeros((len(blocks) * rows,) + blocks[0].shape[1:], blocks[0].dtype)
    for step, block in enumerate(blocks):
        start = ((me ^ step) * rows,) + (0,) * (block.ndim - 1)
        whole = lax.dynamic_update_slice(whole, block, start)
    return whole


def scatter_terms(partial):
    count = lax.axis_size("group")
    me = lax.axis_index("group")
    rows = partial.shape[0] // count
    terms = [lax.dynamic_slice_in_dim(partial, me * rows, rows, 0)]
    for step in range(1, count):
        sent = lax.dynamic_slice_in_dim(partial, (me ^ step) * rows, rows, 0)
        terms.append(swap(sent.astype(bf16), step))
    return terms


def add_terms(terms):
    return sum(term.astype(f32) for term in terms)


def scatter_sum(partial):
    return add_terms(scatter_terms(partial))


def gather_rows(block):
    return lax.all_gather(block, "group", axis=0, tiled=True)


def scatter_rows(partial):
    return lax.psum_scatter(
        partial.astype(bf16), "group", scatter_dimension=0, tiled=True
    ).astype(f32)


def reorder(stack):
    me = lax.axis_index("group")
    count = stack.shape[0]
    bit = 1
    while bit < count:
        pairs = stack.reshape((count // (2 * bit), 2, bit) + stack.shape[1:])
        pairs = jnp.where((me & bit) != 0, pairs[:, ::-1], pairs)
        stack = pairs.reshape(stack.shape)
        bit *= 2
    return stack


def after(value, *others):
    return lax.optimization_barrier((value,) + others)[0]


def core_swap(block):
    count = lax.axis_size("replica")
    return lax.ppermute(block, "replica", [(i, i ^ 1) for i in range(count)])


def core_join(mine, axis):
    core = lax.axis_index("replica") % 2
    other = core_swap(mine)
    first = jnp.where(core == 0, mine, other)
    second = jnp.where(core == 0, other, mine)
    return jnp.concatenate([first, second], axis)


class Order:
    def __init__(self):
        self.last = ()

    def __call__(self, *values):
        values = lax.optimization_barrier(values + self.last)[: len(values)]
        return values[0] if len(values) == 1 else values

    def mark(self, *values):
        self.last = values


def replica_swap(values, step):
    count = lax.axis_size("replica")
    return lax.ppermute(values, "replica", [(i, i ^ step) for i in range(count)])


def shards(
    tokens,
    lengths,
    exit_layers,
    pre_gain,
    pre_shift,
    query_weight,
    query_bias,
    key_weight,
    value_weight,
    value_bias,
    out_weight,
    out_bias,
    mid_gain,
    mid_shift,
    up_weight,
    up_bias,
    down_weight,
    down_bias,
    cotangent,
):
    rows, width = tokens.shape
    count = lax.axis_size("group")
    me = lax.axis_index("group")
    cols = width // count
    local = me * rows + jnp.arange(rows, dtype=jnp.int32)
    active = ((local < lengths[0]) & (exit_layers > LAYER)).astype(f32)[:, None]
    core = lax.axis_index("replica") % 2
    other = core_swap(mine)
    first = jnp.where(core == 0, mine, other)
    second = jnp.where(core == 0, other, mine)
    return jnp.concatenate([first, second], axis)


class Order:
    def __init__(self):
        self.last = ()

    def __call__(self, *values):
        values = lax.optimization_barrier(values + self.last)[: len(values)]
        return values[0] if len(values) == 1 else values

    def mark(self, *values):
        self.last = values


def replica_sum_small(values):
    count = lax.axis_size("replica")
    step = 1
    while step < count:
        values = values + lax.ppermute(values, "replica", [(i, i ^ step) for i in range(count)])
        step *= 2
    return values


def shards(
    tokens,
    lengths,
    exit_layers,
    pre_gain,
    pre_shift,
    query_weight,
    query_bias,
    key_weight,
    value_weight,
    value_bias,
    out_weight,
    out_bias,
    mid_gain,
    mid_shift,
    up_weight,
    up_bias,
    down_weight,
    down_bias,
    cotangent,
):
    rows, width = tokens.shape
    count = lax.axis_size("group")
    me = lax.axis_index("group")
    cols = width // count
    local = me * rows + jnp.arange(rows, dtype=jnp.int32)
    active = ((local < lengths[0]) & (exit_layers > LAYER)).astype(f32)[:, None]
    position = jnp.arange(count * rows, dtype=jnp.int32)
    allowed = position[None, :] <= position[:, None]
    core = lax.axis_index("replica") % 2
    half = cols // 2

    grad_out = cotangent.astype(f32)
    branch_grad = (active * grad_out).astype(bf16)
    vectors = jnp.concatenate([pre_gain, pre_shift, out_bias, mid_gain, mid_shift, down_bias])
    extra = -(-vectors.size // width)
    vectors = jnp.pad(vectors, (0, extra * width - vectors.size)).reshape(extra, width)
    sent = after(jnp.concatenate([tokens, vectors]), branch_grad)
    got = gather_blocks(sent)
    tokens_all = in_order([block[:rows] for block in got])
    vectors = in_order([block[rows:].reshape(1, -1)[:, : 6 * cols] for block in got])
    vectors = vectors.reshape(count, 6, cols).transpose(1, 0, 2).reshape(6, width).astype(f32)
    gain_one, shift_one, obias, gain_two, shift_two, dbias = (vectors[i] for i in range(6))

    def column_block(step, start, length):
        at = (start, (me ^ step) * cols)
        parts = [
            lax.dynamic_slice(w, at, (length, cols)) for w in (query_weight, key_weight, value_weight)
        ]
        return jnp.concatenate(parts, 1)

    normed_all, _ = layer_norm(tokens_all.astype(f32))
    attn_in = (normed_all * gain_one + shift_one).astype(bf16)
    own = column_block(0, 0, cols)
    blocks = exchange([own] + [column_block(step, core * half, half) for step in range(1, count)])
    arrived = [after(block, attn_in, own) for block in blocks[1:]]
    others = [core_swap(block) for block in arrived]
    starts = [(me ^ k) * cols + core * half for k in range(1, count)]
    starts += [(me ^ k) * cols + (1 - core) * half for k in range(1, count)]
    starts = jnp.stack([me * cols] + starts).astype(jnp.int32)
    everyone = ("replica", "group")
    branch_wide = lax.all_gather(branch_grad, everyone, axis=0, tiled=True)
    seq = count * rows
    branch_all = lax.dynamic_slice_in_dim(branch_wide, lax.axis_index("replica") * seq, seq, 0)

    qkv_bias = jnp.concatenate([query_bias, jnp.zeros_like(query_bias), value_bias])
    qkv = qkv_product(attn_in, own, arrived + others, starts, qkv_bias)
    context = attention(qkv)
    attn_out = scatter_halves(matmul(context, out_weight)) + obias
    hidden = tokens.astype(f32) + active * attn_out
    normed_two, factor_two = layer_norm(hidden)
    ffn_in = (normed_two * gain_two + shift_two).astype(bf16)
    act_grad = nt(branch_all, down_weight).astype(bf16)

    def late_act_grad(turn, arrived):
        return [after(block, act_grad) for block in arrived] if turn > 0 else arrived

    ffn_held, ffn_steps = gather_halves(ffn_in, late_act_grad)
    ffn_wide = lax.all_gather(ffn_in, everyone, axis=0, tiled=True)
    here = jnp.full((1,), core, jnp.int32)
    ff = up_weight.shape[1]
    members = (me ^ jnp.arange(count, dtype=jnp.int32)).astype(jnp.int32)
    act_low, pre_grad, _ = gelu_product_halves(
        ffn_held, ffn_steps, members, up_weight, up_bias, act_grad, 256
    )
    order = Order()
    order.mark(act_low, pre_grad)
    split = ff // 2
    down_half = lax.dynamic_slice(down_weight, (core * split, 0), (split, width))

    partial = nt(pre_grad, up_weight).astype(bf16)
    order.mark(partial)
    ffn_in_grad = scatter_terms(partial)
    wide_grad = nt(order(branch_wide), down_half).astype(bf16)
    order.mark(wide_grad)

    ffn_in_grad = add_terms(order(*ffn_in_grad))
    hidden_grad = grad_out + norm_back(ffn_in_grad * gain_two, normed_two, factor_two)
    attn_grad = (active * hidden_grad).astype(bf16)
    order.mark(attn_grad)
    side_work = {}

    def meanwhile(turn, arrived):
        if turn == 0:
            side_work["branch"] = matmul(order(act_low), down_weight)
            order.mark(side_work["branch"])
        else:
            side_work["sums"] = column_sums(order(branch_wide))
            order.mark(side_work["sums"])
        return order(*arrived)

    attn_all = ordered_halves(*gather_halves(attn_grad, meanwhile))
    branch, branch_sums = side_work["branch"], side_work["sums"]
    context_grad = nt(attn_all, out_weight).astype(bf16)
    qkv_grads = attention_back(qkv, context_grad)

    parts = weight_parts(attn_in, *qkv_grads, context, attn_all)
    qkv_grad = jnp.concatenate(qkv_grads, 1)
    piece = lax.psum_scatter(parts, "replica", scatter_dimension=1, tiled=True)
    qkv_weight = jnp.zeros((width, 3 * cols), bf16)
    for start, block in zip([me * cols] + [starts[1 + k] for k in range(2 * count - 2)], [own] + arrived + others):
        block = after(block, hidden)
        qkv_weight = lax.dynamic_update_slice(qkv_weight, block, (start, 0))
    in_part = nt(after(qkv_grad, parts), qkv_weight)
    order.mark(in_part)
    in_grad = scatter_terms(in_part)

    wide_act, wide_grad, wide_sums = gelu_product(
        order(ffn_wide), up_weight, up_bias, wide_grad, here, split, min(512, rows * count), split
    )
    order.mark(wide_act, wide_grad)

    shared = jnp.stack(
        [
            jnp.sum(in_part * normed_all, 0),
            jnp.sum(in_part, 0),
            jnp.sum(ffn_in_grad * normed_two, 0),
            jnp.sum(ffn_in_grad, 0),
        ]
    )
    qkv_bias_part = column_sums(qkv_grad)
    shared = reorder(shared.reshape(4, count, cols).transpose(1, 0, 2))
    shared, qkv_bias_part = order(shared, qkv_bias_part)
    shared = exchange([shared[k] for k in range(count)])

    def join_shared():
        values = jnp.concatenate(
            [
                sum(order(*shared)).reshape(-1),
                lax.dynamic_slice(column_sums(attn_all), (me * cols,), (cols,)),
                qkv_bias_part[:cols],
                qkv_bias_part[2 * cols :],
            ]
        )
        order.mark(values)
        return values, replica_swap(values, 1)

    def small_step(step):
        def run(pair):
            values, arrived = pair
            values = values + order(arrived)
            order.mark(values)
            return values if 2 * step >= replicas else (values, replica_swap(values, 2 * step))

        return run

    replicas = lax.axis_size("replica")
    small_steps, step = [lambda _: join_shared()], 1
    while step < replicas:
        small_steps.append(small_step(step))
        step *= 2

    normed_one, factor_one = layer_norm(tokens.astype(f32))
    in_grad = add_terms(order(*in_grad))
    token_grad = (hidden_grad + norm_back(in_grad * gain_one, normed_one, factor_one)).astype(bf16)
    order.mark(token_grad)

    down_grad = tn(order(wide_act), branch_wide).astype(bf16)
    order.mark(down_grad)
    small = small_steps[0](None)
    piece = order(piece)
    size = (1,) + piece.shape[1:2] + (3 * cols,)
    sent = [lax.dynamic_slice(piece, (me ^ step, 0, 0), size) for step in range(1, count)]
    sent = lax.optimization_barrier(tuple(sent))
    owned = lax.optimization_barrier(tuple(swap(s, k + 1) for k, s in enumerate(sent)))
    for step in range(1, count):
        piece = lax.dynamic_update_slice(piece, owned[step - 1], (me ^ step, 0, 0))
    order.mark(piece)
    attn_wgrad = lax.all_gather(piece, "replica", axis=1, tiled=True)
    small = small_steps[1](small)
    up_grad = tn(order(ffn_wide), wide_grad).astype(bf16)
    order.mark(up_grad)
    branch = scatter_terms(order(branch))
    down_other, up_other = core_swap(down_grad), core_swap(up_grad)
    down_grad = put_half(order(down_grad), here, 0)
    order.mark(down_grad)
    small = small_steps[2](small)
    up_grad = put_half(order(up_grad), here, 1)
    order.mark(up_grad)
    for run in small_steps[3:]:
        small = run(small)
    down_grad = put_half(order(down_other), 1 - here, 0, down_grad)
    up_grad = put_half(up_other, 1 - here, 1, up_grad)
    order.mark(down_grad, up_grad)
    output = (hidden + active * (add_terms(order(*branch)) + dbias)).astype(bf16)
    order.mark(output)
    up_bias_grad = core_join(wide_sums.reshape(-1), 0)
    down_bias_grad = lax.dynamic_slice(branch_sums, (me * cols,), (cols,))

    query_wgrad, key_wgrad, value_wgrad, out_wgrad = put_blocks(order(attn_wgrad))
    small_parts = [small[k * cols : (k + 1) * cols] for k in range(7)]
    return (
        output,
        token_grad,
        small_parts[0],
        small_parts[1],
        query_wgrad,
        small_parts[5],
        key_wgrad,
        value_wgrad,
        small_parts[6],
        out_wgrad,
        small_parts[4],
        small_parts[2],
        small_parts[3],
        up_grad,
        up_bias_grad,
        down_grad,
        down_bias_grad,
    )


def solution(mesh):
    both = P(("replica", "group"), None)
    vector, by_rows, by_cols = P("group"), P("group", None), P(None, "group")
    return jax.shard_map(
        shards,
        mesh=mesh,
        in_specs=(
            both,
            P("replica"),
            P(("replica", "group")),
            vector,
            vector,
            by_rows,
            vector,
            by_rows,
            by_rows,
            vector,
            by_rows,
            vector,
            vector,
            vector,
            by_cols,
            vector,
            by_rows,
            vector,
            both,
        ),
        out_specs=(
            both,
            both,
            vector,
            vector,
            by_rows,
            vector,
            by_rows,
            by_rows,
            vector,
            by_rows,
            vector,
            vector,
            vector,
            by_cols,
            vector,
            by_rows,
            vector,
        ),
        check_vma=False,
    )
```

```python
import functools

import jax
import jax.numpy as jnp
from jax import lax
from jax.experimental import pallas as pl
from jax.experimental.pallas import tpu as pltpu
from jax.sharding import PartitionSpec as P

HD = 64
LAYER = 12
QB = 128

bf16 = jnp.bfloat16
f32 = jnp.float32


def layer_norm(values):
    center = values - jnp.mean(values, -1, keepdims=True)
    spread = jnp.mean(center * center, -1, keepdims=True)
    factor = lax.rsqrt(spread + 1e-05)
    return (center * factor, factor)


def norm_back(grad, normal, factor):
    return factor * (
        grad
        - jnp.mean(grad, -1, keepdims=True)
        - normal * jnp.mean(grad * normal, -1, keepdims=True)
    )


def params(mb=56):
    return pltpu.CompilerParams(vmem_limit_bytes=mb << 20)

def nt(left, right):
    return lax.dot_general(left, right, (((1,), (1,)), ((), ())), preferred_element_type=f32)
def tn(left, right):
    return lax.dot_general(left, right, (((0,), (0,)), ((), ())), preferred_element_type=f32)

def later(keys, first):
    key = lax.broadcasted_iota(jnp.int32, (keys, QB), 0)
    query = lax.broadcasted_iota(jnp.int32, (keys, QB), 1) + first
    return key <= query

def attend_body(q_ref, k_ref, v_ref, out_ref):
    rows = q_ref.shape[0]
    for first in range(0, rows, QB):
        keys = first + QB
        parts = []
        for lane in range(0, q_ref.shape[1], HD):
            at = slice(lane, lane + HD)
            query = q_ref[first:keys, at] * 0.125
            scores = jnp.where(later(keys, first), nt(k_ref[:keys, at], query), -1e30)
            grown = jnp.exp(scores - jnp.max(scores, 0, keepdims=True))
            probs = grown * (1.0 / jnp.sum(grown, 0, keepdims=True))
            parts.append(tn(probs.astype(bf16), v_ref[:keys, at]))
        out_ref[first:keys, :] = jnp.concatenate(parts, 1).astype(bf16)

def attend_back_body(q_ref, k_ref, v_ref, g_ref, dq_ref, dk_ref, dv_ref, key_acc, value_acc):
    rows = q_ref.shape[0]
    key_acc[...] = jnp.zeros_like(key_acc)
    value_acc[...] = jnp.zeros_like(value_acc)
    for first in range(0, rows, QB):
        keys = first + QB
        q_parts, k_parts, v_parts = [], [], []
        for lane in range(0, q_ref.shape[1], HD):
            at = slice(lane, lane + HD)
            query = q_ref[first:keys, at] * 0.125
            grad = g_ref[first:keys, at]
            key = k_ref[:keys, at]
            scores = jnp.where(later(keys, first), nt(key, query), -1e30)
            grown = jnp.exp(scores - jnp.max(scores, 0, keepdims=True))
            probs = grown * (1.0 / jnp.sum(grown, 0, keepdims=True))
            probs_grad = nt(v_ref[:keys, at], grad)
            delta = jnp.sum(probs * probs_grad, 0, keepdims=True)
            score_grad = (probs * (probs_grad - delta)).astype(bf16)
            v_parts.append(jnp.dot(probs.astype(bf16), grad, preferred_element_type=f32))
            k_parts.append(jnp.dot(score_grad, query, preferred_element_type=f32))
            q_parts.append(tn(score_grad, key) * 0.125)
        dq_ref[first:keys, :] = jnp.concatenate(q_parts, 1).astype(bf16)
        key_acc[:keys, :] += jnp.concatenate(k_parts, 1)
        value_acc[:keys, :] += jnp.concatenate(v_parts, 1)
    dk_ref[...] = key_acc[...].astype(bf16)
    dv_ref[...] = value_acc[...].astype(bf16)

def attention(qkv):
    rows, cols = qkv.shape[0], qkv.shape[1] // 3
    lanes = 2 * HD
    pairs = cols // lanes
    spec = lambda part: pl.BlockSpec((rows, lanes), lambda h: (0, part * pairs + h))
    work = 2 * rows * rows * cols
    return pl.pallas_call(
        attend_body, grid=(pairs,), in_specs=[spec(0), spec(1), spec(2)], out_specs=spec(0),
        out_shape=jax.ShapeDtypeStruct((rows, cols), bf16), compiler_params=params(12),
        cost_estimate=pl.CostEstimate(flops=2 * work, bytes_accessed=8 * rows * cols, transcendentals=rows * rows * cols // HD),
    )(qkv, qkv, qkv)

def attention_back(qkv, grad):
    rows, cols = grad.shape
    lanes = 2 * HD
    pairs = cols // lanes
    spec = lambda part: pl.BlockSpec((rows, lanes), lambda h: (0, part * pairs + h))
    work = 2 * rows * rows * cols
    one = jax.ShapeDtypeStruct((rows, cols), bf16)
    return pl.pallas_call(
        attend_back_body, grid=(pairs,), in_specs=[spec(0), spec(1), spec(2), spec(0)], out_specs=[spec(0)] * 3,
        out_shape=[one] * 3, scratch_shapes=[pltpu.VMEM((rows, lanes), f32)] * 2, compiler_params=params(12),
        cost_estimate=pl.CostEstimate(flops=5 * work, bytes_accessed=14 * rows * cols, transcendentals=rows * rows * cols // HD),
    )(qkv, qkv, qkv, grad)

def gelu_tiles(tile, first, x_ref, w_ref, b_ref, g_ref, act_ref, grad_ref, sum_ref):
    for start in range(0, w_ref.shape[1], tile):
        at = slice(start, start + tile)
        value = jnp.dot(x_ref[...], w_ref[:, at], preferred_element_type=f32) + b_ref[:, at].astype(f32)
        square = value * value
        tangent = jnp.tanh(value * (0.7978845608 + (0.7978845608 * 0.044715) * square))
        share = 0.5 * value
        act_ref[:, at] = (share + share * tangent).astype(bf16)
        bend = share * (0.7978845608 + (3.0 * 0.7978845608 * 0.044715) * square)
        slope = (0.5 + 0.5 * tangent) + bend * (1.0 - tangent * tangent)
        grad = g_ref[:, at].astype(f32) * slope
        grad_ref[:, at] = grad.astype(bf16)
        total = jnp.sum(grad, 0, keepdims=True)
        if first is not True:
            total = jnp.where(first, total, sum_ref[:, at] + total)
        sum_ref[:, at] = total


def gelu_body(tile, place_ref, *refs):
    gelu_tiles(tile, pl.program_id(1) == 0, *refs)


def gelu_product(x, weight, bias, grad, place, width, row_tile, col_tile):
    rows, depth = x.shape
    steps = width // col_tile
    grid = pltpu.PrefetchScalarGridSpec(
        num_scalar_prefetch=1, grid=(steps, rows // row_tile),
        in_specs=[
            pl.BlockSpec((row_tile, depth), lambda j, i, s: (i, 0)),
            pl.BlockSpec((depth, col_tile), lambda j, i, s: (0, s[0] * steps + j)),
            pl.BlockSpec((1, col_tile), lambda j, i, s: (0, s[0] * steps + j)),
            pl.BlockSpec((row_tile, col_tile), lambda j, i, s: (i, j)),
        ],
        out_specs=[
            pl.BlockSpec((row_tile, col_tile), lambda j, i, s: (i, j)),
            pl.BlockSpec((row_tile, col_tile), lambda j, i, s: (i, j)),
            pl.BlockSpec((1, col_tile), lambda j, i, s: (0, j)),
        ])
    return pl.pallas_call(
        functools.partial(gelu_body, min(256, col_tile)), grid_spec=grid,
        out_shape=[jax.ShapeDtypeStruct((rows, width), bf16)] * 2 + [jax.ShapeDtypeStruct((1, width), f32)],
        compiler_params=params(30),
        cost_estimate=pl.CostEstimate(flops=2 * rows * depth * width, bytes_accessed=2 * (rows * depth + depth * width + 3 * rows * width), transcendentals=rows * width),
    )(place, x, weight, bias[None], grad)

def parts_body(x_ref, q_ref, k_ref, v_ref, context_ref, grad_ref, out_ref):
    cols = q_ref.shape[1]
    for w, ref in enumerate((q_ref, k_ref, v_ref)):
        out_ref[0, :, w * cols : (w + 1) * cols] = tn(x_ref[...], ref[...]).astype(bf16)
    out_ref[0, :, 3 * cols :] = tn(context_ref[...], grad_ref[...]).astype(bf16)


def weight_parts(x, query_grad, key_grad, value_grad, context, grad):
    rows, cols = context.shape
    count = x.shape[1] // cols
    whole = pl.BlockSpec((rows, cols), lambda i: (0, 0))
    block = pl.BlockSpec((rows, cols), lambda i: (0, i))
    return pl.pallas_call(
        parts_body,
        grid=(count,),
        in_specs=[block, whole, whole, whole, whole, block],
        out_specs=pl.BlockSpec((1, cols, 4 * cols), lambda i: (i, 0, 0)),
        out_shape=jax.ShapeDtypeStruct((count, cols, 4 * cols), bf16),
        compiler_params=params(18),
        cost_estimate=pl.CostEstimate(
            flops=8 * count * rows * cols * cols,
            bytes_accessed=2 * (2 * rows * count * cols + 4 * rows * cols + 4 * count * cols * cols),
            transcendentals=0,
        ),
    )(x, query_grad, key_grad, value_grad, context, grad)


def gelu_halves_body(tile, steps, member_ref, *refs):
    pieces, (w_ref, b_ref, g_ref, act_ref, grad_ref, sum_ref, x_ref) = refs[:-7], refs[-7:]
    rows, width = pieces[0].shape

    @pl.when(pl.program_id(0) == 0)
    def _():
        at = 0
        for side in range(2):
            for group in steps[side]:
                for i, k in enumerate(group):
                    start = pl.multiple_of(member_ref[k] * rows, rows)
                    part = pieces[at][i * rows : (i + 1) * rows, :]
                    x_ref[pl.ds(start, rows), side * width : (side + 1) * width] = part
                at += 1

    gelu_tiles(tile, True, x_ref, w_ref, b_ref, g_ref, act_ref, grad_ref, sum_ref)


def gelu_product_halves(pieces, steps, members, weight, bias, grad, col_tile):
    parts = [piece for side in pieces for piece in side]
    tall, width = grad.shape
    depth = weight.shape[0]
    grid = pltpu.PrefetchScalarGridSpec(
        num_scalar_prefetch=1,
        grid=(width // col_tile,),
        in_specs=[pl.BlockSpec(part.shape, lambda j, s: (0, 0)) for part in parts]
        + [
            pl.BlockSpec((depth, col_tile), lambda j, s: (0, j)),
            pl.BlockSpec((1, col_tile), lambda j, s: (0, j)),
            pl.BlockSpec((tall, col_tile), lambda j, s: (0, j)),
        ],
        out_specs=[
            pl.BlockSpec((tall, col_tile), lambda j, s: (0, j)),
            pl.BlockSpec((tall, col_tile), lambda j, s: (0, j)),
            pl.BlockSpec((1, col_tile), lambda j, s: (0, j)),
        ],
        scratch_shapes=[pltpu.VMEM((tall, depth), bf16)],
    )
    return pl.pallas_call(
        functools.partial(gelu_halves_body, col_tile, steps),
        grid_spec=grid,
        out_shape=[jax.ShapeDtypeStruct((tall, width), bf16)] * 2
        + [jax.ShapeDtypeStruct((1, width), f32)],
        compiler_params=params(24),
        cost_estimate=pl.CostEstimate(
            flops=2 * tall * depth * width,
            bytes_accessed=2 * (tall * depth + depth * width + 3 * tall * width),
            transcendentals=tall * width,
        ),
    )(members, *parts, weight, bias[None], grad)


def qkv_body(count, at_ref, x_ref, own_ref, *refs):
    blocks, b_ref, out_ref = refs[:-2], refs[-2], refs[-1]
    cols = own_ref.shape[0]
    half = cols // 2
    at = pl.multiple_of(at_ref[0], cols)
    total = jnp.dot(x_ref[:, pl.ds(at, cols)], own_ref[...], preferred_element_type=f32)
    for k, block in enumerate(blocks):
        at = pl.multiple_of(at_ref[1 + k], half)
        total += jnp.dot(x_ref[:, pl.ds(at, half)], block[...], preferred_element_type=f32)
    out_ref[...] = (total + b_ref[...].astype(f32)).astype(bf16)


def qkv_product(x, own, blocks, starts, bias):
    rows, width = x.shape
    cols = own.shape[0]
    half = cols // 2
    column = lambda size: pl.BlockSpec((size, cols), lambda j, s: (0, j))
    return pl.pallas_call(
        functools.partial(qkv_body, len(blocks)),
        grid_spec=pltpu.PrefetchScalarGridSpec(
            num_scalar_prefetch=1,
            grid=(3,),
            in_specs=[pl.BlockSpec((rows, width), lambda j, s: (0, 0)), column(cols)]
            + [column(half)] * len(blocks)
            + [column(1)],
            out_specs=column(rows),
        ),
        out_shape=jax.ShapeDtypeStruct((rows, 3 * cols), bf16),
        compiler_params=params(20),
        cost_estimate=pl.CostEstimate(
            flops=6 * rows * width * cols,
            bytes_accessed=2 * (rows * width + 3 * width * cols + 3 * rows * cols),
            transcendentals=0,
        ),
    )(starts, x, own, *blocks, bias[None])


def put_body(place_ref, part_ref, *refs):
    refs[-1][...] = part_ref[...].astype(f32)

def put_half(part, place, axis, whole=None):
    rows, width = part.shape
    tile = min(256, rows)
    steps = rows // tile
    shape = (2 * rows, width) if axis == 0 else (rows, 2 * width)
    at = (lambda i, s: (s[0] * steps + i, 0)) if axis == 0 else (lambda i, s: (i, s[0]))
    in_specs = [pl.BlockSpec((tile, width), lambda i, s: (i, 0))]
    args = [place, part]
    alias = {}
    if whole is not None:
        in_specs.append(pl.BlockSpec(memory_space=pl.ANY))
        args.append(whole)
        alias = {2: 0}
    return pl.pallas_call(
        put_body, grid_spec=pltpu.PrefetchScalarGridSpec(num_scalar_prefetch=1, grid=(steps,), in_specs=in_specs, out_specs=pl.BlockSpec((tile, width), at)),
        out_shape=jax.ShapeDtypeStruct(shape, f32), input_output_aliases=alias, compiler_params=params(12),
        cost_estimate=pl.CostEstimate(flops=0, bytes_accessed=6 * rows * width, transcendentals=0),
    )(*args)


def put_blocks_body(block_ref, *out_refs):
    cols = out_refs[0].shape[1]
    for w, out_ref in enumerate(out_refs):
        out_ref[...] = block_ref[0, :, w * cols : (w + 1) * cols].astype(f32)


def put_blocks(stack):
    count, rows, width = stack.shape
    cols = width // 4
    return pl.pallas_call(
        put_blocks_body,
        grid=(count, 2),
        in_specs=[pl.BlockSpec((1, rows // 2, width), lambda i, h: (i, h, 0))],
        out_specs=[pl.BlockSpec((rows // 2, cols), lambda i, h: (h, i))] * 4,
        out_shape=[jax.ShapeDtypeStruct((rows, count * cols), f32)] * 4,
        compiler_params=params(12),
        cost_estimate=pl.CostEstimate(
            flops=0, bytes_accessed=6 * count * rows * width, transcendentals=0
        ),
    )(stack)


def matmul(left, right):
    return jnp.dot(left, right, preferred_element_type=f32)


def column_sums(matrix):
    return jnp.sum(matrix.astype(f32), 0)


def swap(block, step):
    count = lax.axis_size("group")
    return lax.ppermute(block, "group", [(i, i ^ step) for i in range(count)])


def exchange(blocks):
    return [blocks[0]] + [swap(blocks[step], step) for step in range(1, len(blocks))]


def gather_blocks(block):
    return exchange([block] * lax.axis_size("group"))


def group_bits():
    bits = [1 << b for b in range(lax.axis_size("group").bit_length() - 1)]
    return bits, bits[::-1]


def half_columns(block, side):
    width = block.shape[1] // 2
    return block[:, side * width : (side + 1) * width]


def gather_halves(block, fill=None):
    pieces = [[half_columns(block, side)] for side in range(2)]
    steps = [[[0]], [[0]]]
    paths = group_bits()
    for turn in range(len(paths[0])):
        arrived = []
        for side in range(2):
            mine = pieces[side]
            sent = mine[0] if turn == 0 else jnp.concatenate(mine)
            arrived.append(swap(sent, paths[side][turn]))
        if fill is not None:
            arrived = fill(turn, arrived)
        for side in range(2):
            known = [k for group in steps[side] for k in group]
            pieces[side].append(arrived[side])
            steps[side].append([k ^ paths[side][turn] for k in known])
    return pieces, steps


def ordered_halves(pieces, steps):
    me = lax.axis_index("group")
    count = lax.axis_size("group")
    rows, width = pieces[0][0].shape
    whole = jnp.zeros((count * rows, 2 * width), pieces[0][0].dtype)
    for side in range(2):
        for piece, group in zip(pieces[side], steps[side]):
            for i, k in enumerate(group):
                part = piece[i * rows : (i + 1) * rows]
                whole = lax.dynamic_update_slice(whole, part, ((me ^ k) * rows, side * width))
    return whole


def scatter_halves(partial, fill=None):
    me = lax.axis_index("group")
    count = lax.axis_size("group")
    rows = partial.shape[0] // count
    blocks = []
    for side in range(2):
        columns = half_columns(partial, side)
        blocks.append(
            [lax.dynamic_slice_in_dim(columns, (me ^ k) * rows, rows, 0) for k in range(count)]
        )
    held = [list(range(count)), list(range(count))]
    paths = group_bits()[::-1]
    for turn in range(len(paths[0])):
        arrived, leaving = [], []
        for side in range(2):
            bit = paths[side][turn]
            leaving.append([k for k in held[side] if k & bit])
            sent = jnp.concatenate([blocks[side][k] for k in leaving[side]]).astype(bf16)
            arrived.append(swap(sent, bit))
        if fill is not None:
            arrived = fill(turn, arrived)
        for side in range(2):
            bit = paths[side][turn]
            for i, k in enumerate(leaving[side]):
                part = arrived[side][i * rows : (i + 1) * rows].astype(f32)
                blocks[side][k ^ bit] = blocks[side][k ^ bit].astype(f32) + part
            held[side] = [k for k in held[side] if not k & bit]
    return jnp.concatenate([blocks[0][0], blocks[1][0]], 1).astype(f32)


def in_order(blocks):
    me = lax.axis_index("group")
    rows = blocks[0].shape[0]
    whole = jnp.zeros((len(blocks) * rows,) + blocks[0].shape[1:], blocks[0].dtype)
    for step, block in enumerate(blocks):
        start = ((me ^ step) * rows,) + (0,) * (block.ndim - 1)
        whole = lax.dynamic_update_slice(whole, block, start)
    return whole


def scatter_terms(partial):
    count = lax.axis_size("group")
    me = lax.axis_index("group")
    rows = partial.shape[0] // count
    terms = [lax.dynamic_slice_in_dim(partial, me * rows, rows, 0)]
    for step in range(1, count):
        sent = lax.dynamic_slice_in_dim(partial, (me ^ step) * rows, rows, 0)
        terms.append(swap(sent.astype(bf16), step))
    return terms


def add_terms(terms):
    return sum(term.astype(f32) for term in terms)


def scatter_sum(partial):
    return add_terms(scatter_terms(partial))


def gather_rows(block):
    return lax.all_gather(block, "group", axis=0, tiled=True)


def scatter_rows(partial):
    return lax.psum_scatter(
        partial.astype(bf16), "group", scatter_dimension=0, tiled=True
    ).astype(f32)


def reorder(stack):
    me = lax.axis_index("group")
    count = stack.shape[0]
    bit = 1
    while bit < count:
        pairs = stack.reshape((count // (2 * bit), 2, bit) + stack.shape[1:])
        pairs = jnp.where((me & bit) != 0, pairs[:, ::-1], pairs)
        stack = pairs.reshape(stack.shape)
        bit *= 2
    return stack


def after(value, *others):
    return lax.optimization_barrier((value,) + others)[0]


def core_swap(block):
    count = lax.axis_size("replica")
    return lax.ppermute(block, "replica", [(i, i ^ 1) for i in range(count)])


def core_join(mine, axis):
    core = lax.axis_index("replica") % 2
    other = core_swap(mine)
    first = jnp.where(core == 0, mine, other)
    second = jnp.where(core == 0, other, mine)
    return jnp.concatenate([first, second], axis)


class Order:
    def __init__(self):
        self.last = ()

    def __call__(self, *values):
        values = lax.optimization_barrier(values + self.last)[: len(values)]
        return values[0] if len(values) == 1 else values

    def mark(self, *values):
        self.last = values


def replica_swap(values, step):
    count = lax.axis_size("replica")
    return lax.ppermute(values, "replica", [(i, i ^ step) for i in range(count)])


def shards(
    tokens,
    lengths,
    exit_layers,
    pre_gain,
    pre_shift,
    query_weight,
    query_bias,
    key_weight,
    value_weight,
    value_bias,
    out_weight,
    out_bias,
    mid_gain,
    mid_shift,
    up_weight,
    up_bias,
    down_weight,
    down_bias,
    cotangent,
):
    rows, width = tokens.shape
    count = lax.axis_size("group")
    me = lax.axis_index("group")
    cols = width // count
    local = me * rows + jnp.arange(rows, dtype=jnp.int32)
    active = ((local < lengths[0]) & (exit_layers > LAYER)).astype(f32)[:, None]
    core = lax.axis_index("replica") % 2
    other = core_swap(mine)
    first = jnp.where(core == 0, mine, other)
    second = jnp.where(core == 0, other, mine)
    return jnp.concatenate([first, second], axis)


class Order:
    def __init__(self):
        self.last = ()

    def __call__(self, *values):
        values = lax.optimization_barrier(values + self.last)[: len(values)]
        return values[0] if len(values) == 1 else values

    def mark(self, *values):
        self.last = values


def replica_sum_small(values):
    count = lax.axis_size("replica")
    step = 1
    while step < count:
        values = values + lax.ppermute(values, "replica", [(i, i ^ step) for i in range(count)])
        step *= 2
    return values


def shards(
    tokens,
    lengths,
    exit_layers,
    pre_gain,
    pre_shift,
    query_weight,
    query_bias,
    key_weight,
    value_weight,
    value_bias,
    out_weight,
    out_bias,
    mid_gain,
    mid_shift,
    up_weight,
    up_bias,
    down_weight,
    down_bias,
    cotangent,
):
    rows, width = tokens.shape
    count = lax.axis_size("group")
    me = lax.axis_index("group")
    cols = width // count
    local = me * rows + jnp.arange(rows, dtype=jnp.int32)
    active = ((local < lengths[0]) & (exit_layers > LAYER)).astype(f32)[:, None]
    position = jnp.arange(count * rows, dtype=jnp.int32)
    allowed = position[None, :] <= position[:, None]
    core = lax.axis_index("replica") % 2
    half = cols // 2

    grad_out = cotangent.astype(f32)
    branch_grad = (active * grad_out).astype(bf16)
    vectors = jnp.concatenate([pre_gain, pre_shift, out_bias, mid_gain, mid_shift, down_bias])
    extra = -(-vectors.size // width)
    vectors = jnp.pad(vectors, (0, extra * width - vectors.size)).reshape(extra, width)
    sent = after(jnp.concatenate([tokens, vectors]), branch_grad)
    got = gather_blocks(sent)
    tokens_all = in_order([block[:rows] for block in got])
    vectors = in_order([block[rows:].reshape(1, -1)[:, : 6 * cols] for block in got])
    vectors = vectors.reshape(count, 6, cols).transpose(1, 0, 2).reshape(6, width).astype(f32)
    gain_one, shift_one, obias, gain_two, shift_two, dbias = (vectors[i] for i in range(6))

    def column_block(step, start, length):
        at = (start, (me ^ step) * cols)
        parts = [
            lax.dynamic_slice(w, at, (length, cols)) for w in (query_weight, key_weight, value_weight)
        ]
        return jnp.concatenate(parts, 1)

    normed_all, _ = layer_norm(tokens_all.astype(f32))
    attn_in = (normed_all * gain_one + shift_one).astype(bf16)
    own = column_block(0, 0, cols)
    blocks = exchange([own] + [column_block(step, core * half, half) for step in range(1, count)])
    arrived = [after(block, attn_in, own) for block in blocks[1:]]
    others = [core_swap(block) for block in arrived]
    starts = [(me ^ k) * cols + core * half for k in range(1, count)]
    starts += [(me ^ k) * cols + (1 - core) * half for k in range(1, count)]
    starts = jnp.stack([me * cols] + starts).astype(jnp.int32)
    everyone = ("replica", "group")
    branch_wide = lax.all_gather(branch_grad, everyone, axis=0, tiled=True)
    seq = count * rows
    branch_all = lax.dynamic_slice_in_dim(branch_wide, lax.axis_index("replica") * seq, seq, 0)

    qkv_bias = jnp.concatenate([query_bias, jnp.zeros_like(query_bias), value_bias])
    qkv = qkv_product(attn_in, own, arrived + others, starts, qkv_bias)
    context = attention(qkv)
    attn_out = scatter_halves(matmul(context, out_weight)) + obias
    hidden = tokens.astype(f32) + active * attn_out
    normed_two, factor_two = layer_norm(hidden)
    ffn_in = (normed_two * gain_two + shift_two).astype(bf16)
    act_grad = nt(branch_all, down_weight).astype(bf16)

    def late_act_grad(turn, arrived):
        return [after(block, act_grad) for block in arrived] if turn > 0 else arrived

    ffn_held, ffn_steps = gather_halves(ffn_in, late_act_grad)
    ffn_wide = lax.all_gather(ffn_in, everyone, axis=0, tiled=True)
    here = jnp.full((1,), core, jnp.int32)
    ff = up_weight.shape[1]
    members = (me ^ jnp.arange(count, dtype=jnp.int32)).astype(jnp.int32)
    act_low, pre_grad, _ = gelu_product_halves(
        ffn_held, ffn_steps, members, up_weight, up_bias, act_grad, 256
    )
    order = Order()
    order.mark(act_low, pre_grad)
    split = ff // 2
    down_half = lax.dynamic_slice(down_weight, (core * split, 0), (split, width))

    partial = nt(pre_grad, up_weight).astype(bf16)
    order.mark(partial)
    side_work = {}

    def product_meanwhile(turn, arrived):
        if turn == 0:
            side_work["wide"] = nt(order(branch_wide), down_half).astype(bf16)
            order.mark(side_work["wide"])
        return order(*arrived)

    ffn_in_grad = scatter_halves(partial, product_meanwhile)
    wide_grad = side_work["wide"]
    hidden_grad = grad_out + norm_back(ffn_in_grad * gain_two, normed_two, factor_two)
    attn_grad = (active * hidden_grad).astype(bf16)
    order.mark(attn_grad)

    def meanwhile(turn, arrived):
        if turn == 0:
            side_work["branch"] = matmul(order(act_low), down_weight)
            order.mark(side_work["branch"])
        else:
            side_work["sums"] = column_sums(order(branch_wide))
            order.mark(side_work["sums"])
        return order(*arrived)

    attn_all = ordered_halves(*gather_halves(attn_grad, meanwhile))
    branch, branch_sums = side_work["branch"], side_work["sums"]
    context_grad = nt(attn_all, out_weight).astype(bf16)
    qkv_grads = attention_back(qkv, context_grad)

    parts = weight_parts(attn_in, *qkv_grads, context, attn_all)
    qkv_grad = jnp.concatenate(qkv_grads, 1)
    piece = lax.psum_scatter(parts, "replica", scatter_dimension=1, tiled=True)
    qkv_weight = jnp.zeros((width, 3 * cols), bf16)
    for start, block in zip([me * cols] + [starts[1 + k] for k in range(2 * count - 2)], [own] + arrived + others):
        block = after(block, hidden)
        qkv_weight = lax.dynamic_update_slice(qkv_weight, block, (start, 0))
    in_part = nt(after(qkv_grad, parts), qkv_weight)
    order.mark(in_part)
    in_grad = scatter_terms(in_part)

    wide_act, wide_grad, wide_sums = gelu_product(
        order(ffn_wide), up_weight, up_bias, wide_grad, here, split, min(512, rows * count), split
    )
    order.mark(wide_act, wide_grad)

    shared = jnp.stack(
        [
            jnp.sum(in_part * normed_all, 0),
            jnp.sum(in_part, 0),
            jnp.sum(ffn_in_grad * normed_two, 0),
            jnp.sum(ffn_in_grad, 0),
        ]
    )
    qkv_bias_part = column_sums(qkv_grad)
    shared = reorder(shared.reshape(4, count, cols).transpose(1, 0, 2))
    shared, qkv_bias_part = order(shared, qkv_bias_part)
    shared = exchange([shared[k] for k in range(count)])

    def join_shared():
        values = jnp.concatenate(
            [
                sum(order(*shared)).reshape(-1),
                lax.dynamic_slice(column_sums(attn_all), (me * cols,), (cols,)),
                qkv_bias_part[:cols],
                qkv_bias_part[2 * cols :],
            ]
        )
        order.mark(values)
        return values, replica_swap(values, 1)

    def small_step(step):
        def run(pair):
            values, arrived = pair
            values = values + order(arrived)
            order.mark(values)
            return values if 2 * step >= replicas else (values, replica_swap(values, 2 * step))

        return run

    replicas = lax.axis_size("replica")
    small_steps, step = [lambda _: join_shared()], 1
    while step < replicas:
        small_steps.append(small_step(step))
        step *= 2

    normed_one, factor_one = layer_norm(tokens.astype(f32))
    in_grad = add_terms(order(*in_grad))
    token_grad = (hidden_grad + norm_back(in_grad * gain_one, normed_one, factor_one)).astype(bf16)
    order.mark(token_grad)

    down_grad = tn(order(wide_act), branch_wide).astype(bf16)
    order.mark(down_grad)
    small = small_steps[0](None)
    piece = order(piece)
    size = (1,) + piece.shape[1:2] + (3 * cols,)
    sent = [lax.dynamic_slice(piece, (me ^ step, 0, 0), size) for step in range(1, count)]
    sent = lax.optimization_barrier(tuple(sent))
    owned = lax.optimization_barrier(tuple(swap(s, k + 1) for k, s in enumerate(sent)))
    for step in range(1, count):
        piece = lax.dynamic_update_slice(piece, owned[step - 1], (me ^ step, 0, 0))
    order.mark(piece)
    attn_wgrad = lax.all_gather(piece, "replica", axis=1, tiled=True)
    small = small_steps[1](small)
    up_grad = tn(order(ffn_wide), wide_grad).astype(bf16)
    order.mark(up_grad)
    branch = scatter_terms(order(branch))
    down_other, up_other = core_swap(down_grad), core_swap(up_grad)
    down_grad = put_half(order(down_grad), here, 0)
    order.mark(down_grad)
    small = small_steps[2](small)
    up_grad = put_half(order(up_grad), here, 1)
    order.mark(up_grad)
    for run in small_steps[3:]:
        small = run(small)
    down_grad = put_half(order(down_other), 1 - here, 0, down_grad)
    up_grad = put_half(up_other, 1 - here, 1, up_grad)
    order.mark(down_grad, up_grad)
    output = (hidden + active * (add_terms(order(*branch)) + dbias)).astype(bf16)
    order.mark(output)
    up_bias_grad = core_join(wide_sums.reshape(-1), 0)
    down_bias_grad = lax.dynamic_slice(branch_sums, (me * cols,), (cols,))

    query_wgrad, key_wgrad, value_wgrad, out_wgrad = put_blocks(order(attn_wgrad))
    small_parts = [small[k * cols : (k + 1) * cols] for k in range(7)]
    return (
        output,
        token_grad,
        small_parts[0],
        small_parts[1],
        query_wgrad,
        small_parts[5],
        key_wgrad,
        value_wgrad,
        small_parts[6],
        out_wgrad,
        small_parts[4],
        small_parts[2],
        small_parts[3],
        up_grad,
        up_bias_grad,
        down_grad,
        down_bias_grad,
    )


def solution(mesh):
    both = P(("replica", "group"), None)
    vector, by_rows, by_cols = P("group"), P("group", None), P(None, "group")
    return jax.shard_map(
        shards,
        mesh=mesh,
        in_specs=(
            both,
            P("replica"),
            P(("replica", "group")),
            vector,
            vector,
            by_rows,
            vector,
            by_rows,
            by_rows,
            vector,
            by_rows,
            vector,
            vector,
            vector,
            by_cols,
            vector,
            by_rows,
            vector,
            both,
        ),
        out_specs=(
            both,
            both,
            vector,
            vector,
            by_rows,
            vector,
            by_rows,
            by_rows,
            vector,
            by_rows,
            vector,
            vector,
            vector,
            by_cols,
            vector,
            by_rows,
            vector,
        ),
        check_vma=False,
    )
```
